32 devices in a mesh: seq: 8 (over y, x, core), head: 4 (over z).
Axes of the slice: x: 2, y: 2, z: 4, core: 2. Of those that a mesh axis runs over, the one named last changes fastest.
Arguments:
- tokens: bfloat16 [32768, 512], P(('seq', 'head')), may hold values from -8.4 to 8.4
- cotangent: bfloat16 [32768, 512], P(('seq', 'head')), may hold values from -6 to 6
- w_qkv: bfloat16 [512, 1536], P(('seq', 'head')), may hold values from -0.25 to 0.25
- w_out: bfloat16 [512, 512], P(('seq', 'head')), may hold values from -0.5 to 0.5
- w_up: bfloat16 [512, 2048], P(None, ('seq', 'head')), may hold values from -0.25 to 0.25
- w_down: bfloat16 [2048, 512], P(('seq', 'head')), may hold values from -0.1875 to 0.1875
- gain_one: bfloat16 [512], P(('seq', 'head')), may hold values from 0.099609375 to 1.8984375
- shift_one: bfloat16 [512], P(('seq', 'head')), may hold values from -1.5 to 1.5
- gain_two: bfloat16 [512], P(('seq', 'head')), may hold values from 0.099609375 to 1.8984375
- shift_two: bfloat16 [512], P(('seq', 'head')), may hold values from -1.5 to 1.5
- span_doc: int32 [128], replicated, may hold values from 0 to 15, never falling along the last dimension, each value on 1 to 16 neighbouring positions
Outputs:
- out_tokens: bfloat16 [32768, 512], P(('seq', 'head'))
- d_tokens: float32 [32768, 512], P(('seq', 'head'))
- d_w_qkv: float32 [512, 1536], P(('seq', 'head'))
- d_w_out: float32 [512, 512], P(('seq', 'head'))
- d_w_up: float32 [512, 2048], P(None, ('seq', 'head'))
- d_w_down: float32 [2048, 512], P(('seq', 'head'))
- d_gain_one: float32 [512], P(('seq', 'head'))
- d_shift_one: float32 [512], P(('seq', 'head'))
- d_gain_two: float32 [512], P(('seq', 'head'))
- d_shift_two: float32 [512], P(('seq', 'head'))
The draws below stay inside these ranges and needn't reach their ends.
Inputs may be any that keep to these rules, and one draw needn't show every extreme that they name: span_doc[j] is the document of continuation span j; the numbers never fall along j, every continuation holds 1 to 16 spans, and one holds exactly 16.
All inputs are finite; a program needn't handle non-finite values.
Results may differ from the reference program's by a relative error of at most 0.012.
Values may be sent and summed in bfloat16 or wider, within the bound.
A program may use at most 128 MiB of HBM per device.

```python
import math
import jax
import jax.numpy as jnp
import numpy as np
from jax import lax

D = 512
H = 8
HD = 64
FF = 2048
S = 128
QB = 512
MOST = 16
TOKENS = 32768
SPANS = 256
PSPANS = 128
CSPANS = 128
NCONT = 16


def draw_tokens(key, part):
    key_span, key_row = jax.random.split(jax.random.fold_in(key, 11))
    span_part = jnp.clip(jax.random.normal(key_span, (SPANS, 1, D), jnp.float32), -6.0, 6.0)
    row_part = jnp.clip(jax.random.normal(key_row, (SPANS, S, D), jnp.float32), -6.0, 6.0)
    mixed_rows = 0.7 * span_part + 0.7 * row_part
    return mixed_rows.reshape(TOKENS, D).astype(jnp.bfloat16)


def shard_levels(rng, extent, cuts, smallest, high):
    loudness, own = 1.0, jax.random.fold_in(rng, 6)
    for position, parts in cuts:
        steps = jnp.exp(jax.random.uniform(jax.random.fold_in(own, position), (parts,), jnp.float32, smallest / len(cuts), high / len(cuts)))
        loudness = loudness * jnp.repeat(steps, extent[position] // parts).reshape([-1 if axis == position else 1 for axis in range(len(extent))])
    return loudness


def split_up(amount, total, limit, skew):
    loads = [(1 << 20) // math.isqrt(rank ** skew) + 1 for rank in range(2, amount + 1)]
    surplus, counts = total - limit - (amount - 1), [1] * (amount - 1)
    while surplus > 0:
        free = [i for i in range(amount - 1) if counts[i] < limit]
        pool, budget = sum([loads[i] for i in free]), surplus
        for i in free:
            addition = min(limit - counts[i], max(1, budget * loads[i] // pool), surplus)
            counts[i] = counts[i] + addition
            surplus = surplus - addition
    return np.array([limit] + counts)


def ragged_sizes(key, number_of, total, limit, slope):
    if number_of == 2:
        one = jax.random.randint(key, (), max(1, total - limit), min(limit, total - 1) + 1)
        return jnp.stack([one, total - one])
    sizes = jnp.asarray(split_up(number_of, total, limit, slope), jnp.int32)
    couples = (number_of - 1) // 2
    source_of, receiver = sizes[1:1 + 2 * couples:2], sizes[2:2 + 2 * couples:2]
    slack = jnp.minimum(source_of - 1, limit - receiver)
    moved = jax.random.randint(jax.random.fold_in(key, 1), (couples,), 0, 1 << 20) % (slack + 1)
    sizes = sizes.at[1:1 + 2 * couples:2].set(source_of - moved).at[2:2 + 2 * couples:2].set(receiver + moved)
    return sizes[jax.random.permutation(jax.random.fold_in(key, 2), number_of)]


def scatter_about(own_key, dims, width, most, cuts=(), kind=jnp.bfloat16):
    loudness = shard_levels(own_key, dims, cuts, -0.22, 0.18) if cuts else 1.0
    entries = jax.random.normal(own_key, dims, jnp.float32) * width * loudness
    return jnp.minimum(jnp.maximum(entries, -most), most).astype(kind)


def setup_inputs(seed: int = 0) -> dict:
    key_list = jax.random.split(jax.random.key(seed), 12)
    return {
        "tokens": draw_tokens(jax.random.fold_in(key_list[11], 71), 0),
        "cotangent": scatter_about(key_list[1], (TOKENS, D), 1.0, 6.0, ((0, 32),)),
        "w_qkv": scatter_about(key_list[2], (D, 3 * D), D ** -0.5, 0.25, ((0, 32),)),
        "w_out": scatter_about(key_list[3], (D, D), (D // 4) ** -0.5, 0.5, ((0, 32),)),
        "w_up": scatter_about(key_list[4], (D, FF), D ** -0.5, 0.25, ((1, 32),)),
        "w_down": scatter_about(key_list[5], (FF, D), (FF // 2) ** -0.5, 0.1875, ((0, 32),)),
        "gain_one": jnp.clip(1.0 + 0.18 * jax.random.normal(key_list[6], (D,), jnp.float32), 0.099609375, 1.8984375).astype(jnp.bfloat16),
        "shift_one": scatter_about(key_list[7], (D,), 0.3, 1.5, ((0, 32),)),
        "gain_two": jnp.clip(1.0 + 0.18 * jax.random.normal(key_list[8], (D,), jnp.float32), 0.099609375, 1.8984375).astype(jnp.bfloat16),
        "shift_two": scatter_about(key_list[9], (D,), 0.3, 1.5, ((0, 32),)),
        "span_doc": jnp.searchsorted(jnp.cumsum(ragged_sizes(key_list[10], NCONT, CSPANS, MOST, 1)), jnp.arange(CSPANS), side="right").astype(jnp.int32),
    }


@jax.custom_vjp
def low(v):
    return lax.optimization_barrier(v.astype(jnp.bfloat16)).astype(jnp.float32)

@jax.custom_vjp
def low_back(v):
    return v

def low_keep(v):
    return (low(v), None)

def low_pass(kept, grad):
    return (grad,)

def back_keep(v):
    return (v, None)

def back_low(kept, grad):
    return (low(grad),)
low.defvjp(low_keep, low_pass)
low_back.defvjp(back_keep, back_low)
epsilon = 1e-05
highest = lax.Precision.HIGHEST
masked_score = -1e+30

def layer_norm(values, gain, shift):
    row_mean = lax.optimization_barrier(jnp.mean(values, axis=-1, keepdims=True))
    centred = values - row_mean
    variance = lax.optimization_barrier(jnp.mean(centred * centred, axis=-1, keepdims=True))
    return centred * lax.rsqrt(variance + epsilon) * gain + shift

def product(left, right):
    return jnp.dot(left, right, precision=highest, preferred_element_type=jnp.float32)

def attend_block(block_id, q_blk, k_blk, v_blk, sum_keys_all, sum_vals_all, docs_all):
    spans_blk = QB // S
    window = MOST + spans_blk
    first_span = (block_id * spans_blk).astype(jnp.int32)
    win_start = jnp.maximum(first_span - MOST, 0).astype(jnp.int32)
    win_keys = lax.dynamic_slice_in_dim(sum_keys_all, win_start, window, 0)
    win_vals = lax.dynamic_slice_in_dim(sum_vals_all, win_start, window, 0)
    win_docs = lax.dynamic_slice_in_dim(docs_all, win_start, window, 0)
    sum_keys = jnp.concatenate([sum_keys_all[:PSPANS], win_keys], axis=0)
    sum_vals = jnp.concatenate([sum_vals_all[:PSPANS], win_vals], axis=0)
    sum_index = jnp.concatenate([jnp.arange(PSPANS, dtype=jnp.int32), win_start + jnp.arange(window, dtype=jnp.int32)])
    row_docs = jnp.concatenate([jnp.full((PSPANS,), -2, jnp.int32), win_docs])
    prompt_row = jnp.arange(PSPANS + window) < PSPANS
    query_span = first_span + jnp.arange(spans_blk, dtype=jnp.int32)
    query_doc = lax.dynamic_slice_in_dim(docs_all, first_span, spans_blk, 0)
    earlier = sum_index[None, :] < query_span[:, None]
    same_doc = (sum_index[None, :] >= PSPANS) & (row_docs[None, :] == query_doc[:, None])
    allowed = (earlier & (prompt_row[None, :] | same_doc))[:, None, :]
    score_scale = 1.0 / math.sqrt(HD)
    q_spans = q_blk.reshape(spans_blk, S, H, HD)
    direct = low_back(jnp.einsum('nihe,njhe->hnij', q_spans, k_blk, precision=highest) * score_scale)
    causal = jnp.arange(S)[:, None] >= jnp.arange(S)[None, :]
    direct = jnp.where(causal, direct, masked_score)
    summary = low_back(jnp.einsum('nihe,the->hnit', q_spans, sum_keys, precision=highest) * score_scale)
    summary = jnp.where(allowed, summary, masked_score)
    row_top = jnp.maximum(lax.optimization_barrier(jnp.max(direct, axis=-1)), lax.optimization_barrier(jnp.max(summary, axis=-1)))
    exp_dir = jnp.exp(direct - row_top[..., None])
    exp_sum = jnp.exp(summary - row_top[..., None])
    denominator = lax.optimization_barrier(jnp.sum(exp_dir, axis=-1)) + lax.optimization_barrier(jnp.sum(exp_sum, axis=-1))
    prob_dir = low(exp_dir / denominator[..., None])
    prob_sum = low(exp_sum / denominator[..., None])
    mixed_rows = jnp.einsum('hnij,njhe->nihe', prob_dir, v_blk, precision=highest)
    mixed_rows = mixed_rows + jnp.einsum('hnit,the->nihe', prob_sum, sum_vals, precision=highest)
    return mixed_rows.reshape(QB, H * HD)

def forward(tokens, w_qkv, w_out, w_up, w_down, gain_one, shift_one, gain_two, shift_two, docs_all):
    rows_blk = min(4096, TOKENS)
    blocks_rows = TOKENS // rows_blk
    blocks_query = TOKENS // QB
    spans_blk = QB // S

    def project_rows(rows):
        normed = low(layer_norm(rows, gain_one, shift_one))
        return low(product(normed, w_qkv))
    qkv_all = lax.map(jax.checkpoint(project_rows), tokens.reshape(blocks_rows, rows_blk, D))
    qkv_all = low_back(qkv_all.reshape(TOKENS, H, 3, HD))
    queries = qkv_all[:, :, 0]
    keys_all = qkv_all[:, :, 1]
    vals_all = qkv_all[:, :, 2]
    sum_keys_all = low(lax.optimization_barrier(jnp.mean(keys_all.reshape(SPANS, S, H, HD), axis=1)))
    sum_vals_all = low(lax.optimization_barrier(jnp.mean(vals_all.reshape(SPANS, S, H, HD), axis=1)))

    def attend(inputs):
        block_id, q_blk, k_blk, v_blk = inputs
        return attend_block(block_id, q_blk, k_blk, v_blk, sum_keys_all, sum_vals_all, docs_all)
    mixed_all = lax.map(jax.checkpoint(attend), (jnp.arange(blocks_query, dtype=jnp.int32), queries.reshape(blocks_query, QB, H, HD), keys_all.reshape(blocks_query, spans_blk, S, H, HD), vals_all.reshape(blocks_query, spans_blk, S, H, HD)))
    mixed_all = low_back(low(mixed_all.reshape(TOKENS, D)))

    def finish_rows(inputs):
        rows, attn_rows = inputs
        resid = rows + low_back(product(attn_rows, w_out))
        normed = low(layer_norm(resid, gain_two, shift_two))
        hidden = low_back(product(normed, w_up))
        acted = low(jax.nn.gelu(hidden, approximate=True))
        return resid + low_back(product(acted, w_down))
    result = lax.map(jax.checkpoint(finish_rows), (tokens.reshape(blocks_rows, rows_blk, D), mixed_all.reshape(blocks_rows, rows_blk, D)))
    return result.reshape(TOKENS, D)

def reference(tokens, cotangent, w_qkv, w_out, w_up, w_down, gain_one, shift_one, gain_two, shift_two, span_doc):
    docs_all = jnp.concatenate([jnp.full((PSPANS,), -1, jnp.int32), span_doc.astype(jnp.int32)])

    def run(tok_in, qkv_in, out_in, up_in, down_in, gone_in, sone_in, gtwo_in, stwo_in):
        return forward(tok_in, qkv_in, out_in, up_in, down_in, gone_in, sone_in, gtwo_in, stwo_in, docs_all)
    floats = tuple((array_in.astype(jnp.float32) for array_in in (tokens, w_qkv, w_out, w_up, w_down, gain_one, shift_one, gain_two, shift_two)))
    result, pullback = jax.vjp(run, *floats)
    grads = pullback(cotangent.astype(jnp.float32))
    grad_scale = 1.0 / math.sqrt(TOKENS)
    return (result.astype(jnp.bfloat16), grads[0], grads[1] * grad_scale, grads[2] * grad_scale, grads[3] * grad_scale, grads[4] * grad_scale, grads[5] * grad_scale, grads[6] * grad_scale, grads[7] * grad_scale, grads[8] * grad_scale)
```

```python
import functools
import math

import jax
import jax.numpy as jnp
from jax import lax
from jax.experimental import pallas as pl
from jax.experimental.pallas import tpu as pltpu
from jax.sharding import PartitionSpec as P

H = 8
HD = 64
D = H * HD
S = 128
MOST = 16
PSPANS = 128
WIN = 2 * MOST
PAIRS = H // 2
LANES = 2 * HD
KEYS = S + PSPANS + WIN
EPS = 1e-05
MASKED = -1e30
F32 = jnp.float32
BF16 = jnp.bfloat16
VMEM = pltpu.MemorySpace.VMEM
VMEM_LIMIT = 60 * 2**20


def nn(a, b):
    return lax.dot_general(a, b, (((1,), (0,)), ((), ())), preferred_element_type=F32)


def nt(a, b):
    return lax.dot_general(a, b, (((1,), (1,)), ((), ())), preferred_element_type=F32)


def tn(a, b):
    return lax.dot_general(a, b, (((0,), (0,)), ((), ())), preferred_element_type=F32)


def window_base(first):
    return jnp.maximum((first - (MOST - 1)) // MOST, 0) * MOST


def summary_bias(first, span, docs_ref):
    base = pl.multiple_of(window_base(first), MOST)
    index = first + span
    row = lax.broadcasted_iota(jnp.int32, (PSPANS, S), 0)
    prompt = jnp.where(row < index, 0.0, MASKED)
    wrow = base + lax.broadcasted_iota(jnp.int32, (WIN, S), 0)
    same = docs_ref[pl.ds(base, WIN), :] == docs_ref[pl.ds(index, 1), :]
    window = jnp.where(same & (wrow >= PSPANS) & (wrow < index), 0.0, MASKED)
    return jnp.concatenate([prompt, window], axis=0).astype(F32)


def head_masks(scale):
    lane = lax.broadcasted_iota(jnp.int32, (1, LANES), 1)
    first = jnp.where(lane < HD, scale, 0.0).astype(BF16)
    second = jnp.where(lane < HD, 0.0, scale).astype(BF16)
    return first, second


def stack_heads(block, masks):
    return jnp.concatenate([block * masks[0], block * masks[1]], axis=0)


def pair_cols(part, pair):
    return slice(part * D + pair * LANES, part * D + (pair + 1) * LANES)


def all_keys(part, pair, rows, qkv_ref, psum_ref, wsum_ref):
    cols = pair_cols(part, pair)
    scols = pair_cols(part - 1, pair)
    return jnp.concatenate([qkv_ref[rows, cols], psum_ref[:, scols], wsum_ref[:, scols]], axis=0)


def unstack(pair_t):
    return jnp.concatenate([pair_t[:HD, :S], pair_t[HD:, S:]], axis=0)


def attend_span(span, first, qkv_ref, psum_ref, wsum_ref, docs_ref, attn_t_ref, probs_ref):
    rows = pl.ds(pl.multiple_of(span * S, S), S)
    bias = summary_bias(first, span, docs_ref)
    key_row = lax.broadcasted_iota(jnp.int32, (S, S), 0)
    query = lax.broadcasted_iota(jnp.int32, (S, S), 1)
    causal = jnp.where(key_row <= query, 0.0, MASKED).astype(F32)
    bias = jnp.concatenate([causal, bias], axis=0)
    bias = jnp.concatenate([bias, bias], axis=1)
    masks = head_masks(1.0 / math.sqrt(HD))
    for pair in range(PAIRS):
        queries = stack_heads(qkv_ref[rows, pair_cols(0, pair)], masks)
        keys = all_keys(1, pair, rows, qkv_ref, psum_ref, wsum_ref)
        vals = all_keys(2, pair, rows, qkv_ref, psum_ref, wsum_ref)
        scores = nt(keys, queries) + bias
        top = jnp.max(scores, axis=0, keepdims=True)
        grown = jnp.exp(scores - top)
        share = 1.0 / jnp.sum(grown, axis=0, keepdims=True)
        probs = (grown * share).astype(BF16)
        probs_ref[span * PAIRS + pair] = probs
        mixed = nn(vals.T, probs)
        attn_t_ref[pair * LANES : (pair + 1) * LANES, rows] = unstack(mixed).astype(BF16)


def attend_span_back(
    span, qkv_ref, psum_ref, wsum_ref, probs_ref, dattn_ref, dq_ref, dkv_ref, dsum_ref
):
    rows = pl.ds(pl.multiple_of(span * S, S), S)
    scale = 1.0 / math.sqrt(HD)
    masks = head_masks(scale)
    ones = head_masks(1.0)
    for pair in range(PAIRS):
        cols = pair_cols(0, pair)
        queries = stack_heads(qkv_ref[rows, cols], masks)
        keys = all_keys(1, pair, rows, qkv_ref, psum_ref, wsum_ref)
        vals = all_keys(2, pair, rows, qkv_ref, psum_ref, wsum_ref)
        grads = stack_heads(dattn_ref[rows, cols], ones)
        probs = probs_ref[span * PAIRS + pair]
        wide = probs.astype(F32)
        dprobs = nt(vals, grads)
        delta = jnp.sum(wide * dprobs, axis=0, keepdims=True)
        dscores = (wide * (dprobs - delta)).astype(BF16)
        dq_t = unstack(nn(keys.T, dscores)) * scale
        dq_ref[rows, cols] = dq_t.T.astype(BF16)
        dkeys = nn(dscores, queries)
        dvals = nn(probs, grads)
        vcols = pair_cols(1, pair)
        dkv_ref[rows, cols] = dkeys[:S]
        dkv_ref[rows, vcols] = dvals[:S]
        dsum_ref[:, cols] += dkeys[S:]
        dsum_ref[:, vcols] += dvals[S:]


def attention_kernel(spans, qkv_ref, psum_ref, wsum_ref, docs_ref, attn_t_ref, probs_ref):
    first = (lax.axis_index("seq") * lax.axis_size("head") + lax.axis_index("head")) * spans

    def step(span, carry):
        attend_span(span, first, qkv_ref, psum_ref, wsum_ref, docs_ref, attn_t_ref, probs_ref)
        return carry

    lax.fori_loop(0, spans, step, 0)


def attention_back_kernel(
    spans, qkv_ref, psum_ref, wsum_ref, probs_ref, dattn_ref, dq_ref, dkv_ref, dsum_ref
):
    dsum_ref[...] = jnp.zeros_like(dsum_ref)

    def step(span, carry):
        attend_span_back(
            span, qkv_ref, psum_ref, wsum_ref, probs_ref, dattn_ref, dq_ref, dkv_ref, dsum_ref
        )
        return carry

    lax.fori_loop(0, spans, step, 0)


def attention(qkv, psum, wsum, docs):
    tok = qkv.shape[0]
    spans = tok // S
    whole = pl.BlockSpec(memory_space=VMEM)
    return pl.pallas_call(
        functools.partial(attention_kernel, spans),
        out_shape=(
            jax.ShapeDtypeStruct((D, tok), BF16),
            jax.ShapeDtypeStruct((spans * PAIRS, KEYS, 2 * S), BF16),
        ),
        in_specs=[whole] * 4,
        out_specs=(whole, whole),
        compiler_params=pltpu.CompilerParams(vmem_limit_bytes=VMEM_LIMIT),
        name="attention",
    )(qkv, psum, wsum, docs)


def attention_back(qkv, psum, wsum, probs, dattn):
    tok = qkv.shape[0]
    spans = tok // S
    whole = pl.BlockSpec(memory_space=VMEM)
    return pl.pallas_call(
        functools.partial(attention_back_kernel, spans),
        out_shape=(
            jax.ShapeDtypeStruct((tok, D), BF16),
            jax.ShapeDtypeStruct((tok, 2 * D), F32),
            jax.ShapeDtypeStruct((PSPANS + WIN, 2 * D), F32),
        ),
        in_specs=[whole] * 5,
        out_specs=(whole, whole, whole),
        compiler_params=pltpu.CompilerParams(vmem_limit_bytes=VMEM_LIMIT),
        name="attention_back",
    )(qkv, psum, wsum, probs, dattn)


def layer_norm(values, gain, shift):
    row_mean = jnp.mean(values, axis=-1, keepdims=True)
    centred = values - row_mean
    variance = jnp.mean(centred * centred, axis=-1, keepdims=True)
    return centred * lax.rsqrt(variance + EPS) * gain + shift


def gelu_tanh(values):
    return jax.nn.gelu(values, approximate=True)


BOTH = ("seq", "head")


def split_parts(weight):
    rows = weight.shape[0]
    return weight.reshape(rows, H, 3, HD).transpose(0, 2, 1, 3).reshape(rows, 3 * D)


def join_parts(weight):
    rows = weight.shape[0]
    return weight.reshape(rows, 3, H, HD).transpose(0, 2, 1, 3).reshape(rows, 3 * D)


def shards(tokens, cotangent, w_qkv, w_out, w_up, w_down, gain_one, shift_one, gain_two, shift_two, span_doc):
    tok = tokens.shape[0]
    spans = tok // S
    devices = lax.axis_size("seq") * lax.axis_size("head")
    me = lax.axis_index("seq") * lax.axis_size("head") + lax.axis_index("head")
    first = me * spans
    grad_scale = 1.0 / math.sqrt(tok * devices)
    docs = jnp.concatenate([jnp.full((PSPANS,), -1, jnp.int32), span_doc])
    docs = jnp.broadcast_to(docs[:, None], (docs.shape[0], S))

    def gather(x, axis=0):
        return lax.all_gather(x, BOTH, axis=axis, tiled=True)

    def scatter(x, axis=0):
        return lax.psum_scatter(x, BOTH, scatter_dimension=axis, tiled=True)

    qkv_mat = gather(split_parts(w_qkv))
    out_mat = gather(w_out)
    up_mat = gather(w_up.T)
    down_mat = gather(w_down)
    small = gather(jnp.stack([gain_one, shift_one, gain_two, shift_two]), 1).astype(F32)
    x_rows = tokens.astype(F32)
    norm_one, back_one = jax.vjp(layer_norm, x_rows, small[0], small[1])
    act_one = norm_one.astype(BF16)
    qkv = jnp.dot(act_one, qkv_mat, preferred_element_type=F32).astype(BF16)
    span_kv = jnp.mean(qkv[:, D:].astype(F32).reshape(spans, S, 2 * D), axis=1).astype(BF16)
    all_kv = gather(span_kv)
    base = window_base(first)
    psum = all_kv[:PSPANS]
    wsum = lax.dynamic_slice_in_dim(all_kv, base, WIN, 0)
    attn_t, probs = attention(qkv, psum, wsum, docs)
    resid = x_rows + tn(attn_t, out_mat)
    norm_two, back_two = jax.vjp(layer_norm, resid, small[2], small[3])
    act_two = norm_two.astype(BF16)
    hidden = nt(act_two, up_mat)
    acted, back_gelu = jax.vjp(gelu_tanh, hidden)
    acted = acted.astype(BF16)
    out_tokens = (resid + nn(acted, down_mat)).astype(BF16)
    d_hidden = back_gelu(nt(cotangent, down_mat))[0].astype(BF16)
    grad_down = tn(acted, cotangent)
    grad_up = tn(d_hidden, act_two)
    d_resid_norm, grad_gain_two, grad_shift_two = back_two(nn(d_hidden, up_mat))
    d_resid = cotangent.astype(F32) + d_resid_norm
    d_branch = d_resid.astype(BF16)
    grad_out = nn(attn_t, d_branch)
    d_attn = nt(d_branch, out_mat).astype(BF16)
    dq, dkv, dsum = attention_back(qkv, psum, wsum, probs, d_attn)
    flat = jnp.zeros((all_kv.shape[0], 2 * D), F32)
    flat = lax.dynamic_update_slice_in_dim(flat, dsum[PSPANS:], base, 0)
    row = jnp.arange(flat.shape[0])[:, None]
    flat = jnp.where(row < PSPANS, 0.0, flat)
    flat = flat.at[:PSPANS].add(dsum[:PSPANS])
    span_grads = scatter(flat.astype(BF16)).astype(F32) / S
    dkv = (dkv.reshape(spans, S, 2 * D) + span_grads[:, None]).reshape(tok, 2 * D)
    dqkv = jnp.concatenate([dq, dkv.astype(BF16)], axis=1)
    grad_qkv = tn(act_one, dqkv)
    d_x_norm, grad_gain_one, grad_shift_one = back_one(nt(dqkv, qkv_mat))
    d_tokens = d_resid + d_x_norm
    small_grads = scatter(jnp.stack([grad_gain_one, grad_shift_one, grad_gain_two, grad_shift_two]), 1) * grad_scale
    return (
        out_tokens,
        d_tokens,
        join_parts(scatter(grad_qkv) * grad_scale),
        scatter(grad_out) * grad_scale,
        scatter(grad_up).T * grad_scale,
        scatter(grad_down) * grad_scale,
        small_grads[0],
        small_grads[1],
        small_grads[2],
        small_grads[3],
    )


def solution(mesh):
    rows, cols, vec = P(BOTH, None), P(None, BOTH), P(BOTH)
    in_specs = (rows, rows, rows, rows, cols, rows, vec, vec, vec, vec, P())
    out_specs = (rows, rows, rows, rows, cols, rows, vec, vec, vec, vec)
    return jax.shard_map(shards, mesh=mesh, in_specs=in_specs, out_specs=out_specs, check_vma=False)
```

```python
import functools
import math

import jax
import jax.numpy as jnp
from jax import lax
from jax.experimental import pallas as pl
from jax.experimental.pallas import tpu as pltpu
from jax.sharding import PartitionSpec as P

H = 8
HD = 64
D = H * HD
S = 128
MOST = 16
PSPANS = 128
WIN = 2 * MOST
PAIRS = H // 2
LANES = 2 * HD
KEYS = S + PSPANS + WIN
EPS = 1e-05
MASKED = -1e30
F32 = jnp.float32
BF16 = jnp.bfloat16
VMEM = pltpu.MemorySpace.VMEM
VMEM_LIMIT = 60 * 2**20


def nn(a, b):
    return lax.dot_general(a, b, (((1,), (0,)), ((), ())), preferred_element_type=F32)


def nt(a, b):
    return lax.dot_general(a, b, (((1,), (1,)), ((), ())), preferred_element_type=F32)


def tn(a, b):
    return lax.dot_general(a, b, (((0,), (0,)), ((), ())), preferred_element_type=F32)


def summary_bias(first, span, docs_ref):
    index = first + span
    row = lax.broadcasted_iota(jnp.int32, (PSPANS, S), 0)
    prompt = jnp.where(row < index, 0.0, MASKED)
    wrow = first - MOST + lax.broadcasted_iota(jnp.int32, (WIN, S), 0)
    same = docs_ref[pl.ds(pl.multiple_of(first, 8), WIN), :] == docs_ref[pl.ds(index + MOST, 1), :]
    window = jnp.where(same & (wrow >= PSPANS) & (wrow < index), 0.0, MASKED)
    return jnp.concatenate([prompt, window], axis=0).astype(F32)


def head_masks(scale):
    lane = lax.broadcasted_iota(jnp.int32, (1, LANES), 1)
    first = jnp.where(lane < HD, scale, 0.0).astype(BF16)
    second = jnp.where(lane < HD, 0.0, scale).astype(BF16)
    return first, second


def stack_heads(block, masks):
    return jnp.concatenate([block * masks[0], block * masks[1]], axis=0)


def pair_cols(part, pair):
    return slice(part * D + pair * LANES, part * D + (pair + 1) * LANES)


def all_keys(part, pair, rows, qkv_ref, psum_ref, wsum_ref):
    cols = pair_cols(part, pair)
    scols = pair_cols(part - 1, pair)
    return jnp.concatenate([qkv_ref[rows, cols], psum_ref[:, scols], wsum_ref[:, scols]], axis=0)


def unstack(pair_t):
    return jnp.concatenate([pair_t[:HD, :S], pair_t[HD:, S:]], axis=0)


def attend_span(span, first, qkv_ref, psum_ref, wsum_ref, docs_ref, attn_t_ref, probs_ref):
    rows = pl.ds(pl.multiple_of(span * S, S), S)
    bias = summary_bias(first, span, docs_ref)
    key_row = lax.broadcasted_iota(jnp.int32, (S, S), 0)
    query = lax.broadcasted_iota(jnp.int32, (S, S), 1)
    causal = jnp.where(key_row <= query, 0.0, MASKED).astype(F32)
    bias = jnp.concatenate([causal, bias], axis=0)
    bias = jnp.concatenate([bias, bias], axis=1)
    masks = head_masks(1.0 / math.sqrt(HD))
    for pair in range(PAIRS):
        queries = stack_heads(qkv_ref[rows, pair_cols(0, pair)], masks)
        keys = all_keys(1, pair, rows, qkv_ref, psum_ref, wsum_ref)
        vals = all_keys(2, pair, rows, qkv_ref, psum_ref, wsum_ref)
        scores = nt(keys, queries) + bias
        top = jnp.max(scores, axis=0, keepdims=True)
        grown = jnp.exp(scores - top)
        share = 1.0 / jnp.sum(grown, axis=0, keepdims=True)
        probs = (grown * share).astype(BF16)
        probs_ref[span * PAIRS + pair] = probs
        mixed = nn(vals.T, probs)
        attn_t_ref[pair * LANES : (pair + 1) * LANES, rows] = unstack(mixed).astype(BF16)


def attend_span_back(
    span, qkv_ref, psum_ref, wsum_ref, probs_ref, dattn_ref, dq_ref, dkv_ref, dsum_ref
):
    rows = pl.ds(pl.multiple_of(span * S, S), S)
    scale = 1.0 / math.sqrt(HD)
    masks = head_masks(scale)
    ones = head_masks(1.0)
    for pair in range(PAIRS):
        cols = pair_cols(0, pair)
        queries = stack_heads(qkv_ref[rows, cols], masks)
        keys = all_keys(1, pair, rows, qkv_ref, psum_ref, wsum_ref)
        vals = all_keys(2, pair, rows, qkv_ref, psum_ref, wsum_ref)
        grads = stack_heads(dattn_ref[rows, cols], ones)
        probs = probs_ref[span * PAIRS + pair]
        wide = probs.astype(F32)
        dprobs = nt(vals, grads)
        delta = jnp.sum(wide * dprobs, axis=0, keepdims=True)
        dscores = (wide * (dprobs - delta)).astype(BF16)
        dq_t = unstack(nn(keys.T, dscores)) * scale
        dq_ref[rows, cols] = dq_t.T.astype(BF16)
        dkeys = nn(dscores, queries)
        dvals = nn(probs, grads)
        vcols = pair_cols(1, pair)
        dkv_ref[rows, cols] = dkeys[:S]
        dkv_ref[rows, vcols] = dvals[:S]
        dsum_ref[:, cols] += dkeys[S:]
        dsum_ref[:, vcols] += dvals[S:]


MESH = pl.DeviceIdType.MESH
BOTH = ("seq", "head")


class Place:
    def __init__(self):
        seq, self.z = lax.axis_index("seq"), lax.axis_index("head")
        self.side = math.isqrt(lax.axis_size("seq") // 2)
        self.deep = lax.axis_size("head")
        self.devices = lax.axis_size("seq") * self.deep
        self.c = lax.rem(seq, 2)
        self.x = lax.rem(seq // 2, self.side)
        self.y = seq // 2 // self.side
        self.me = seq * self.deep + self.z

    def seq(self, y, x, c):
        return (y * self.side + x) * 2 + c

    def along(self, axis, step):
        n, turn = self.side, self.c if axis == 0 else 1 - self.c
        return lax.rem(self.y + turn * step, n), lax.rem(self.x + (1 - turn) * step, n)

    def sibling(self):
        return (self.seq(self.y, self.x, 1 - self.c), self.z)

    def peers(self, axis):
        if axis == "z":
            seq = self.seq(self.y, self.x, self.c)
            return [(seq, lax.rem(self.z + d, self.deep)) for d in range(1, self.deep)]
        return [(self.seq(*self.along(axis, d), self.c), self.z) for d in range(1, self.side)]

    def greet(self):
        barrier = pltpu.get_barrier_semaphore()
        others = [self.sibling(), *self.peers(0), *self.peers(1), *self.peers("z")]
        for other in others:
            pl.semaphore_signal(barrier, inc=1, device_id=other, device_id_type=MESH)
        pl.semaphore_wait(barrier, len(others))


class Wires:
    def __init__(self, send, recv):
        self.send, self.recv, self.used, self.sent = send, recv, 0, []

    def copy(self, src, dst, device):
        i = self.used
        self.used += 1
        move = pltpu.make_async_remote_copy(
            src_ref=src, dst_ref=dst, send_sem=self.send.at[i], recv_sem=self.recv.at[i],
            device_id=device, device_id_type=MESH,
        )
        move.start()
        self.sent.append(move)
        return move

    def local(self, src, dst):
        i = self.used
        self.used += 1
        move = pltpu.make_async_copy(src, dst, self.send.at[i])
        move.start()
        return move

    def finish(self):
        for move in self.sent:
            move.wait_send()


def copies_of_gather(side, deep, with_z):
    return 1 + (deep - 1 if with_z else 0) + (side - 1) + (side - 1) * side + side * side


class Gather:
    def __init__(self, wires, place, shard, full, rows, with_z):
        self.w, self.p, self.full, self.shard = wires, place, full, shard
        self.rows, self.with_z = rows, with_z
        self.group = rows * place.deep if with_z else rows

    def block(self, y, x):
        start = self.p.seq(y, x, self.p.c) * self.group
        return self.full.at[pl.ds(pl.multiple_of(start, self.group), self.group)]

    def step0(self):
        p = self.p
        start = pl.multiple_of(p.me * self.rows, self.rows) if self.with_z else p.seq(p.y, p.x, p.c) * self.rows
        own = self.full.at[pl.ds(start, self.rows)]
        self.moves = [self.w.copy(self.shard, own, d) for d in p.peers("z")] if self.with_z else []
        self.placed = self.w.local(self.shard, own)

    def _next(self, sources, axis, fresh):
        for move in self.moves:
            move.wait_recv()
        p = self.p
        self.moves = []
        if axis is not None:
            self.moves = [self.w.copy(self.block(*s), self.block(*s), d) for d in p.peers(axis) for s in sources]
        self.across += [self.w.copy(self.block(*s), self.block(*s), p.sibling()) for s in fresh]

    def step1(self):
        self.placed.wait()
        self.across = []
        here = [(self.p.y, self.p.x)]
        self._next(here, 0, here)

    def _line(self, step):
        p, n = self.p, self.p.side
        mine = [p.along(0, d) for d in range(n)]
        if step == 0:
            return mine
        y1, x1 = p.along(1, step)
        turn = 1 - p.c
        return [(turn * y1 + (1 - turn) * y, turn * x + (1 - turn) * x1) for y, x in mine]

    def step2(self):
        line = self._line(0)
        self._next(line, 1, line[1:])

    def step3(self):
        self._next([], None, [s for e in range(1, self.p.side) for s in self._line(e)])

    def step4(self):
        for move in self.across:
            move.wait_recv()


def layer_norm_rows(values, gain, shift):
    mean = jnp.mean(values, axis=-1, keepdims=True)
    centred = values - mean
    variance = jnp.mean(centred * centred, axis=-1, keepdims=True)
    return centred * lax.rsqrt(variance + EPS) * gain + shift


def spread_small(gathered, devices):
    width = D // devices
    table = gathered.reshape(devices * 8, LANES).astype(BF16)
    pick = lax.broadcasted_iota(jnp.int32, (LANES, D), 0) == lax.broadcasted_iota(jnp.int32, (LANES, D), 1) % width
    every = nn(table, jnp.where(pick, 1.0, 0.0).astype(BF16))
    owner = lax.broadcasted_iota(jnp.int32, (devices * 8, D), 0) // 8
    column = lax.broadcasted_iota(jnp.int32, (devices * 8, D), 1) // width
    return jnp.sum(jnp.where(owner == column, every, 0.0).reshape(devices, 8, D), axis=0)


def forward_kernel(
    with_z,
    x_ref, wq_ref, wo_ref, wu_ref, wd_ref, small_ref, docs_ref,
    act_ref, qkv_ref, probs_ref, attn_t_ref, psum_ref, wsum_ref,
    qkv_mat, out_mat, up_mat, down_mat, gains_ref,
    small_all, own_sums, sums_all, send, recv,
):
    place = Place()
    wires = Wires(send, recv)
    tok = x_ref.shape[0]
    spans = tok // S
    first = place.me * spans
    small = Gather(wires, place, small_ref, small_all, 1, True)
    gathers = [
        Gather(wires, place, shard, full, shard.shape[0], with_z)
        for shard, full in ((wq_ref, qkv_mat), (wo_ref, out_mat), (wd_ref, down_mat), (wu_ref, up_mat))
    ]
    g_qkv, g_out, g_down, g_up = gathers
    place.greet()
    small.step0()
    for g in gathers:
        g.step0()
    small.step1()
    g_qkv.step1()
    small.step2()
    g_qkv.step2()
    small.step3()
    g_qkv.step3()
    g_out.step1()
    g_down.step1()
    small.step4()
    gains_ref[...] = spread_small(small_all[...], place.devices)

    def norm(i, carry):
        rows = pl.ds(pl.multiple_of(i * S, S), S)
        normed = layer_norm_rows(x_ref[rows, :].astype(F32), gains_ref[0:1, :], gains_ref[1:2, :])
        act_ref[rows, :] = normed.astype(BF16)
        return carry

    lax.fori_loop(0, spans, norm, 0)
    g_qkv.step4()
    for part in (1, 2):
        cols = slice(part * D, (part + 1) * D)
        block = nn(act_ref[...], qkv_mat[:, cols]).astype(BF16)
        qkv_ref[:, cols] = block
        mean = jnp.sum(block.astype(F32).reshape(spans, S, D), axis=1) * (1.0 / S)
        own_sums[0, :, (part - 1) * D : part * D] = mean.astype(BF16)
    sums = Gather(wires, place, own_sums, sums_all, 1, True)
    sums.step0()
    qkv_ref[:, :D] = nn(act_ref[...], qkv_mat[:, :D]).astype(BF16)
    sums.step1()
    g_up.step1()
    sums.step2()
    sums.step3()
    g_out.step2()
    g_down.step2()
    sums.step4()
    for i in range(PSPANS // MOST):
        two = sums_all[pl.ds(2 * i, 2)].astype(F32)
        psum_ref[MOST * i : MOST * (i + 1), :] = two.reshape(MOST, 2 * D).astype(BF16)
    before = sums_all[pl.ds(lax.rem(place.me + place.devices - 2, place.devices), 1)].astype(F32)
    last = sums_all[pl.ds(lax.rem(place.me + place.devices - 1, place.devices), 1)].astype(F32)
    here = sums_all[pl.ds(place.me, 1)].astype(F32)
    wsum_ref[:MOST, :] = jnp.concatenate([before, last], axis=0).reshape(MOST, 2 * D).astype(BF16)
    wsum_ref[MOST:, :] = jnp.concatenate([here, jnp.zeros_like(here)], axis=0).reshape(MOST, 2 * D).astype(BF16)

    def step(span, carry):
        attend_span(span, first, qkv_ref, psum_ref, wsum_ref, docs_ref, attn_t_ref, probs_ref)
        return carry

    lax.fori_loop(0, spans // 2, step, 0)
    g_out.step3()
    g_down.step3()
    g_up.step2()
    lax.fori_loop(spans // 2, spans, step, 0)
    g_up.step3()
    for g in (g_out, g_down, g_up):
        g.step4()
    wires.finish()


def forward(x, wq, wo, wu, wd, small, docs, with_z):
    tok = x.shape[0]
    spans = tok // S
    deep = lax.axis_size("head")
    side = math.isqrt(lax.axis_size("seq") // 2)
    devices = 2 * side * side * deep
    whole = pl.BlockSpec(memory_space=VMEM)
    n = copies_of_gather(side, deep, True) * 6
    shape = jax.ShapeDtypeStruct
    return pl.pallas_call(
        functools.partial(forward_kernel, with_z),
        out_shape=(
            shape((tok, D), BF16),
            shape((tok, 3 * D), BF16),
            shape((spans * PAIRS, KEYS, 2 * S), BF16),
            shape((D, tok), BF16),
            shape((PSPANS, 2 * D), BF16),
            shape((WIN, 2 * D), BF16),
            shape((D, 3 * D), BF16),
            shape((D, D), BF16),
            shape((4 * D, D), BF16),
            shape((4 * D, D), BF16),
            shape((8, D), F32),
        ),
        in_specs=[whole] * 7,
        out_specs=(whole,) * 11,
        scratch_shapes=[
            pltpu.VMEM((devices, 8, LANES), F32),
            pltpu.VMEM((1, spans, 2 * D), BF16),
            pltpu.VMEM((devices, spans, 2 * D), BF16),
            pltpu.SemaphoreType.DMA((n,)),
            pltpu.SemaphoreType.DMA((n,)),
        ],
        compiler_params=pltpu.CompilerParams(vmem_limit_bytes=VMEM_LIMIT, collective_id=0, has_side_effects=True),
        name="gather_and_attend",
    )(x, wq, wo, wu, wd, small, docs)


def attention_back_kernel(
    spans, qkv_ref, psum_ref, wsum_ref, probs_ref, dattn_ref, dq_ref, dkv_ref, dsum_ref
):
    dsum_ref[...] = jnp.zeros_like(dsum_ref)

    def step(span, carry):
        attend_span_back(
            span, qkv_ref, psum_ref, wsum_ref, probs_ref, dattn_ref, dq_ref, dkv_ref, dsum_ref
        )
        return carry

    lax.fori_loop(0, spans, step, 0)


def attention_back(qkv, psum, wsum, probs, dattn):
    tok = qkv.shape[0]
    spans = tok // S
    whole = pl.BlockSpec(memory_space=VMEM)
    return pl.pallas_call(
        functools.partial(attention_back_kernel, spans),
        out_shape=(
            jax.ShapeDtypeStruct((tok, D), BF16),
            jax.ShapeDtypeStruct((tok, 2 * D), F32),
            jax.ShapeDtypeStruct((PSPANS + WIN, 2 * D), F32),
        ),
        in_specs=[whole] * 5,
        out_specs=(whole, whole, whole),
        compiler_params=pltpu.CompilerParams(vmem_limit_bytes=VMEM_LIMIT),
        name="attention_back",
    )(qkv, psum, wsum, probs, dattn)


def layer_norm(values, gain, shift):
    row_mean = jnp.mean(values, axis=-1, keepdims=True)
    centred = values - row_mean
    variance = jnp.mean(centred * centred, axis=-1, keepdims=True)
    return centred * lax.rsqrt(variance + EPS) * gain + shift


def gelu_tanh(values):
    return jax.nn.gelu(values, approximate=True)


def split_parts(weight):
    rows = weight.shape[0]
    return weight.reshape(rows, H, 3, HD).transpose(0, 2, 1, 3).reshape(rows, 3 * D)


def join_parts(weight):
    rows = weight.shape[0]
    return weight.reshape(rows, 3, H, HD).transpose(0, 2, 1, 3).reshape(rows, 3 * D)


def shards(tokens, cotangent, w_qkv, w_out, w_up, w_down, gain_one, shift_one, gain_two, shift_two, span_doc):
    tok = tokens.shape[0]
    spans = tok // S
    devices = lax.axis_size("seq") * lax.axis_size("head")
    me = lax.axis_index("seq") * lax.axis_size("head") + lax.axis_index("head")
    first = me * spans
    grad_scale = 1.0 / math.sqrt(tok * devices)
    docs = jnp.concatenate([jnp.full((PSPANS + MOST,), -1, jnp.int32), span_doc, jnp.full((MOST,), -1, jnp.int32)])
    docs = jnp.broadcast_to(docs[:, None], (docs.shape[0], S))

    def scatter(x, axis=0):
        return lax.psum_scatter(x, BOTH, scatter_dimension=axis, tiled=True)

    with_z = w_qkv.shape[0] % 16 == 0
    weights = (split_parts(w_qkv), w_out, w_up.T, w_down)
    if not with_z:
        weights = tuple(lax.all_gather(w, "head", axis=0, tiled=True) for w in weights)
    small = jnp.stack([gain_one, shift_one, gain_two, shift_two]).astype(F32)
    small = jnp.pad(small, ((0, 4), (0, LANES - small.shape[1])))[None]
    act_one, qkv, probs, attn_t, psum, wsum, qkv_mat, out_mat, up_mat, down_mat, gains = forward(
        tokens, *weights, small, docs, with_z
    )
    x_rows = tokens.astype(F32)
    _, back_one = jax.vjp(layer_norm, x_rows, gains[0], gains[1])
    resid = x_rows + tn(attn_t, out_mat)
    norm_two, back_two = jax.vjp(layer_norm, resid, gains[2], gains[3])
    act_two = norm_two.astype(BF16)
    hidden = nt(act_two, up_mat)
    acted, back_gelu = jax.vjp(gelu_tanh, hidden)
    acted = acted.astype(BF16)
    out_tokens = (resid + nn(acted, down_mat)).astype(BF16)
    d_hidden = back_gelu(nt(cotangent, down_mat))[0].astype(BF16)
    grad_down = tn(acted, cotangent)
    grad_up = tn(d_hidden, act_two)
    d_resid_norm, grad_gain_two, grad_shift_two = back_two(nn(d_hidden, up_mat))
    d_resid = cotangent.astype(F32) + d_resid_norm
    d_branch = d_resid.astype(BF16)
    grad_out = nn(attn_t, d_branch)
    d_attn = nt(d_branch, out_mat).astype(BF16)
    dq, dkv, dsum = attention_back(qkv, psum, wsum, probs, d_attn)
    flat = jnp.zeros((devices * spans + 2 * MOST, 2 * D), F32)
    flat = lax.dynamic_update_slice_in_dim(flat, dsum[PSPANS:], first, 0)[MOST:-MOST]
    row = jnp.arange(flat.shape[0])[:, None]
    flat = jnp.where(row < PSPANS, 0.0, flat)
    flat = flat.at[:PSPANS].add(dsum[:PSPANS])
    span_grads = scatter(flat.astype(BF16)).astype(F32) / S
    dkv = (dkv.reshape(spans, S, 2 * D) + span_grads[:, None]).reshape(tok, 2 * D)
    dqkv = jnp.concatenate([dq, dkv.astype(BF16)], axis=1)
    grad_qkv = tn(act_one, dqkv)
    d_x_norm, grad_gain_one, grad_shift_one = back_one(nt(dqkv, qkv_mat))
    d_tokens = d_resid + d_x_norm
    small_grads = scatter(jnp.stack([grad_gain_one, grad_shift_one, grad_gain_two, grad_shift_two]), 1) * grad_scale
    return (
        out_tokens,
        d_tokens,
        join_parts(scatter(grad_qkv) * grad_scale),
        scatter(grad_out) * grad_scale,
        scatter(grad_up).T * grad_scale,
        scatter(grad_down) * grad_scale,
        small_grads[0],
        small_grads[1],
        small_grads[2],
        small_grads[3],
    )


def solution(mesh):
    rows, cols, vec = P(BOTH, None), P(None, BOTH), P(BOTH)
    in_specs = (rows, rows, rows, rows, cols, rows, vec, vec, vec, vec, P())
    out_specs = (rows, rows, rows, rows, cols, rows, vec, vec, vec, vec)
    return jax.shard_map(shards, mesh=mesh, in_specs=in_specs, out_specs=out_specs, check_vma=False)
```

```python
import functools
import math

import jax
import jax.numpy as jnp
from jax import lax
from jax.experimental import pallas as pl
from jax.experimental.pallas import tpu as pltpu
from jax.sharding import PartitionSpec as P

H = 8
HD = 64
D = H * HD
S = 128
MOST = 16
PSPANS = 128
WIN = 2 * MOST
PAIRS = H // 2
LANES = 2 * HD
KEYS = S + PSPANS + WIN
EPS = 1e-05
MASKED = -1e30
F32 = jnp.float32
BF16 = jnp.bfloat16
VMEM = pltpu.MemorySpace.VMEM
VMEM_LIMIT = 60 * 2**20


def nn(a, b):
    return lax.dot_general(a, b, (((1,), (0,)), ((), ())), preferred_element_type=F32)


def nt(a, b):
    return lax.dot_general(a, b, (((1,), (1,)), ((), ())), preferred_element_type=F32)


def tn(a, b):
    return lax.dot_general(a, b, (((0,), (0,)), ((), ())), preferred_element_type=F32)


def summary_bias(first, span, docs_ref):
    index = first + span
    row = lax.broadcasted_iota(jnp.int32, (PSPANS, S), 0)
    prompt = jnp.where(row < index, 0.0, MASKED)
    wrow = first - MOST + lax.broadcasted_iota(jnp.int32, (WIN, S), 0)
    same = docs_ref[pl.ds(pl.multiple_of(first, 8), WIN), :] == docs_ref[pl.ds(index + MOST, 1), :]
    window = jnp.where(same & (wrow >= PSPANS) & (wrow < index), 0.0, MASKED)
    return jnp.concatenate([prompt, window], axis=0).astype(F32)


def head_masks(scale):
    lane = lax.broadcasted_iota(jnp.int32, (1, LANES), 1)
    first = jnp.where(lane < HD, scale, 0.0).astype(BF16)
    second = jnp.where(lane < HD, 0.0, scale).astype(BF16)
    return first, second


def stack_heads(block, masks):
    return jnp.concatenate([block * masks[0], block * masks[1]], axis=0)


def pair_cols(part, pair):
    return slice(part * D + pair * LANES, part * D + (pair + 1) * LANES)


def all_keys(part, pair, rows, qkv_ref, psum_ref, wsum_ref):
    cols = pair_cols(part, pair)
    scols = pair_cols(part - 1, pair)
    return jnp.concatenate([qkv_ref[rows, cols], psum_ref[:, scols], wsum_ref[:, scols]], axis=0)


def unstack(pair_t):
    return jnp.concatenate([pair_t[:HD, :S], pair_t[HD:, S:]], axis=0)


def attend_span(span, first, qkv_ref, psum_ref, wsum_ref, docs_ref, attn_t_ref, probs_ref):
    rows = pl.ds(pl.multiple_of(span * S, S), S)
    bias = summary_bias(first, span, docs_ref)
    key_row = lax.broadcasted_iota(jnp.int32, (S, S), 0)
    query = lax.broadcasted_iota(jnp.int32, (S, S), 1)
    causal = jnp.where(key_row <= query, 0.0, MASKED).astype(F32)
    bias = jnp.concatenate([causal, bias], axis=0)
    bias = jnp.concatenate([bias, bias], axis=1)
    masks = head_masks(1.0 / math.sqrt(HD))
    for pair in range(PAIRS):
        queries = stack_heads(qkv_ref[rows, pair_cols(0, pair)], masks)
        keys = all_keys(1, pair, rows, qkv_ref, psum_ref, wsum_ref)
        vals = all_keys(2, pair, rows, qkv_ref, psum_ref, wsum_ref)
        scores = nt(keys, queries) + bias
        top = jnp.max(scores, axis=0, keepdims=True)
        grown = jnp.exp(scores - top)
        share = 1.0 / jnp.sum(grown, axis=0, keepdims=True)
        probs = (grown * share).astype(BF16)
        probs_ref[span * PAIRS + pair] = probs
        mixed = nn(vals.T, probs)
        attn_t_ref[pair * LANES : (pair + 1) * LANES, rows] = unstack(mixed).astype(BF16)


def attend_span_back(
    span, qkv_ref, psum_ref, wsum_ref, probs_ref, dattn_ref, dq_ref, dkv_ref, dsum_ref
):
    rows = pl.ds(pl.multiple_of(span * S, S), S)
    scale = 1.0 / math.sqrt(HD)
    masks = head_masks(scale)
    ones = head_masks(1.0)
    for pair in range(PAIRS):
        cols = pair_cols(0, pair)
        queries = stack_heads(qkv_ref[rows, cols], masks)
        keys = all_keys(1, pair, rows, qkv_ref, psum_ref, wsum_ref)
        vals = all_keys(2, pair, rows, qkv_ref, psum_ref, wsum_ref)
        grads = stack_heads(dattn_ref[rows, cols], ones)
        probs = probs_ref[span * PAIRS + pair]
        wide = probs.astype(F32)
        dprobs = nt(vals, grads)
        delta = jnp.sum(wide * dprobs, axis=0, keepdims=True)
        dscores = (wide * (dprobs - delta)).astype(BF16)
        dq_t = unstack(nn(keys.T, dscores)) * scale
        dq_ref[rows, cols] = dq_t.T.astype(BF16)
        dkeys = nn(dscores, queries)
        dvals = nn(probs, grads)
        vcols = pair_cols(1, pair)
        dkv_ref[rows, cols] = dkeys[:S]
        dkv_ref[rows, vcols] = dvals[:S]
        dsum_ref[:, cols] += dkeys[S:]
        dsum_ref[:, vcols] += dvals[S:]


MESH = pl.DeviceIdType.MESH
BOTH = ("seq", "head")


class Place:
    def __init__(self):
        seq, self.z = lax.axis_index("seq"), lax.axis_index("head")
        self.side = math.isqrt(lax.axis_size("seq") // 2)
        self.deep = lax.axis_size("head")
        self.devices = lax.axis_size("seq") * self.deep
        self.c = lax.rem(seq, 2)
        self.x = lax.rem(seq // 2, self.side)
        self.y = seq // 2 // self.side
        self.me = seq * self.deep + self.z

    def seq(self, y, x, c):
        return (y * self.side + x) * 2 + c

    def along(self, axis, step):
        n, turn = self.side, self.c if axis == 0 else 1 - self.c
        return lax.rem(self.y + turn * step, n), lax.rem(self.x + (1 - turn) * step, n)

    def sibling(self):
        return (self.seq(self.y, self.x, 1 - self.c), self.z)

    def peers(self, axis):
        if axis == "z":
            seq = self.seq(self.y, self.x, self.c)
            return [(seq, lax.rem(self.z + d, self.deep)) for d in range(1, self.deep)]
        return [(self.seq(*self.along(axis, d), self.c), self.z) for d in range(1, self.side)]

    def greet(self):
        barrier = pltpu.get_barrier_semaphore()
        others = [self.sibling(), *self.peers(0), *self.peers(1), *self.peers("z")]
        for other in others:
            pl.semaphore_signal(barrier, inc=1, device_id=other, device_id_type=MESH)
        pl.semaphore_wait(barrier, len(others))


class Wires:
    def __init__(self, send, recv):
        self.send, self.recv, self.used, self.sent = send, recv, 0, []

    def copy(self, src, dst, device):
        i = self.used
        self.used += 1
        move = pltpu.make_async_remote_copy(
            src_ref=src, dst_ref=dst, send_sem=self.send.at[i], recv_sem=self.recv.at[i],
            device_id=device, device_id_type=MESH,
        )
        move.start()
        self.sent.append(move)
        return move

    def local(self, src, dst):
        i = self.used
        self.used += 1
        move = pltpu.make_async_copy(src, dst, self.send.at[i])
        move.start()
        return move

    def finish(self):
        for move in self.sent:
            move.wait_send()


def copies_of_gather(side, deep, with_z):
    return 1 + (deep - 1 if with_z else 0) + (side - 1) + (side - 1) * side + side * side


class Gather:
    def __init__(self, wires, place, shard, full, rows, with_z):
        self.w, self.p, self.full, self.shard = wires, place, full, shard
        self.rows, self.with_z = rows, with_z
        self.group = rows * place.deep if with_z else rows

    def block(self, y, x):
        start = self.p.seq(y, x, self.p.c) * self.group
        return self.full.at[pl.ds(pl.multiple_of(start, self.group), self.group)]

    def step0(self):
        p = self.p
        start = pl.multiple_of(p.me * self.rows, self.rows) if self.with_z else p.seq(p.y, p.x, p.c) * self.rows
        own = self.full.at[pl.ds(start, self.rows)]
        self.moves = [self.w.copy(self.shard, own, d) for d in p.peers("z")] if self.with_z else []
        self.placed = self.w.local(self.shard, own)

    def _next(self, sources, axis, fresh):
        for move in self.moves:
            move.wait_recv()
        p = self.p
        self.moves = []
        if axis is not None:
            self.moves = [self.w.copy(self.block(*s), self.block(*s), d) for d in p.peers(axis) for s in sources]
        self.across += [self.w.copy(self.block(*s), self.block(*s), p.sibling()) for s in fresh]

    def step1(self):
        self.placed.wait()
        self.across = []
        here = [(self.p.y, self.p.x)]
        self._next(here, 0, here)

    def _line(self, step):
        p, n = self.p, self.p.side
        mine = [p.along(0, d) for d in range(n)]
        if step == 0:
            return mine
        y1, x1 = p.along(1, step)
        turn = 1 - p.c
        return [(turn * y1 + (1 - turn) * y, turn * x + (1 - turn) * x1) for y, x in mine]

    def step2(self):
        line = self._line(0)
        self._next(line, 1, line[1:])

    def step3(self):
        self._next([], None, [s for e in range(1, self.p.side) for s in self._line(e)])

    def step4(self):
        for move in self.across:
            move.wait_recv()


def spread_small(gathered, devices):
    width = D // devices
    table = gathered.reshape(devices * 8, LANES).astype(BF16)
    pick = lax.broadcasted_iota(jnp.int32, (LANES, D), 0) == lax.broadcasted_iota(jnp.int32, (LANES, D), 1) % width
    every = nn(table, jnp.where(pick, 1.0, 0.0).astype(BF16))
    owner = lax.broadcasted_iota(jnp.int32, (devices * 8, D), 0) // 8
    column = lax.broadcasted_iota(jnp.int32, (devices * 8, D), 1) // width
    return jnp.sum(jnp.where(owner == column, every, 0.0).reshape(devices, 8, D), axis=0)


def forward_kernel(
    with_z,
    x_ref, wq_ref, wo_ref, wu_ref, wd_ref, small_ref, docs_ref,
    act_ref, qkv_ref, probs_ref, attn_t_ref, psum_ref, wsum_ref,
    qkv_mat, out_mat, up_mat, down_mat, gains_ref,
    small_all, own_sums, sums_all, send, recv,
):
    place = Place()
    wires = Wires(send, recv)
    tok = x_ref.shape[0]
    spans = tok // S
    first = place.me * spans
    small = Gather(wires, place, small_ref, small_all, 1, True)
    gathers = [
        Gather(wires, place, shard, full, shard.shape[0], with_z)
        for shard, full in ((wq_ref, qkv_mat), (wo_ref, out_mat), (wd_ref, down_mat), (wu_ref, up_mat))
    ]
    g_qkv, g_out, g_down, g_up = gathers
    place.greet()
    small.step0()
    for g in gathers:
        g.step0()
    small.step1()
    g_qkv.step1()
    small.step2()
    g_qkv.step2()
    small.step3()
    g_qkv.step3()
    g_out.step1()
    g_down.step1()
    small.step4()
    gains_ref[...] = spread_small(small_all[...], place.devices)

    def norm(i, carry):
        rows = pl.ds(pl.multiple_of(i * S, S), S)
        xhat, _ = normed_parts(x_ref[rows, :].astype(F32))
        act_ref[rows, :] = (xhat * gains_ref[0:1, :] + gains_ref[1:2, :]).astype(BF16)
        return carry

    lax.fori_loop(0, spans, norm, 0)
    g_qkv.step4()
    for part in (1, 2):
        cols = slice(part * D, (part + 1) * D)
        block = nn(act_ref[...], qkv_mat[:, cols]).astype(BF16)
        qkv_ref[:, cols] = block
        mean = jnp.sum(block.astype(F32).reshape(spans, S, D), axis=1) * (1.0 / S)
        own_sums[0, :, (part - 1) * D : part * D] = mean.astype(BF16)
    sums = Gather(wires, place, own_sums, sums_all, 1, True)
    sums.step0()
    qkv_ref[:, :D] = nn(act_ref[...], qkv_mat[:, :D]).astype(BF16)
    sums.step1()
    g_up.step1()
    sums.step2()
    sums.step3()
    g_out.step2()
    g_down.step2()
    sums.step4()
    for i in range(PSPANS // MOST):
        two = sums_all[pl.ds(2 * i, 2)].astype(F32)
        psum_ref[MOST * i : MOST * (i + 1), :] = two.reshape(MOST, 2 * D).astype(BF16)
    before = sums_all[pl.ds(lax.rem(place.me + place.devices - 2, place.devices), 1)].astype(F32)
    last = sums_all[pl.ds(lax.rem(place.me + place.devices - 1, place.devices), 1)].astype(F32)
    here = sums_all[pl.ds(place.me, 1)].astype(F32)
    wsum_ref[:MOST, :] = jnp.concatenate([before, last], axis=0).reshape(MOST, 2 * D).astype(BF16)
    wsum_ref[MOST:, :] = jnp.concatenate([here, jnp.zeros_like(here)], axis=0).reshape(MOST, 2 * D).astype(BF16)

    def step(span, carry):
        attend_span(span, first, qkv_ref, psum_ref, wsum_ref, docs_ref, attn_t_ref, probs_ref)
        return carry

    lax.fori_loop(0, spans // 2, step, 0)
    g_out.step3()
    g_down.step3()
    g_up.step2()
    lax.fori_loop(spans // 2, spans, step, 0)
    g_up.step3()
    for g in (g_out, g_down, g_up):
        g.step4()
    wires.finish()


def forward(x, wq, wo, wu, wd, small, docs, with_z):
    tok = x.shape[0]
    spans = tok // S
    deep = lax.axis_size("head")
    side = math.isqrt(lax.axis_size("seq") // 2)
    devices = 2 * side * side * deep
    whole = pl.BlockSpec(memory_space=VMEM)
    n = copies_of_gather(side, deep, True) * 6
    shape = jax.ShapeDtypeStruct
    return pl.pallas_call(
        functools.partial(forward_kernel, with_z),
        out_shape=(
            shape((tok, D), BF16),
            shape((tok, 3 * D), BF16),
            shape((spans * PAIRS, KEYS, 2 * S), BF16),
            shape((D, tok), BF16),
            shape((PSPANS, 2 * D), BF16),
            shape((WIN, 2 * D), BF16),
            shape((D, 3 * D), BF16),
            shape((D, D), BF16),
            shape((4 * D, D), BF16),
            shape((4 * D, D), BF16),
            shape((8, D), F32),
        ),
        in_specs=[whole] * 7,
        out_specs=(whole,) * 11,
        scratch_shapes=[
            pltpu.VMEM((devices, 8, LANES), F32),
            pltpu.VMEM((1, spans, 2 * D), BF16),
            pltpu.VMEM((devices, spans, 2 * D), BF16),
            pltpu.SemaphoreType.DMA((n,)),
            pltpu.SemaphoreType.DMA((n,)),
        ],
        compiler_params=pltpu.CompilerParams(vmem_limit_bytes=VMEM_LIMIT, collective_id=0, has_side_effects=True),
        name="gather_and_attend",
    )(x, wq, wo, wu, wd, small, docs)


def normed_parts(values):
    mean = jnp.mean(values, axis=-1, keepdims=True)
    centred = values - mean
    inverse = lax.rsqrt(jnp.mean(centred * centred, axis=-1, keepdims=True) + EPS)
    return centred * inverse, inverse


def norm_back(dnormed, xhat, inverse, gain):
    grown = dnormed * gain
    along = jnp.mean(grown * xhat, axis=-1, keepdims=True)
    return (grown - jnp.mean(grown, axis=-1, keepdims=True) - xhat * along) * inverse


def gelu_parts(h):
    square = h * h
    t = jnp.tanh(0.7978845608 * (h + 0.044715 * h * square))
    half = 0.5 * (1.0 + t)
    slope = 0.7978845608 * (1.0 + 3 * 0.044715 * square)
    return h * half, half + 0.5 * h * (1.0 - t * t) * slope


TILE = 256
CHUNK = 256


def dense_kernel(
    x_ref, cot_ref, attn_t_ref, out_mat, up_mat, down_mat, gains_ref,
    out_ref, dresid_ref, dattn_ref, gdown_ref, gup_ref, gout_ref, small_ref,
    resid_ref, act_ref, acted_ref, dhid_ref, branch_ref,
):
    tok = x_ref.shape[0]
    hidden_size = up_mat.shape[0]

    def residual(i, carry):
        rows = pl.ds(pl.multiple_of(i * TILE, TILE), TILE)
        resid = x_ref[rows, :].astype(F32) + tn(attn_t_ref[:, rows], out_mat[...])
        resid_ref[rows, :] = resid
        xhat, _ = normed_parts(resid)
        act_ref[rows, :] = (xhat * gains_ref[2:3, :] + gains_ref[3:4, :]).astype(BF16)
        return carry

    lax.fori_loop(0, tok // TILE, residual, 0)

    def feed(i, carry):
        part = pl.ds(pl.multiple_of(i * CHUNK, CHUNK), CHUNK)
        acted, slope = gelu_parts(nt(act_ref[...], up_mat[part, :]))
        acted = acted.astype(BF16)
        acted_ref[:, part] = acted
        dhid = (nt(cot_ref[...], down_mat[part, :]) * slope).astype(BF16)
        dhid_ref[:, part] = dhid
        gdown_ref[part, :] = tn(acted, cot_ref[...]).astype(BF16)
        gup_ref[part, :] = tn(dhid, act_ref[...]).astype(BF16)
        return carry

    lax.fori_loop(0, hidden_size // CHUNK, feed, 0)
    small_ref[...] = jnp.zeros_like(small_ref)

    def finish(i, carry):
        rows = pl.ds(pl.multiple_of(i * TILE, TILE), TILE)
        resid = resid_ref[rows, :]
        out_ref[rows, :] = (resid + nn(acted_ref[rows, :], down_mat[...])).astype(BF16)
        dnormed = nn(dhid_ref[rows, :], up_mat[...])
        xhat, inverse = normed_parts(resid)
        small_ref[2:3, :] += jnp.sum(dnormed * xhat, axis=0, keepdims=True)
        small_ref[3:4, :] += jnp.sum(dnormed, axis=0, keepdims=True)
        dresid = cot_ref[rows, :].astype(F32) + norm_back(dnormed, xhat, inverse, gains_ref[2:3, :])
        dresid_ref[rows, :] = dresid
        branch = dresid.astype(BF16)
        branch_ref[rows, :] = branch
        dattn_ref[rows, :] = nt(branch, out_mat[...]).astype(BF16)
        return carry

    lax.fori_loop(0, tok // TILE, finish, 0)
    gout_ref[...] = nn(attn_t_ref[...], branch_ref[...]).astype(BF16)


def dense(x, cotangent, attn_t, out_mat, up_mat, down_mat, gains):
    tok = x.shape[0]
    hidden_size = up_mat.shape[0]
    whole = pl.BlockSpec(memory_space=VMEM)
    shape = jax.ShapeDtypeStruct
    return pl.pallas_call(
        dense_kernel,
        out_shape=(
            shape((tok, D), BF16),
            shape((tok, D), F32),
            shape((tok, D), BF16),
            shape((hidden_size, D), BF16),
            shape((hidden_size, D), BF16),
            shape((D, D), BF16),
            shape((8, D), F32),
        ),
        in_specs=[whole] * 7,
        out_specs=(whole,) * 7,
        scratch_shapes=[
            pltpu.VMEM((tok, D), F32),
            pltpu.VMEM((tok, D), BF16),
            pltpu.VMEM((tok, hidden_size), BF16),
            pltpu.VMEM((tok, hidden_size), BF16),
            pltpu.VMEM((tok, D), BF16),
        ],
        compiler_params=pltpu.CompilerParams(vmem_limit_bytes=VMEM_LIMIT),
        name="dense",
    )(x, cotangent, attn_t, out_mat, up_mat, down_mat, gains)


def add_into(held, index, others):
    total = held[index].astype(F32)
    for other in others:
        total = total + other.astype(F32)
    held[index] = total.astype(held.dtype)


class Scatter:
    def __init__(self, wires, place, grads, held, hop1, hop2, hopz):
        self.w, self.p, self.grads, self.held = wires, place, grads, held
        self.hop1, self.hop2, self.hopz = hop1, hop2, hopz
        self.group = held.shape[1]

    def at(self, turn, d, e):
        p, n = self.p, self.p.side
        y = lax.rem(p.y + turn * d + (1 - turn) * e, n)
        x = lax.rem(p.x + turn * e + (1 - turn) * d, n)
        return y * n + x

    def rows_of(self, j, core):
        return pl.ds(pl.multiple_of((2 * j + core) * self.group, self.group), self.group)

    def order(self):
        n = self.p.side
        return [(d, e) for d in [*range(1, n), 0] for e in range(n)]

    def step0(self):
        p = self.p
        self.moves = {}
        for d, e in self.order():
            j = self.at(1 - p.c, d, e)
            self.moves[d, e] = self.w.copy(self.grads.at[self.rows_of(j, 1 - p.c)], self.held.at[j], p.sibling())

    def step1(self):
        p, came = self.p, self.moves
        self.moves = {}
        peers = p.peers(0)
        for d, e in self.order():
            j = self.at(p.c, d, e)
            came[d, e].wait_recv()
            add_into(self.held, j, [self.grads[self.rows_of(j, p.c)]])
            if d:
                self.moves[d, e] = self.w.copy(self.held.at[j], self.hop1.at[d - 1, e], peers[d - 1])

    def step2(self):
        p, n, came = self.p, self.p.side, self.moves
        self.moves = []
        peers = p.peers(1)
        for e in [*range(1, n), 0]:
            j = self.at(p.c, 0, e)
            for d in range(1, n):
                came[d, e].wait_recv()
            add_into(self.held, j, [self.hop1[d - 1, e] for d in range(1, n)])
            if e:
                self.moves.append(self.w.copy(self.held.at[j], self.hop2.at[e - 1], peers[e - 1]))

    def step3(self):
        p = self.p
        for move in self.moves:
            move.wait_recv()
        self.mine = self.at(p.c, 0, 0)
        add_into(self.held, self.mine, [self.hop2[e - 1] for e in range(1, p.side)])
        self.moves = []
        if self.hopz is not None:
            self.unit = self.group // p.deep
            for d, other in enumerate(p.peers("z"), 1):
                self.moves.append(self.w.copy(self.held.at[self.mine, self.unit_rows(d)], self.hopz.at[d - 1], other))

    def unit_rows(self, d):
        p = self.p
        return pl.ds(pl.multiple_of(lax.rem(p.z + d, p.deep) * self.unit, self.unit), self.unit)

    def step4(self):
        if self.hopz is None:
            return self.held[self.mine].astype(F32)
        total = self.held[self.mine, self.unit_rows(0)].astype(F32)
        for d, move in enumerate(self.moves):
            move.wait_recv()
            total = total + self.hopz[d].astype(F32)
        return total


def scatter_scratch(side, deep, unit, tail, with_z):
    group = deep * unit
    shapes = [(side * side, group), (side - 1, side, group), (side - 1, group)]
    if with_z:
        shapes.append((deep - 1, unit))
    return [pltpu.VMEM((*shape, *tail), BF16) for shape in shapes]


class Total:
    def __init__(self, wires, place, sums, came):
        self.w, self.p, self.sums, self.came = wires, place, sums, came
        self.slot = 0

    def send(self, level):
        p = self.p
        peers = [[p.sibling()], p.peers(0), p.peers(1), p.peers("z")][level]
        self.moves = []
        for peer in peers:
            self.moves.append(self.w.copy(self.sums.at[level], self.came.at[self.slot], peer))
            self.slot += 1

    def take(self, level):
        total = self.sums[level]
        for i, move in enumerate(self.moves):
            move.wait_recv()
            total = total + self.came[self.slot - len(self.moves) + i]
        self.sums[level + 1] = total


def backward_kernel(
    with_z, grad_scale,
    x_ref, act_ref, qkv_ref, probs_ref, psum_ref, wsum_ref, qkv_mat, gains_ref,
    dattn_ref, dresid_ref, gdown_ref, gup_ref, gout_ref, small_ref,
    dtok_ref, wqkv_ref, wout_ref, wup_ref, wdown_ref, total_ref,
    dqkv_ref, dkv_ref, dsum_ref, dsums_ref, gq_ref, gkv_ref, dnorm_ref, sums_ref, came_ref, send, recv, *held,
):
    place = Place()
    wires = Wires(send, recv)
    tok = x_ref.shape[0]
    spans = tok // S
    per = 4 if with_z else 3
    held = list(held)

    def scatter(grads, z):
        count = 4 if z else 3
        parts = [held.pop(0) for _ in range(count)]
        return Scatter(wires, place, grads, *parts, *([] if z else [None]))

    s_sum = scatter(dsums_ref, True)
    s_down, s_up, s_out, s_q, s_kv = [scatter(g, with_z) for g in (gdown_ref, gup_ref, gout_ref, gq_ref, gkv_ref)]
    place.greet()
    s_down.step0()
    s_up.step0()
    s_out.step0()
    dsum_ref[...] = jnp.zeros_like(dsum_ref)

    def step(span, carry):
        attend_span_back(
            span, qkv_ref, psum_ref, wsum_ref, probs_ref, dattn_ref, dqkv_ref, dkv_ref, dsum_ref
        )
        return carry

    quarter = spans // 4
    lax.fori_loop(0, quarter, step, 0)
    s_down.step1()
    s_up.step1()
    s_out.step1()
    lax.fori_loop(quarter, 2 * quarter, step, 0)
    s_down.step2()
    lax.fori_loop(2 * quarter, 3 * quarter, step, 0)
    s_up.step2()
    s_out.step2()
    s_down.step3()
    lax.fori_loop(3 * quarter, spans, step, 0)

    dsums_ref[...] = jnp.zeros_like(dsums_ref)
    for i in range(3):
        block = lax.rem(place.me + place.devices - 2 + i, place.devices)
        rows = slice(PSPANS + i * spans, PSPANS + (i + 1) * spans)
        dsums_ref[pl.ds(block, 1)] = dsum_ref[rows, :].astype(BF16)[None]
    for i in range(PSPANS // spans):
        dsums_ref[i] = dsum_ref[i * spans : (i + 1) * spans, :].astype(BF16)
    s_sum.step0()
    gq_ref[...] = tn(act_ref[...], dqkv_ref[:, :D]).astype(BF16)
    s_q.step0()
    s_sum.step1()
    s_up.step3()
    s_out.step3()
    dnorm_ref[...] = nt(dqkv_ref[:, :D], qkv_mat[:, :D])
    s_sum.step2()
    wdown_ref[...] = s_down.step4() * grad_scale
    s_sum.step3()
    s_q.step1()
    wup_ref[...] = s_up.step4() * grad_scale
    wout_ref[...] = s_out.step4() * grad_scale
    shares = s_sum.step4()[0] * (1.0 / S)
    for span in range(spans):
        rows = slice(span * S, (span + 1) * S)
        dqkv_ref[rows, D:] = (dkv_ref[rows, :] + shares[span : span + 1, :]).astype(BF16)
    gkv_ref[...] = tn(act_ref[...], dqkv_ref[:, D:]).astype(BF16)
    s_kv.step0()
    s_q.step2()
    sums_ref[0] = small_ref[...]

    def finish(i, carry):
        rows = pl.ds(pl.multiple_of(i * TILE, TILE), TILE)
        dnormed = dnorm_ref[rows, :] + nt(dqkv_ref[rows, D:], qkv_mat[:, D:])
        xhat, inverse = normed_parts(x_ref[rows, :].astype(F32))
        sums_ref[0, 0:1, :] += jnp.sum(dnormed * xhat, axis=0, keepdims=True)
        sums_ref[0, 1:2, :] += jnp.sum(dnormed, axis=0, keepdims=True)
        dtok_ref[rows, :] = dresid_ref[rows, :] + norm_back(dnormed, xhat, inverse, gains_ref[0:1, :])
        return carry

    half = tok // TILE // 2
    lax.fori_loop(0, half, finish, 0)
    s_kv.step1()
    s_q.step3()
    lax.fori_loop(half, 2 * half, finish, 0)
    small = Total(wires, place, sums_ref, came_ref)
    small.send(0)
    s_kv.step2()
    small.take(0)
    small.send(1)
    wqkv_ref[:, :D] = s_q.step4() * grad_scale
    s_kv.step3()
    small.take(1)
    small.send(2)
    small.take(2)
    small.send(3)
    wqkv_ref[:, D:] = s_kv.step4() * grad_scale
    small.take(3)
    total_ref[...] = sums_ref[4] * grad_scale
    wires.finish()


def backward(with_z, grad_scale, x, act, qkv, probs, psum, wsum, qkv_mat, gains, dattn, dresid, gdown, gup, gout, small):
    tok = x.shape[0]
    spans = tok // S
    deep = lax.axis_size("head")
    side = math.isqrt(lax.axis_size("seq") // 2)
    devices = 2 * side * side * deep
    hidden_size = gup.shape[0]
    whole = pl.BlockSpec(memory_space=VMEM)
    shape = jax.ShapeDtypeStruct
    owned = devices if with_z else devices // deep
    peers = 1 + 2 * (side - 1) + deep - 1
    n = 6 * (side * side + (side - 1) * side + side - 1 + deep - 1) + peers
    scratch = scatter_scratch(side, deep, 1, (spans, 2 * D), True)
    for total, columns in ((hidden_size, D), (hidden_size, D), (D, D), (D, D), (D, 2 * D)):
        scratch += scatter_scratch(side, deep, total // devices, (columns,), with_z)
    return pl.pallas_call(
        functools.partial(backward_kernel, with_z, grad_scale),
        out_shape=(
            shape((tok, D), F32),
            shape((D // owned, 3 * D), F32),
            shape((D // owned, D), F32),
            shape((hidden_size // owned, D), F32),
            shape((hidden_size // owned, D), F32),
            shape((8, D), F32),
        ),
        in_specs=[whole] * 14,
        out_specs=(whole,) * 6,
        scratch_shapes=[
            pltpu.VMEM((tok, 3 * D), BF16),
            pltpu.VMEM((tok, 2 * D), F32),
            pltpu.VMEM((PSPANS + WIN, 2 * D), F32),
            pltpu.VMEM((devices, spans, 2 * D), BF16),
            pltpu.VMEM((D, D), BF16),
            pltpu.VMEM((D, 2 * D), BF16),
            pltpu.VMEM((tok, D), F32),
            pltpu.VMEM((5, 8, D), F32),
            pltpu.VMEM((peers, 8, D), F32),
            pltpu.SemaphoreType.DMA((n,)),
            pltpu.SemaphoreType.DMA((n,)),
            *scratch,
        ],
        compiler_params=pltpu.CompilerParams(vmem_limit_bytes=VMEM_LIMIT, collective_id=1, has_side_effects=True),
        name="attend_back_and_scatter",
    )(x, act, qkv, probs, psum, wsum, qkv_mat, gains, dattn, dresid, gdown, gup, gout, small)


def split_parts(weight):
    rows = weight.shape[0]
    return weight.reshape(rows, H, 3, HD).transpose(0, 2, 1, 3).reshape(rows, 3 * D)


def join_parts(weight):
    rows = weight.shape[0]
    return weight.reshape(rows, 3, H, HD).transpose(0, 2, 1, 3).reshape(rows, 3 * D)


def shards(tokens, cotangent, w_qkv, w_out, w_up, w_down, gain_one, shift_one, gain_two, shift_two, span_doc):
    tok = tokens.shape[0]
    devices = lax.axis_size("seq") * lax.axis_size("head")
    me = lax.axis_index("seq") * lax.axis_size("head") + lax.axis_index("head")
    grad_scale = 1.0 / math.sqrt(tok * devices)
    docs = jnp.concatenate([jnp.full((PSPANS + MOST,), -1, jnp.int32), span_doc, jnp.full((MOST,), -1, jnp.int32)])
    docs = jnp.broadcast_to(docs[:, None], (docs.shape[0], S))
    with_z = w_qkv.shape[0] % 16 == 0
    weights = (split_parts(w_qkv), w_out, w_up.T, w_down)
    if not with_z:
        weights = tuple(lax.all_gather(w, "head", axis=0, tiled=True) for w in weights)
    small = jnp.stack([gain_one, shift_one, gain_two, shift_two]).astype(F32)
    width = small.shape[1]
    small = jnp.pad(small, ((0, 4), (0, LANES - width)))[None]
    act, qkv, probs, attn_t, psum, wsum, qkv_mat, out_mat, up_mat, down_mat, gains = forward(
        tokens, *weights, small, docs, with_z
    )
    out_tokens, dresid, dattn, gdown, gup, gout, dsmall = dense(
        tokens, cotangent, attn_t, out_mat, up_mat, down_mat, gains
    )
    d_tokens, d_qkv, d_out, d_up, d_down, total = backward(
        with_z, grad_scale, tokens, act, qkv, probs, psum, wsum, qkv_mat, gains, dattn, dresid, gdown, gup, gout, dsmall
    )
    if not with_z:
        d_qkv, d_out, d_up, d_down = (
            lax.psum_scatter(g, "head", scatter_dimension=0, tiled=True) for g in (d_qkv, d_out, d_up, d_down)
        )
    own = lax.dynamic_slice_in_dim(total, me * width, width, 1)
    return out_tokens, d_tokens, join_parts(d_qkv), d_out, d_up.T, d_down, own[0], own[1], own[2], own[3]


def solution(mesh):
    rows, cols, vec = P(BOTH, None), P(None, BOTH), P(BOTH)
    in_specs = (rows, rows, rows, rows, cols, rows, vec, vec, vec, vec, P())
    out_specs = (rows, rows, rows, rows, cols, rows, vec, vec, vec, vec)
    return jax.shard_map(shards, mesh=mesh, in_specs=in_specs, out_specs=out_specs, check_vma=False)
```

```python
import functools
import math

import jax
import jax.numpy as jnp
from jax import lax
from jax.experimental import pallas as pl
from jax.experimental.pallas import tpu as pltpu
from jax.sharding import PartitionSpec as P

H = 8
HD = 64
D = H * HD
S = 128
MOST = 16
PSPANS = 128
WIN = 2 * MOST
PAIRS = H // 2
LANES = 2 * HD
KEYS = S + PSPANS + WIN
EPS = 1e-05
MASKED = -1e30
F32 = jnp.float32
BF16 = jnp.bfloat16
VMEM = pltpu.MemorySpace.VMEM
VMEM_LIMIT = 67043328
TILE = 256
CHUNK = 256


def nn(a, b):
    return lax.dot_general(a, b, (((1,), (0,)), ((), ())), preferred_element_type=F32)


def nt(a, b):
    return lax.dot_general(a, b, (((1,), (1,)), ((), ())), preferred_element_type=F32)


def tn(a, b):
    return lax.dot_general(a, b, (((0,), (0,)), ((), ())), preferred_element_type=F32)


def summary_bias(first, span, docs_ref):
    index = first + span
    row = lax.broadcasted_iota(jnp.int32, (PSPANS, S), 0)
    prompt = jnp.where(row < index, 0.0, MASKED)
    wrow = first - MOST + lax.broadcasted_iota(jnp.int32, (WIN, S), 0)
    same = docs_ref[...] == docs_ref[pl.ds(span + MOST, 1), :]
    window = jnp.where(same & (wrow >= PSPANS) & (wrow < index), 0.0, MASKED)
    return jnp.concatenate([prompt, window], axis=0).astype(F32)


def head_masks(scale):
    lane = lax.broadcasted_iota(jnp.int32, (1, LANES), 1)
    first = jnp.where(lane < HD, scale, 0.0).astype(BF16)
    second = jnp.where(lane < HD, 0.0, scale).astype(BF16)
    return first, second


def stack_heads(block, masks):
    return jnp.concatenate([block * masks[0], block * masks[1]], axis=0)


def pair_cols(part, pair):
    return slice(part * D + pair * LANES, part * D + (pair + 1) * LANES)


def all_keys(part, pair, rows, qkv_ref, psum_ref, wsum_ref):
    cols = pair_cols(part, pair)
    scols = pair_cols(part - 1, pair)
    return jnp.concatenate([qkv_ref[rows, cols], psum_ref[:, scols], wsum_ref[:, scols]], axis=0)


def unstack(pair_t):
    return jnp.concatenate([pair_t[:HD, :S], pair_t[HD:, S:]], axis=0)


def attend_span(span, first, qkv_ref, psum_ref, wsum_ref, docs_ref, attn_t_ref, probs_ref):
    rows = pl.ds(pl.multiple_of(span * S, S), S)
    bias = summary_bias(first, span, docs_ref)
    key_row = lax.broadcasted_iota(jnp.int32, (S, S), 0)
    query = lax.broadcasted_iota(jnp.int32, (S, S), 1)
    causal = jnp.where(key_row <= query, 0.0, MASKED).astype(F32)
    bias = jnp.concatenate([causal, bias], axis=0)
    bias = jnp.concatenate([bias, bias], axis=1)
    masks = head_masks(1.0 / math.sqrt(HD))
    for pair in range(PAIRS):
        queries = stack_heads(qkv_ref[rows, pair_cols(0, pair)], masks)
        keys = all_keys(1, pair, rows, qkv_ref, psum_ref, wsum_ref)
        vals = all_keys(2, pair, rows, qkv_ref, psum_ref, wsum_ref)
        scores = nt(keys, queries) + bias
        top = jnp.max(scores, axis=0, keepdims=True)
        grown = jnp.exp(scores - top)
        share = 1.0 / jnp.sum(grown, axis=0, keepdims=True)
        probs = (grown * share).astype(BF16)
        probs_ref[span * PAIRS + pair] = probs
        mixed = nn(vals.T, probs)
        attn_t_ref[pair * LANES : (pair + 1) * LANES, rows] = unstack(mixed).astype(BF16)


def attend_span_back(
    span, qkv_ref, psum_ref, wsum_ref, probs_ref, dattn_ref, dq_ref, dkv_ref, dsum_ref
):
    rows = pl.ds(pl.multiple_of(span * S, S), S)
    scale = 1.0 / math.sqrt(HD)
    masks = head_masks(scale)
    ones = head_masks(1.0)
    for pair in range(PAIRS):
        cols = pair_cols(0, pair)
        queries = stack_heads(qkv_ref[rows, cols], masks)
        keys = all_keys(1, pair, rows, qkv_ref, psum_ref, wsum_ref)
        vals = all_keys(2, pair, rows, qkv_ref, psum_ref, wsum_ref)
        grads = stack_heads(dattn_ref[rows, cols], ones)
        probs = probs_ref[span * PAIRS + pair]
        wide = probs.astype(F32)
        dprobs = nt(vals, grads)
        delta = jnp.sum(wide * dprobs, axis=0, keepdims=True)
        dscores = (wide * (dprobs - delta)).astype(BF16)
        dq_t = unstack(nn(keys.T, dscores)) * scale
        dq_ref[rows, cols] = dq_t.T.astype(BF16)
        dkeys = nn(dscores, queries)
        dvals = nn(probs, grads)
        vcols = pair_cols(1, pair)
        dkv_ref[rows, cols] = dkeys[:S]
        dkv_ref[rows, vcols] = dvals[:S]
        dsum_ref[:, cols] += dkeys[S:]
        dsum_ref[:, vcols] += dvals[S:]


MESH = pl.DeviceIdType.MESH
BOTH = ("seq", "head")


class Place:
    def __init__(self):
        seq, self.z = lax.axis_index("seq"), lax.axis_index("head")
        self.side = math.isqrt(lax.axis_size("seq") // 2)
        self.deep = lax.axis_size("head")
        self.devices = lax.axis_size("seq") * self.deep
        self.c = lax.rem(seq, 2)
        self.x = lax.rem(seq // 2, self.side)
        self.y = seq // 2 // self.side
        self.me = seq * self.deep + self.z

    def seq(self, y, x, c):
        return (y * self.side + x) * 2 + c

    def along(self, axis, step):
        n, turn = self.side, self.c if axis == 0 else 1 - self.c
        return lax.rem(self.y + turn * step, n), lax.rem(self.x + (1 - turn) * step, n)

    def sibling(self):
        return (self.seq(self.y, self.x, 1 - self.c), self.z)

    def peers(self, axis):
        if axis == "z":
            seq = self.seq(self.y, self.x, self.c)
            return [(seq, lax.rem(self.z + d, self.deep)) for d in range(1, self.deep)]
        return [(self.seq(*self.along(axis, d), self.c), self.z) for d in range(1, self.side)]

    def greet(self):
        barrier = pltpu.get_barrier_semaphore()
        others = [self.sibling(), *self.peers(0), *self.peers(1), *self.peers("z")]
        for other in others:
            pl.semaphore_signal(barrier, inc=1, device_id=other, device_id_type=MESH)
        pl.semaphore_wait(barrier, len(others))


class Wires:
    def __init__(self, send, recv):
        self.send, self.recv, self.used, self.sent = send, recv, 0, []

    def copy(self, src, dst, device):
        i = self.used
        self.used += 1
        move = pltpu.make_async_remote_copy(
            src_ref=src, dst_ref=dst, send_sem=self.send.at[i], recv_sem=self.recv.at[i],
            device_id=device, device_id_type=MESH,
        )
        move.start()
        self.sent.append(move)
        return move

    def local(self, src, dst):
        i = self.used
        self.used += 1
        move = pltpu.make_async_copy(src, dst, self.send.at[i])
        move.start()
        return move

    def settle(self, moves):
        for move in moves:
            move.wait_send()
        done = {id(move) for move in moves}
        self.sent = [move for move in self.sent if id(move) not in done]

    def finish(self):
        self.settle(list(self.sent))


def copies_of_gather(side, deep, with_z):
    return 1 + (deep - 1 if with_z else 0) + (side - 1) + (side - 1) * side + side * side


class Gather:
    def __init__(self, wires, place, shard, full, rows, with_z):
        self.w, self.p, self.full, self.shard = wires, place, full, shard
        self.rows, self.with_z, self.sent = rows, with_z, []
        self.group = rows * place.deep if with_z else rows

    def block(self, y, x):
        start = self.p.seq(y, x, self.p.c) * self.group
        return self.full.at[pl.ds(pl.multiple_of(start, self.group), self.group)]

    def step0(self):
        p = self.p
        start = pl.multiple_of(p.me * self.rows, self.rows) if self.with_z else p.seq(p.y, p.x, p.c) * self.rows
        own = self.full.at[pl.ds(start, self.rows)]
        self.moves = [self.w.copy(self.shard, own, d) for d in p.peers("z")] if self.with_z else []
        self.sent += self.moves
        self.placed = self.w.local(self.shard, own)

    def _next(self, sources, axis, fresh):
        for move in self.moves:
            move.wait_recv()
        p = self.p
        self.moves = []
        if axis is not None:
            self.moves = [self.w.copy(self.block(*s), self.block(*s), d) for d in p.peers(axis) for s in sources]
        more = [self.w.copy(self.block(*s), self.block(*s), p.sibling()) for s in fresh]
        self.across += more
        self.sent += self.moves + more

    def step1(self):
        self.placed.wait()
        self.across = []
        here = [(self.p.y, self.p.x)]
        self._next(here, 0, here)

    def _line(self, step):
        p, n = self.p, self.p.side
        mine = [p.along(0, d) for d in range(n)]
        if step == 0:
            return mine
        y1, x1 = p.along(1, step)
        turn = 1 - p.c
        return [(turn * y1 + (1 - turn) * y, turn * x + (1 - turn) * x1) for y, x in mine]

    def step2(self):
        line = self._line(0)
        self._next(line, 1, line[1:])

    def step3(self):
        self._next([], None, [s for e in range(1, self.p.side) for s in self._line(e)])

    def step4(self):
        for move in self.across:
            move.wait_recv()


def spread_small(gathered, devices):
    width = D // devices
    table = gathered.reshape(devices * 8, LANES).astype(BF16)
    pick = lax.broadcasted_iota(jnp.int32, (LANES, D), 0) == lax.broadcasted_iota(jnp.int32, (LANES, D), 1) % width
    every = nn(table, jnp.where(pick, 1.0, 0.0).astype(BF16))
    owner = lax.broadcasted_iota(jnp.int32, (devices * 8, D), 0) // 8
    column = lax.broadcasted_iota(jnp.int32, (devices * 8, D), 1) // width
    return jnp.sum(jnp.where(owner == column, every, 0.0).reshape(devices, 8, D), axis=0)


def normed_parts(values):
    mean = jnp.mean(values, axis=-1, keepdims=True)
    centred = values - mean
    inverse = lax.rsqrt(jnp.mean(centred * centred, axis=-1, keepdims=True) + EPS)
    return centred * inverse, inverse


def norm_back(dnormed, xhat, inverse, gain):
    grown = dnormed * gain
    along = jnp.mean(grown * xhat, axis=-1, keepdims=True)
    return (grown - jnp.mean(grown, axis=-1, keepdims=True) - xhat * along) * inverse


def gelu_parts(h):
    square = h * h
    t = jnp.tanh(0.7978845608 * (h + 0.044715 * h * square))
    half = 0.5 * (1.0 + t)
    slope = 0.7978845608 * (1.0 + 3 * 0.044715 * square)
    return h * half, half + 0.5 * h * (1.0 - t * t) * slope


def add_into(held, index, others):
    total = held[index].astype(F32)
    for other in others:
        total = total + other.astype(F32)
    held[index] = total.astype(held.dtype)


class Scatter:
    def __init__(self, wires, place, grads, held, hop1, hop2, hopz):
        self.w, self.p, self.grads, self.held = wires, place, grads, held
        self.hop1, self.hop2, self.hopz = hop1, hop2, hopz
        self.group = held.shape[1]
        self.crossed, self.first, self.second, self.third = {}, {}, {}, []
        n = place.side
        self.line = [*range(1, n), 0]
        self.order = [(d, e) for d in self.line for e in self.line]

    def at(self, turn, d, e):
        p, n = self.p, self.p.side
        y = lax.rem(p.y + turn * d + (1 - turn) * e, n)
        x = lax.rem(p.x + turn * e + (1 - turn) * d, n)
        return y * n + x

    def rows_of(self, j, core):
        return pl.ds(pl.multiple_of((2 * j + core) * self.group, self.group), self.group)

    def cross(self, d, e):
        p = self.p
        j = self.at(1 - p.c, d, e)
        self.crossed[d, e] = self.w.copy(self.grads.at[self.rows_of(j, 1 - p.c)], self.held.at[j], p.sibling())

    def fold(self, d, e):
        p = self.p
        j = self.at(p.c, d, e)
        self.crossed[d, e].wait_recv()
        add_into(self.held, j, [self.grads[self.rows_of(j, p.c)]])
        if d:
            self.first[d, e] = self.w.copy(self.held.at[j], self.hop1.at[d - 1, e], p.peers(0)[d - 1])

    def turn(self, e):
        p, n = self.p, self.p.side
        j = self.at(p.c, 0, e)
        for d in range(1, n):
            self.first[d, e].wait_recv()
        add_into(self.held, j, [self.hop1[d - 1, e] for d in range(1, n)])
        if e:
            self.second[e] = self.w.copy(self.held.at[j], self.hop2.at[e - 1], p.peers(1)[e - 1])

    def step0(self):
        for d, e in self.order:
            self.cross(d, e)

    def step1(self):
        for d, e in self.order:
            self.fold(d, e)

    def step2(self):
        for e in self.line:
            self.turn(e)

    def step3(self):
        p = self.p
        for move in self.second.values():
            move.wait_recv()
        self.mine = self.at(p.c, 0, 0)
        add_into(self.held, self.mine, [self.hop2[e - 1] for e in range(1, p.side)])
        if self.hopz is not None:
            self.unit = self.group // p.deep
            for d, other in enumerate(p.peers("z"), 1):
                self.third.append(self.w.copy(self.held.at[self.mine, self.unit_rows(d)], self.hopz.at[d - 1], other))

    def unit_rows(self, d):
        p = self.p
        return pl.ds(pl.multiple_of(lax.rem(p.z + d, p.deep) * self.unit, self.unit), self.unit)

    def step4(self):
        if self.hopz is None:
            return self.held[self.mine].astype(F32)
        total = self.held[self.mine, self.unit_rows(0)].astype(F32)
        for d, move in enumerate(self.third):
            move.wait_recv()
            total = total + self.hopz[d].astype(F32)
        return total


def scatter_scratch(side, deep, unit, tail, with_z):
    group = deep * unit
    shapes = [(side * side, group), (side - 1, side, group), (side - 1, group)]
    if with_z:
        shapes.append((deep - 1, unit))
    return [pltpu.VMEM((*shape, *tail), BF16) for shape in shapes]


class Total:
    def __init__(self, wires, place, sums, came):
        self.w, self.p, self.sums, self.came = wires, place, sums, came
        self.slot = 0

    def send(self, level):
        p = self.p
        peers = [[p.sibling()], p.peers(0), p.peers(1), p.peers("z")][level]
        self.moves = []
        for peer in peers:
            self.moves.append(self.w.copy(self.sums.at[level], self.came.at[self.slot], peer))
            self.slot += 1

    def take(self, level):
        total = self.sums[level]
        for i, move in enumerate(self.moves):
            move.wait_recv()
            total = total + self.came[self.slot - len(self.moves) + i]
        self.sums[level + 1] = total


def loop(start, stop, body):
    def step(i, carry):
        body(i)
        return carry

    lax.fori_loop(start, stop, step, 0)


def tile_rows(i, size):
    return pl.ds(pl.multiple_of(i * size, size), size)


def layer_kernel(
    with_z, grad_scale,
    x_ref, cot_ref, wq_ref, wkv_ref, wo_ref, wu_ref, wd_ref, small_ref, docs_ref,
    out_ref, dtok_ref, dwq_ref, dwkv_ref, dwo_ref, dwu_ref, dwd_ref, total_ref,
    q_mat, kv_mat, out_mat, up_mat, down_mat, gains_ref, small_all, own_sums, sums_all, psum_ref, wsum_ref,
    act_ref, qkv_ref, probs_ref, attn_t_ref, resid_ref, act2_ref, acted_ref, dhid_ref, dattn_ref,
    gdown_ref, gup_ref, gout_ref, gq_ref, gkv_ref, dkv_ref, dsum_ref, sums_ref, came_ref, send, recv, *held,
):
    place = Place()
    wires = Wires(send, recv)
    tok = x_ref.shape[0]
    spans = tok // S
    first = place.me * spans
    held = list(held)

    def gather(shard, full):
        return Gather(wires, place, shard, full, shard.shape[0], with_z)

    def scatter(grads, z):
        parts = [held.pop(0) for _ in range(4 if z else 3)]
        return Scatter(wires, place, grads, *parts, *([] if z else [None]))

    small = Gather(wires, place, small_ref, small_all, 1, True)
    sums = Gather(wires, place, own_sums, sums_all, 1, True)
    g_kv, g_q, g_out = gather(wkv_ref, kv_mat), gather(wq_ref, q_mat), gather(wo_ref, out_mat)
    g_down, g_up = gather(wd_ref, down_mat), gather(wu_ref, up_mat)
    dsums_ref = sums_all
    s_sum = scatter(dsums_ref, True)
    s_down, s_up, s_out, s_q, s_kv = [scatter(g, with_z) for g in (gdown_ref, gup_ref, gout_ref, gq_ref, gkv_ref)]

    place.greet()
    for g in (small, g_kv, g_q, g_out, g_down, g_up):
        g.step0()
    small.step1()
    g_kv.step1()
    g_q.step1()
    small.step2()
    g_kv.step2()
    g_q.step2()
    small.step3()
    g_kv.step3()
    small.step4()
    gains_ref[...] = spread_small(small_all[...], place.devices)

    def norm(i):
        rows = tile_rows(i, S)
        xhat, _ = normed_parts(x_ref[rows, :].astype(F32))
        act_ref[rows, :] = (xhat * gains_ref[0:1, :] + gains_ref[1:2, :]).astype(BF16)

    loop(0, spans, norm)
    g_kv.step4()
    g_q.step3()
    g_out.step1()
    for part in (0, 1):
        block = nn(act_ref[...], kv_mat[:, part * D : (part + 1) * D]).astype(BF16)
        qkv_ref[:, (part + 1) * D : (part + 2) * D] = block
        mean = jnp.sum(block.astype(F32).reshape(spans, S, D), axis=1) * (1.0 / S)
        own_sums[0, :, part * D : (part + 1) * D] = mean.astype(BF16)
        if part == 0:
            g_down.step1()
    sums.step0()
    g_q.step4()
    qkv_ref[:, :D] = nn(act_ref[...], q_mat[...]).astype(BF16)
    sums.step1()
    g_out.step2()
    g_down.step2()
    sums.step2()
    g_up.step1()
    sums.step3()
    sums.step4()
    for i in range(PSPANS // MOST):
        two = sums_all[pl.ds(2 * i, 2)].astype(F32)
        psum_ref[MOST * i : MOST * (i + 1), :] = two.reshape(MOST, 2 * D).astype(BF16)
    before = sums_all[pl.ds(lax.rem(place.me + place.devices - 2, place.devices), 1)].astype(F32)
    last = sums_all[pl.ds(lax.rem(place.me + place.devices - 1, place.devices), 1)].astype(F32)
    here = sums_all[pl.ds(place.me, 1)].astype(F32)
    wsum_ref[:MOST, :] = jnp.concatenate([before, last], axis=0).reshape(MOST, 2 * D).astype(BF16)
    wsum_ref[MOST:, :] = jnp.concatenate([here, jnp.zeros_like(here)], axis=0).reshape(MOST, 2 * D).astype(BF16)

    def attend(span):
        attend_span(span, first, qkv_ref, psum_ref, wsum_ref, docs_ref, attn_t_ref, probs_ref)

    quarter = spans // 4
    loop(0, quarter, attend)
    g_up.step2()
    g_out.step3()
    loop(quarter, 2 * quarter, attend)
    g_down.step3()
    loop(2 * quarter, 3 * quarter, attend)
    g_up.step3()
    loop(3 * quarter, spans, attend)
    g_out.step4()

    def residual(i):
        rows = tile_rows(i, TILE)
        resid = x_ref[rows, :].astype(F32) + tn(attn_t_ref[:, rows], out_mat[...])
        resid_ref[rows, :] = resid
        xhat, _ = normed_parts(resid)
        act2_ref[rows, :] = (xhat * gains_ref[2:3, :] + gains_ref[3:4, :]).astype(BF16)

    loop(0, tok // TILE, residual)
    g_down.step4()
    g_up.step4()

    def feed(i):
        part = tile_rows(i, CHUNK)
        acted, slope = gelu_parts(nt(act2_ref[...], up_mat[part, :]))
        acted = acted.astype(BF16)
        acted_ref[:, part] = acted
        dhid = (nt(cot_ref[...], down_mat[part, :]) * slope).astype(BF16)
        dhid_ref[:, part] = dhid
        gdown_ref[part, :] = tn(acted, cot_ref[...]).astype(BF16)
        gup_ref[part, :] = tn(dhid, act2_ref[...]).astype(BF16)

    both = (s_down, s_up)
    if s_up.group == CHUNK:
        for d, e in s_up.order:
            theirs = 2 * s_up.at(1 - place.c, d, e) + 1 - place.c
            ours = 2 * s_up.at(place.c, d, e) + place.c
            loop(0, 2, lambda i: feed(theirs + i * (ours - theirs)))
            for s in both:
                s.cross(d, e)
            for s in both:
                s.fold(d, e)
            if d == 0:
                for s in both:
                    s.turn(e)
    else:
        loop(0, up_mat.shape[0] // CHUNK, feed)
        for s in both:
            s.step0()
        for s in both:
            s.step1()
        for s in both:
            s.step2()
    sums_ref[...] = jnp.zeros_like(sums_ref)

    def finish(i):
        rows = tile_rows(i, TILE)
        dnormed = nn(dhid_ref[rows, :], up_mat[...])
        xhat, inverse = normed_parts(resid_ref[rows, :])
        sums_ref[0, 2:3, :] += jnp.sum(dnormed * xhat, axis=0, keepdims=True)
        sums_ref[0, 3:4, :] += jnp.sum(dnormed, axis=0, keepdims=True)
        dresid = cot_ref[rows, :].astype(F32) + norm_back(dnormed, xhat, inverse, gains_ref[2:3, :])
        dtok_ref[rows, :] = dresid
        branch = dresid.astype(BF16)
        act2_ref[rows, :] = branch
        dattn_ref[rows, :] = nt(branch, out_mat[...]).astype(BF16)

    loop(0, tok // TILE, finish)
    for s in both:
        s.step3()
    gout_ref[...] = nn(attn_t_ref[...], act2_ref[...]).astype(BF16)
    s_out.step0()
    dsum_ref[...] = jnp.zeros_like(dsum_ref)

    def attend_back(span):
        attend_span_back(
            span, qkv_ref, psum_ref, wsum_ref, probs_ref, dattn_ref, dhid_ref, dkv_ref, dsum_ref
        )

    loop(0, quarter, attend_back)
    s_out.step1()
    loop(quarter, 2 * quarter, attend_back)
    s_out.step2()
    loop(2 * quarter, 3 * quarter, attend_back)
    s_out.step3()
    loop(3 * quarter, spans, attend_back)

    wires.settle(sums.sent)
    dsums_ref[...] = jnp.zeros_like(dsums_ref)
    for i in range(3):
        block = lax.rem(place.me + place.devices - 2 + i, place.devices)
        rows = slice(PSPANS + i * spans, PSPANS + (i + 1) * spans)
        dsums_ref[pl.ds(block, 1)] = dsum_ref[rows, :].astype(BF16)[None]
    for i in range(PSPANS // spans):
        dsums_ref[i] = dsum_ref[i * spans : (i + 1) * spans, :].astype(BF16)
    s_sum.step0()
    gq_ref[...] = tn(act_ref[...], dhid_ref[:, :D]).astype(BF16)
    s_sum.step1()
    s_q.step0()
    s_sum.step2()
    s_q.step1()
    dwd_ref[...] = s_down.step4() * grad_scale
    dwu_ref[...] = s_up.step4() * grad_scale
    dwo_ref[...] = s_out.step4() * grad_scale
    s_sum.step3()
    s_q.step2()
    shares = s_sum.step4()[0] * (1.0 / S)
    for span in range(spans):
        rows = slice(span * S, (span + 1) * S)
        dhid_ref[rows, D : 3 * D] = (dkv_ref[rows, :] + shares[span : span + 1, :]).astype(BF16)
    gkv_ref[...] = tn(act_ref[...], dhid_ref[:, D : 3 * D]).astype(BF16)
    s_kv.step0()
    s_q.step3()

    def last(i):
        rows = tile_rows(i, TILE)
        dnormed = nt(dhid_ref[rows, :D], q_mat[...]) + nt(dhid_ref[rows, D : 3 * D], kv_mat[...])
        xhat, inverse = normed_parts(x_ref[rows, :].astype(F32))
        sums_ref[0, 0:1, :] += jnp.sum(dnormed * xhat, axis=0, keepdims=True)
        sums_ref[0, 1:2, :] += jnp.sum(dnormed, axis=0, keepdims=True)
        dtok_ref[rows, :] += norm_back(dnormed, xhat, inverse, gains_ref[0:1, :])

    def output(i):
        rows = tile_rows(i, TILE)
        out_ref[rows, :] = (resid_ref[rows, :] + nn(acted_ref[rows, :], down_mat[...])).astype(BF16)

    half = tok // TILE // 2
    loop(0, half, last)
    s_kv.step1()
    loop(half, 2 * half, last)
    total = Total(wires, place, sums_ref, came_ref)
    total.send(0)
    loop(0, half, output)
    total.take(0)
    total.send(1)
    s_kv.step2()
    loop(half, 2 * half, output)
    total.take(1)
    total.send(2)
    s_kv.step3()
    dwq_ref[...] = s_q.step4() * grad_scale
    total.take(2)
    total.send(3)
    dwkv_ref[...] = s_kv.step4() * grad_scale
    total.take(3)
    total_ref[...] = sums_ref[4] * grad_scale
    wires.finish()


def layer(with_z, grad_scale, x, cotangent, wq, wkv, wo, wu, wd, small, docs):
    tok = x.shape[0]
    spans = tok // S
    deep = lax.axis_size("head")
    side = math.isqrt(lax.axis_size("seq") // 2)
    devices = 2 * side * side * deep
    owned = devices if with_z else devices // deep
    hidden_size = wu.shape[0] * owned
    whole = pl.BlockSpec(memory_space=VMEM)
    shape = jax.ShapeDtypeStruct
    peers = 1 + 2 * (side - 1) + deep - 1
    n = 7 * copies_of_gather(side, deep, True) + 7
    n += 6 * (side * side + (side - 1) * side + side - 1 + deep - 1) + peers
    held = scatter_scratch(side, deep, 1, (spans, 2 * D), True)
    for total, columns in ((hidden_size, D), (hidden_size, D), (D, D), (D, D), (D, 2 * D)):
        held += scatter_scratch(side, deep, total // devices, (columns,), with_z)
    return pl.pallas_call(
        functools.partial(layer_kernel, with_z, grad_scale),
        out_shape=(
            shape((tok, D), BF16),
            shape((tok, D), F32),
            shape((D // owned, D), F32),
            shape((D // owned, 2 * D), F32),
            shape((D // owned, D), F32),
            shape((hidden_size // owned, D), F32),
            shape((hidden_size // owned, D), F32),
            shape((8, D), F32),
        ),
        in_specs=[whole] * 9,
        out_specs=(whole,) * 8,
        scratch_shapes=[
            pltpu.VMEM((D, D), BF16),
            pltpu.VMEM((D, 2 * D), BF16),
            pltpu.VMEM((D, D), BF16),
            pltpu.VMEM((hidden_size, D), BF16),
            pltpu.VMEM((hidden_size, D), BF16),
            pltpu.VMEM((8, D), F32),
            pltpu.VMEM((devices, 8, LANES), F32),
            pltpu.VMEM((1, spans, 2 * D), BF16),
            pltpu.VMEM((devices, spans, 2 * D), BF16),
            pltpu.VMEM((PSPANS, 2 * D), BF16),
            pltpu.VMEM((WIN, 2 * D), BF16),
            pltpu.VMEM((tok, D), BF16),
            pltpu.VMEM((tok, 3 * D), BF16),
            pltpu.VMEM((spans * PAIRS, KEYS, 2 * S), BF16),
            pltpu.VMEM((D, tok), BF16),
            pltpu.VMEM((tok, D), F32),
            pltpu.VMEM((tok, D), BF16),
            pltpu.VMEM((tok, hidden_size), BF16),
            pltpu.VMEM((tok, hidden_size), BF16),
            pltpu.VMEM((tok, D), BF16),
            pltpu.VMEM((hidden_size, D), BF16),
            pltpu.VMEM((hidden_size, D), BF16),
            pltpu.VMEM((D, D), BF16),
            pltpu.VMEM((D, D), BF16),
            pltpu.VMEM((D, 2 * D), BF16),
            pltpu.VMEM((tok, 2 * D), F32),
            pltpu.VMEM((PSPANS + WIN, 2 * D), F32),
            pltpu.VMEM((5, 8, D), F32),
            pltpu.VMEM((peers, 8, D), F32),
            pltpu.SemaphoreType.DMA((n,)),
            pltpu.SemaphoreType.DMA((n,)),
            *held,
        ],
        compiler_params=pltpu.CompilerParams(vmem_limit_bytes=VMEM_LIMIT, collective_id=0, has_side_effects=True),
        name="mega_layer",
    )(x, cotangent, wq, wkv, wo, wu, wd, small, docs)


def split_parts(weight):
    rows = weight.shape[0]
    return weight.reshape(rows, H, 3, HD).transpose(0, 2, 1, 3).reshape(rows, 3 * D)


def join_parts(weight):
    rows = weight.shape[0]
    return weight.reshape(rows, 3, H, HD).transpose(0, 2, 1, 3).reshape(rows, 3 * D)


def shards(tokens, cotangent, w_qkv, w_out, w_up, w_down, gain_one, shift_one, gain_two, shift_two, span_doc):
    tok = tokens.shape[0]
    devices = lax.axis_size("seq") * lax.axis_size("head")
    me = lax.axis_index("seq") * lax.axis_size("head") + lax.axis_index("head")
    grad_scale = 1.0 / math.sqrt(tok * devices)
    docs = jnp.concatenate([jnp.full((PSPANS + MOST,), -1, jnp.int32), span_doc, jnp.full((MOST,), -1, jnp.int32)])
    docs = lax.dynamic_slice_in_dim(docs, me * (tok // S), WIN, 0)
    docs = jnp.broadcast_to(docs[:, None], (WIN, S))
    with_z = w_qkv.shape[0] % 16 == 0
    w_qkv = split_parts(w_qkv)
    weights = (w_qkv[:, :D], w_qkv[:, D:], w_out, w_up.T, w_down)
    if not with_z:
        weights = tuple(lax.all_gather(w, "head", axis=0, tiled=True) for w in weights)
    small = jnp.stack([gain_one, shift_one, gain_two, shift_two]).astype(F32)
    width = small.shape[1]
    small = jnp.pad(small, ((0, 4), (0, LANES - width)))[None]
    out_tokens, d_tokens, d_q, d_kv, d_out, d_up, d_down, total = layer(
        with_z, grad_scale, tokens, cotangent, *weights, small, docs
    )
    d_qkv = jnp.concatenate([d_q, d_kv], axis=1)
    if not with_z:
        d_qkv, d_out, d_up, d_down = (
            lax.psum_scatter(g, "head", scatter_dimension=0, tiled=True) for g in (d_qkv, d_out, d_up, d_down)
        )
    own = lax.dynamic_slice_in_dim(total, me * width, width, 1)
    return out_tokens, d_tokens, join_parts(d_qkv), d_out, d_up.T, d_down, own[0], own[1], own[2], own[3]


def solution(mesh):
    rows, cols, vec = P(BOTH, None), P(None, BOTH), P(BOTH)
    in_specs = (rows, rows, rows, rows, cols, rows, vec, vec, vec, vec, P())
    out_specs = (rows, rows, rows, rows, cols, rows, vec, vec, vec, vec)
    return jax.shard_map(shards, mesh=mesh, in_specs=in_specs, out_specs=out_specs, check_vma=False)
```

```python
import functools
import math

import jax
import jax.numpy as jnp
from jax import lax
from jax.experimental import pallas as pl
from jax.experimental.pallas import tpu as pltpu
from jax.sharding import PartitionSpec as P

H = 8
HD = 64
D = H * HD
S = 128
MOST = 16
PSPANS = 128
WIN = 2 * MOST
PAIRS = H // 2
LANES = 2 * HD
FAR = PSPANS + WIN
KEYS = S + FAR
EPS = 1e-05
MASKED = -1e30
F32 = jnp.float32
BF16 = jnp.bfloat16
VMEM = pltpu.MemorySpace.VMEM
VMEM_LIMIT = 67043328
TILE = 256
CHUNK = 256


def nn(a, b):
    return lax.dot_general(a, b, (((1,), (0,)), ((), ())), preferred_element_type=F32)


def nt(a, b):
    return lax.dot_general(a, b, (((1,), (1,)), ((), ())), preferred_element_type=F32)


def tn(a, b):
    return lax.dot_general(a, b, (((0,), (0,)), ((), ())), preferred_element_type=F32)


def loop(start, stop, body):
    def step(i, carry):
        body(i)
        return carry

    lax.fori_loop(start, stop, step, 0)


def tile_rows(i, size):
    return pl.ds(pl.multiple_of(i * size, size), size)


def summary_bias(first, span, docs_ref):
    index = first + span
    row = lax.broadcasted_iota(jnp.int32, (PSPANS, S), 0)
    prompt = jnp.where(row < index, 0.0, MASKED)
    wrow = first - MOST + lax.broadcasted_iota(jnp.int32, (WIN, S), 0)
    same = docs_ref[...] == docs_ref[pl.ds(span + MOST, 1), :]
    window = jnp.where(same & (wrow >= PSPANS) & (wrow < index), 0.0, MASKED)
    return jnp.concatenate([prompt, window], axis=0).astype(F32)


def window_docs(first, spans, span_doc_ref):
    row = lax.broadcasted_iota(jnp.int32, (WIN, S), 0)
    docs = jnp.full((WIN, S), -1, jnp.int32)
    for i in range(MOST + spans):
        at = first - MOST - PSPANS + i
        docs = jnp.where((row == i) & (at >= 0), span_doc_ref[jnp.maximum(at, 0)], docs)
    return docs


def head_masks(scale):
    lane = lax.broadcasted_iota(jnp.int32, (1, LANES), 1)
    first = jnp.where(lane < HD, scale, 0.0).astype(BF16)
    second = jnp.where(lane < HD, 0.0, scale).astype(BF16)
    return first, second


def stack_heads(block, masks):
    return jnp.concatenate([block * masks[0], block * masks[1]], axis=0)


def pair_cols(part, pair):
    return slice(part * D + pair * LANES, part * D + (pair + 1) * LANES)


def unstack(pair_t):
    return jnp.concatenate([pair_t[:HD, :S], pair_t[HD:, S:]], axis=0)


def both_heads(pair):
    return slice(pair * 2 * S, (pair + 1) * 2 * S)


def span_scores(span, qkv_ref, scores_ref):
    rows = tile_rows(span, S)
    key_row = lax.broadcasted_iota(jnp.int32, (S, S), 0)
    query = lax.broadcasted_iota(jnp.int32, (S, S), 1)
    causal = jnp.where(key_row <= query, 0.0, MASKED).astype(F32)
    causal = jnp.concatenate([causal, causal], axis=1)
    masks = head_masks(1.0 / math.sqrt(HD))
    for pair in range(PAIRS):
        queries = stack_heads(qkv_ref[rows, pair_cols(0, pair)], masks)
        scores_ref[rows, both_heads(pair)] = nt(qkv_ref[rows, pair_cols(1, pair)], queries) + causal


def attend_span(span, first, qkv_ref, sums_ref, sums_t_ref, docs_ref, scores_ref, attn_t_ref, probs_ref):
    rows = tile_rows(span, S)
    bias = summary_bias(first, span, docs_ref)
    bias = jnp.concatenate([bias, bias], axis=1)
    masks = head_masks(1.0 / math.sqrt(HD))
    for pair in range(PAIRS):
        queries = stack_heads(qkv_ref[rows, pair_cols(0, pair)], masks)
        own = scores_ref[rows, both_heads(pair)]
        far = nt(sums_ref[:, pair_cols(0, pair)], queries) + bias
        top = jnp.maximum(jnp.max(own, axis=0, keepdims=True), jnp.max(far, axis=0, keepdims=True))
        own, far = jnp.exp(own - top), jnp.exp(far - top)
        share = 1.0 / (jnp.sum(own, axis=0, keepdims=True) + jnp.sum(far, axis=0, keepdims=True))
        probs = jnp.concatenate([(own * share).astype(BF16), (far * share).astype(BF16)], axis=0)
        probs_ref[span * PAIRS + pair] = probs
        vals_t = jnp.concatenate([qkv_ref[rows, pair_cols(2, pair)].T, sums_t_ref[pair_cols(1, pair), :]], axis=1)
        attn_t_ref[pair * LANES : (pair + 1) * LANES, rows] = unstack(nn(vals_t, probs)).astype(BF16)


def summary_back(span, qkv_ref, sums_ref, probs_ref, attn_t_ref, dattn_ref, delta_ref, dsum_ref):
    rows = tile_rows(span, S)
    masks = head_masks(1.0 / math.sqrt(HD))
    ones = head_masks(1.0)
    for pair in range(PAIRS):
        cols, vcols = pair_cols(0, pair), pair_cols(1, pair)
        block = dattn_ref[rows, cols]
        each = block.T.astype(F32) * attn_t_ref[pair * LANES : (pair + 1) * LANES, rows].astype(F32)
        delta = jnp.concatenate(
            [jnp.sum(each[:HD], axis=0, keepdims=True), jnp.sum(each[HD:], axis=0, keepdims=True)], axis=1
        )
        delta_ref[pl.ds(span * PAIRS + pair, 1), :] = delta
        queries = stack_heads(qkv_ref[rows, cols], masks)
        grads = stack_heads(block, ones)
        probs = probs_ref[span * PAIRS + pair, S:, :]
        dprobs = nt(sums_ref[:, vcols], grads)
        dscores = (probs.astype(F32) * (dprobs - delta)).astype(BF16)
        dsum_ref[:, cols] += nn(dscores, queries)
        dsum_ref[:, vcols] += nn(probs, grads)
        probs_ref[span * PAIRS + pair, S:, :] = dscores


def span_back(span, qkv_ref, sums_t_ref, probs_ref, dattn_ref, delta_ref, dqkv_ref, dkv_ref):
    rows = tile_rows(span, S)
    scale = 1.0 / math.sqrt(HD)
    masks = head_masks(scale)
    ones = head_masks(1.0)
    for pair in range(PAIRS):
        cols, vcols = pair_cols(0, pair), pair_cols(1, pair)
        queries = stack_heads(qkv_ref[rows, cols], masks)
        grads = stack_heads(dattn_ref[rows, cols], ones)
        probs = probs_ref[span * PAIRS + pair, :S, :]
        dprobs = nt(qkv_ref[rows, pair_cols(2, pair)], grads)
        delta = delta_ref[pl.ds(span * PAIRS + pair, 1), :]
        dscores = (probs.astype(F32) * (dprobs - delta)).astype(BF16)
        dkv_ref[rows, cols] = nn(dscores, queries)
        dkv_ref[rows, vcols] = nn(probs, grads)
        every = jnp.concatenate([dscores, probs_ref[span * PAIRS + pair, S:, :]], axis=0)
        keys_t = jnp.concatenate([qkv_ref[rows, pair_cols(1, pair)].T, sums_t_ref[cols, :]], axis=1)
        dq_t = unstack(nn(keys_t, every)) * scale
        dqkv_ref[rows, cols] = dq_t.T.astype(BF16)


def split_heads(block, parts):
    low = lax.broadcasted_iota(jnp.int32, (1, LANES), 1) < HD
    for pair in range(PAIRS):
        one, two, three = [block[:, (3 * pair + i) * LANES : (3 * pair + i + 1) * LANES].astype(F32) for i in range(3)]
        mixed = jnp.where(low, one, two), pltpu.roll(jnp.where(low, three, one), HD, 1), jnp.where(low, two, three)
        for part, value in zip(parts, mixed):
            part[:, pair * LANES : (pair + 1) * LANES] = value.astype(part.dtype)


def join_heads(parts, out_ref):
    low = lax.broadcasted_iota(jnp.int32, (1, LANES), 1) < HD
    for pair in range(PAIRS):
        q, k, v = [part[:, pair * LANES : (pair + 1) * LANES] for part in parts]
        k = pltpu.roll(k, HD, 1)
        for i, value in enumerate((jnp.where(low, q, k), jnp.where(low, v, q), jnp.where(low, k, v))):
            out_ref[:, (3 * pair + i) * LANES : (3 * pair + i + 1) * LANES] = value


MESH = pl.DeviceIdType.MESH
BOTH = ("seq", "head")


class Place:
    def __init__(self):
        seq, self.z = lax.axis_index("seq"), lax.axis_index("head")
        self.side = math.isqrt(lax.axis_size("seq") // 2)
        self.deep = lax.axis_size("head")
        self.devices = lax.axis_size("seq") * self.deep
        self.c = lax.rem(seq, 2)
        self.x = lax.rem(seq // 2, self.side)
        self.y = seq // 2 // self.side
        self.me = seq * self.deep + self.z

    def seq(self, y, x, c):
        return (y * self.side + x) * 2 + c

    def along(self, axis, step):
        n, turn = self.side, self.c if axis == 0 else 1 - self.c
        return lax.rem(self.y + turn * step, n), lax.rem(self.x + (1 - turn) * step, n)

    def sibling(self):
        return (self.seq(self.y, self.x, 1 - self.c), self.z)

    def peers(self, axis):
        if axis == "z":
            seq = self.seq(self.y, self.x, self.c)
            return [(seq, lax.rem(self.z + d, self.deep)) for d in range(1, self.deep)]
        return [(self.seq(*self.along(axis, d), self.c), self.z) for d in range(1, self.side)]

    def greet(self):
        barrier = pltpu.get_barrier_semaphore()
        others = [self.sibling(), *self.peers(0), *self.peers(1), *self.peers("z")]
        for other in others:
            pl.semaphore_signal(barrier, inc=1, device_id=other, device_id_type=MESH)
        pl.semaphore_wait(barrier, len(others))


class Wires:
    def __init__(self, send, recv):
        self.send, self.recv, self.used, self.sent = send, recv, 0, []

    def copy(self, src, dst, device):
        i = self.used
        self.used += 1
        move = pltpu.make_async_remote_copy(
            src_ref=src, dst_ref=dst, send_sem=self.send.at[i], recv_sem=self.recv.at[i],
            device_id=device, device_id_type=MESH,
        )
        move.start()
        self.sent.append(move)
        return move

    def local(self, src, dst):
        i = self.used
        self.used += 1
        move = pltpu.make_async_copy(src, dst, self.send.at[i])
        move.start()
        return move

    def settle(self, moves):
        for move in moves:
            move.wait_send()
        done = {id(move) for move in moves}
        self.sent = [move for move in self.sent if id(move) not in done]

    def finish(self):
        self.settle(list(self.sent))


def copies_of_gather(side, deep, with_z):
    return 1 + (deep - 1 if with_z else 0) + (side - 1) + (side - 1) * side + side * side


class Gather:
    def __init__(self, wires, place, shard, full, rows, with_z):
        self.w, self.p, self.full, self.shard = wires, place, full, shard
        self.rows, self.with_z, self.sent = rows, with_z, []
        self.group = rows * place.deep if with_z else rows

    def block(self, y, x):
        start = self.p.seq(y, x, self.p.c) * self.group
        return self.full.at[pl.ds(pl.multiple_of(start, self.group), self.group)]

    def step0(self):
        p = self.p
        start = pl.multiple_of(p.me * self.rows, self.rows) if self.with_z else p.seq(p.y, p.x, p.c) * self.rows
        own = self.full.at[pl.ds(start, self.rows)]
        self.moves = [self.w.copy(self.shard, own, d) for d in p.peers("z")] if self.with_z else []
        self.sent += self.moves
        self.placed = self.w.local(self.shard, own)

    def _line(self, step):
        p, n = self.p, self.p.side
        y1, x1 = p.along(1, step)
        turn = 1 - p.c
        mine = [p.along(0, d) for d in range(n)]
        return [(turn * y1 + (1 - turn) * y, turn * x + (1 - turn) * x1) for y, x in mine]

    def _send(self, place, device):
        move = self.w.copy(self.block(*place), self.block(*place), device)
        self.sent.append(move)
        return move

    def step1(self):
        p = self.p
        for move in self.moves:
            move.wait_recv()
        self.placed.wait()
        own = (p.y, p.x)
        self.moves = [self._send(own, d) for d in p.peers(0)]
        self.turned = [self._send(own, d) for d in p.peers(1)]
        self.across = [self._send(own, p.sibling())]

    def step2(self):
        p = self.p
        for move in self.moves:
            move.wait_recv()
        line = self._line(0)[1:]
        self.turned += [self._send(place, d) for d in p.peers(1) for place in line]
        self.across += [self._send(place, p.sibling()) for place in line]

    def step3(self):
        for move in self.turned:
            move.wait_recv()
        p = self.p
        self.across += [self._send(place, p.sibling()) for e in range(1, p.side) for place in self._line(e)]

    def step4(self):
        for move in self.across:
            move.wait_recv()


def spread_small(gathered, devices):
    width = D // devices
    table = gathered.reshape(devices * 8, LANES).astype(BF16)
    pick = lax.broadcasted_iota(jnp.int32, (LANES, D), 0) == lax.broadcasted_iota(jnp.int32, (LANES, D), 1) % width
    every = nn(table, jnp.where(pick, 1.0, 0.0).astype(BF16))
    owner = lax.broadcasted_iota(jnp.int32, (devices * 8, D), 0) // 8
    column = lax.broadcasted_iota(jnp.int32, (devices * 8, D), 1) // width
    return jnp.sum(jnp.where(owner == column, every, 0.0).reshape(devices, 8, D), axis=0)


def normed_parts(values):
    mean = jnp.mean(values, axis=-1, keepdims=True)
    centred = values - mean
    inverse = lax.rsqrt(jnp.mean(centred * centred, axis=-1, keepdims=True) + EPS)
    return centred * inverse, inverse


def norm_back(dnormed, xhat, inverse, gain):
    grown = dnormed * gain
    along = jnp.mean(grown * xhat, axis=-1, keepdims=True)
    return (grown - jnp.mean(grown, axis=-1, keepdims=True) - xhat * along) * inverse


def gelu_parts(h):
    square = h * h
    t = jnp.tanh(0.7978845608 * (h + 0.044715 * h * square))
    half = 0.5 * (1.0 + t)
    slope = 0.7978845608 * (1.0 + 3 * 0.044715 * square)
    return h * half, half + 0.5 * h * (1.0 - t * t) * slope


def add_into(held, index, others):
    total = held[index].astype(F32)
    for other in others:
        total = total + other.astype(F32)
    held[index] = total.astype(held.dtype)


class Scatter:
    def __init__(self, wires, place, grads, held, hop1, hop2, hopz):
        self.w, self.p, self.grads, self.held = wires, place, grads, held
        self.hop1, self.hop2, self.hopz = hop1, hop2, hopz
        self.group = held.shape[1]
        self.crossed, self.first, self.second, self.third = {}, {}, {}, []
        n = place.side
        self.line = [*range(1, n), 0]
        self.order = [(d, e) for d in self.line for e in self.line]

    def at(self, turn, d, e):
        p, n = self.p, self.p.side
        y = lax.rem(p.y + turn * d + (1 - turn) * e, n)
        x = lax.rem(p.x + turn * e + (1 - turn) * d, n)
        return y * n + x

    def rows_of(self, j, core):
        return pl.ds(pl.multiple_of((2 * j + core) * self.group, self.group), self.group)

    def cross(self, d, e):
        p = self.p
        j = self.at(1 - p.c, d, e)
        self.crossed[d, e] = self.w.copy(self.grads.at[self.rows_of(j, 1 - p.c)], self.held.at[j], p.sibling())

    def fold(self, d, e):
        p = self.p
        j = self.at(p.c, d, e)
        self.crossed[d, e].wait_recv()
        add_into(self.held, j, [self.grads[self.rows_of(j, p.c)]])
        if d:
            self.first[d, e] = self.w.copy(self.held.at[j], self.hop1.at[d - 1, e], p.peers(0)[d - 1])

    def turn(self, e):
        p, n = self.p, self.p.side
        j = self.at(p.c, 0, e)
        for d in range(1, n):
            self.first[d, e].wait_recv()
        add_into(self.held, j, [self.hop1[d - 1, e] for d in range(1, n)])
        if e:
            self.second[e] = self.w.copy(self.held.at[j], self.hop2.at[e - 1], p.peers(1)[e - 1])

    def step0(self):
        for d, e in self.order:
            self.cross(d, e)

    def step1(self):
        for d, e in self.order:
            self.fold(d, e)

    def step2(self):
        for e in self.line:
            self.turn(e)

    def step3(self):
        p = self.p
        for move in self.second.values():
            move.wait_recv()
        self.mine = self.at(p.c, 0, 0)
        add_into(self.held, self.mine, [self.hop2[e - 1] for e in range(1, p.side)])
        if self.hopz is not None:
            self.unit = self.group // p.deep
            for d, other in enumerate(p.peers("z"), 1):
                self.third.append(self.w.copy(self.held.at[self.mine, self.unit_rows(d)], self.hopz.at[d - 1], other))

    def unit_rows(self, d):
        p = self.p
        return pl.ds(pl.multiple_of(lax.rem(p.z + d, p.deep) * self.unit, self.unit), self.unit)

    def step4(self):
        if self.hopz is None:
            return self.held[self.mine].astype(F32)
        total = self.held[self.mine, self.unit_rows(0)].astype(F32)
        for d, move in enumerate(self.third):
            move.wait_recv()
            total = total + self.hopz[d].astype(F32)
        return total


def scatter_scratch(side, deep, unit, tail, with_z):
    group = deep * unit
    shapes = [(side * side, group), (side - 1, side, group), (side - 1, group)]
    if with_z:
        shapes.append((deep - 1, unit))
    return [pltpu.VMEM((*shape, *tail), BF16) for shape in shapes]


class Total:
    def __init__(self, wires, place, sums, came):
        self.w, self.p, self.sums, self.came = wires, place, sums, came
        self.slot = 0

    def send(self, level):
        p = self.p
        peers = [[p.sibling()], p.peers(0), p.peers(1), p.peers("z")][level]
        self.moves = []
        for peer in peers:
            self.moves.append(self.w.copy(self.sums.at[level], self.came.at[self.slot], peer))
            self.slot += 1

    def take(self, level):
        total = self.sums[level]
        for i, move in enumerate(self.moves):
            move.wait_recv()
            total = total + self.came[self.slot - len(self.moves) + i]
        self.sums[level + 1] = total


def layer_kernel(
    with_z, grad_scale,
    x_hbm, cot_hbm, wqkv_ref, wo_ref, wu_ref, wd_ref, gain1_ref, shift1_ref, gain2_ref, shift2_ref, span_doc_ref,
    out_hbm, dtok_hbm, dwqkv_ref, dwo_hbm, dwu_hbm, dwd_hbm, total_ref,
    x_ref, cot_ref, dtok_ref, dwo_ref, dwu_ref, dwd_ref, small_ref, docs_ref, own_q, own_k, own_v,
    q_mat, k_mat, v_mat, out_mat, up_mat, down_mat, gains_ref, small_all, own_sums, sums_all, sums_ref, sums_t_ref,
    act_ref, qkv_ref, probs_ref, attn_t_ref, resid_ref, act2_ref, acted_ref, dhid_ref, dattn_ref,
    gdown_ref, gup_ref, gout_ref, gq_ref, gk_ref, gv_ref, dkv_ref, delta_ref, dsum_ref, levels_ref, came_ref,
    send, recv, place_sem, *held,
):
    place = Place()
    wires = Wires(send, recv)
    tok = x_ref.shape[0]
    spans = tok // S
    tiles = tok // TILE
    first = place.me * spans
    held = list(held)
    local = [pltpu.make_async_copy(x_hbm, x_ref, place_sem.at[0]), pltpu.make_async_copy(cot_hbm, cot_ref, place_sem.at[1])]
    for move in local:
        move.start()

    def gather(shard, full):
        return Gather(wires, place, shard, full, shard.shape[0], with_z)

    def scatter(grads, z):
        parts = [held.pop(0) for _ in range(4 if z else 3)]
        return Scatter(wires, place, grads, *parts, *([] if z else [None]))

    small = Gather(wires, place, small_ref, small_all, 1, True)
    sums = Gather(wires, place, own_sums, sums_all, 1, True)
    g_k, g_v, g_q, g_out = gather(own_k, k_mat), gather(own_v, v_mat), gather(own_q, q_mat), gather(wo_ref, out_mat)
    g_down, g_up = gather(wd_ref, down_mat), gather(wu_ref, up_mat)
    s_sum = scatter(sums_all, True)
    s_down, s_up, s_out, s_q, s_k, s_v = [
        scatter(g, with_z) for g in (gdown_ref, gup_ref, gout_ref, gq_ref, gk_ref, gv_ref)
    ]

    width = gain1_ref.shape[1]
    small_ref[...] = jnp.zeros_like(small_ref)
    for k, ref in enumerate((gain1_ref, shift1_ref, gain2_ref, shift2_ref)):
        small_ref[0, k : k + 1, :width] = ref[...].astype(F32)
    split_heads(wqkv_ref[...], (own_q, own_k, own_v))
    place.greet()
    for g in (small, g_k, g_v, g_q, g_down, g_out, g_up):
        g.step0()
    small.step1()
    g_k.step1()
    g_v.step1()
    small.step2()
    g_k.step2()
    g_q.step1()
    g_v.step2()
    small.step3()
    g_k.step3()
    g_q.step2()
    docs_ref[...] = window_docs(first, spans, span_doc_ref)
    small.step4()
    gains_ref[...] = spread_small(small_all[...], place.devices)
    local[0].wait()

    def norm(i):
        rows = tile_rows(i, S)
        xhat, _ = normed_parts(x_ref[rows, :].astype(F32))
        act_ref[rows, :] = (xhat * gains_ref[0:1, :] + gains_ref[1:2, :]).astype(BF16)

    loop(0, spans, norm)
    g_v.step3()
    g_k.step4()
    g_down.step1()
    g_out.step1()

    def project(mat, part):
        block = nn(act_ref[...], mat[...]).astype(BF16)
        qkv_ref[:, part * D : (part + 1) * D] = block
        if part:
            mean = jnp.sum(block.astype(F32).reshape(spans, S, D), axis=1) * (1.0 / S)
            own_sums[0, :, (part - 1) * D : part * D] = mean.astype(BF16)

    project(k_mat, 1)
    g_q.step3()
    g_v.step4()
    project(v_mat, 2)
    sums.step0()
    g_q.step4()
    project(q_mat, 0)
    sums.step1()
    half = spans // 2
    loop(0, half, lambda i: span_scores(i, qkv_ref, dkv_ref))
    sums.step2()
    g_out.step2()
    g_down.step2()
    loop(half, spans, lambda i: span_scores(i, qkv_ref, dkv_ref))
    sums.step3()
    g_up.step1()
    sums.step4()
    for i in range(PSPANS // MOST):
        two = sums_all[pl.ds(2 * i, 2)].astype(F32)
        sums_ref[MOST * i : MOST * (i + 1), :] = two.reshape(MOST, 2 * D).astype(BF16)
    before = sums_all[pl.ds(lax.rem(place.me + place.devices - 2, place.devices), 1)].astype(F32)
    last = sums_all[pl.ds(lax.rem(place.me + place.devices - 1, place.devices), 1)].astype(F32)
    here = sums_all[pl.ds(place.me, 1)].astype(F32)
    nothing = jnp.zeros_like(here)
    sums_ref[PSPANS : PSPANS + MOST, :] = jnp.concatenate([before, last], axis=0).reshape(MOST, 2 * D).astype(BF16)
    sums_ref[PSPANS + MOST :, :] = jnp.concatenate([here, nothing], axis=0).reshape(MOST, 2 * D).astype(BF16)
    sums_t_ref[...] = sums_ref[...].T

    def attend(span):
        attend_span(span, first, qkv_ref, sums_ref, sums_t_ref, docs_ref, dkv_ref, attn_t_ref, probs_ref)

    quarter = spans // 4
    loop(0, quarter, attend)
    g_out.step3()
    loop(quarter, 2 * quarter, attend)
    g_up.step2()
    g_down.step3()
    loop(2 * quarter, spans, attend)
    g_out.step4()

    def residual(i):
        rows = tile_rows(i, TILE)
        resid = x_ref[rows, :].astype(F32) + tn(attn_t_ref[:, rows], out_mat[...])
        resid_ref[rows, :] = resid
        xhat, _ = normed_parts(resid)
        act2_ref[rows, :] = (xhat * gains_ref[2:3, :] + gains_ref[3:4, :]).astype(BF16)

    loop(0, tiles, residual)
    local[1].wait()
    g_up.step3()
    g_down.step4()
    g_up.step4()

    def feed(i):
        part = tile_rows(i, CHUNK)
        acted, slope = gelu_parts(nt(act2_ref[...], up_mat[part, :]))
        acted = acted.astype(BF16)
        acted_ref[:, part] = acted
        dhid = (nt(cot_ref[...], down_mat[part, :]) * slope).astype(BF16)
        dhid_ref[:, part] = dhid
        gdown_ref[part, :] = tn(acted, cot_ref[...]).astype(BF16)
        gup_ref[part, :] = tn(dhid, act2_ref[...]).astype(BF16)

    both = (s_down, s_up)
    waiting = []
    if s_up.group == CHUNK:
        for d, e in s_up.order:
            theirs = 2 * s_up.at(1 - place.c, d, e) + 1 - place.c
            ours = 2 * s_up.at(place.c, d, e) + place.c
            loop(0, 2, lambda i: feed(theirs + i * (ours - theirs)))
            for s in both:
                s.cross(d, e)
            waiting.append((d, e))
            if len(waiting) > 1:
                fold_all(both, *waiting.pop(0))
    else:
        loop(0, up_mat.shape[0] // CHUNK, feed)
        for s in both:
            s.step0()
        waiting = list(s_up.order)
    levels_ref[...] = jnp.zeros_like(levels_ref)

    def finish(i):
        rows = tile_rows(i, TILE)
        dnormed = nn(dhid_ref[rows, :], up_mat[...])
        xhat, inverse = normed_parts(resid_ref[rows, :])
        levels_ref[0, 2:3, :] += jnp.sum(dnormed * xhat, axis=0, keepdims=True)
        levels_ref[0, 3:4, :] += jnp.sum(dnormed, axis=0, keepdims=True)
        dresid = cot_ref[rows, :].astype(F32) + norm_back(dnormed, xhat, inverse, gains_ref[2:3, :])
        dtok_ref[rows, :] = dresid
        branch = dresid.astype(BF16)
        act2_ref[rows, :] = branch
        dattn_ref[rows, :] = nt(branch, out_mat[...]).astype(BF16)

    loop(0, tiles // 2, finish)
    for d, e in waiting:
        fold_all(both, d, e)
    for e in s_up.line[:-1]:
        for s in both:
            s.turn(e)
    loop(tiles // 2, tiles, finish)
    gout_ref[...] = nn(attn_t_ref[...], act2_ref[...]).astype(BF16)
    s_out.step0()
    dsum_ref[...] = jnp.zeros_like(dsum_ref)

    def back_far(span):
        summary_back(span, qkv_ref, sums_ref, probs_ref, attn_t_ref, dattn_ref, delta_ref, dsum_ref)

    def back_near(span):
        span_back(span, qkv_ref, sums_t_ref, probs_ref, dattn_ref, delta_ref, dhid_ref, dkv_ref)

    loop(0, quarter, back_far)
    s_out.step1()
    loop(quarter, 2 * quarter, back_far)
    for s in both:
        s.turn(0)
    loop(2 * quarter, 3 * quarter, back_far)
    s_out.step2()
    loop(3 * quarter, spans, back_far)
    wires.settle(sums.sent)
    sums_all[...] = jnp.zeros_like(sums_all)
    for i in range(3):
        block = lax.rem(place.me + place.devices - 2 + i, place.devices)
        rows = slice(PSPANS + i * spans, PSPANS + (i + 1) * spans)
        sums_all[pl.ds(block, 1)] = dsum_ref[rows, :].astype(BF16)[None]
    for i in range(PSPANS // spans):
        sums_all[i] = dsum_ref[i * spans : (i + 1) * spans, :].astype(BF16)
    s_sum.step0()
    loop(0, quarter, back_near)
    s_sum.step1()
    loop(quarter, 2 * quarter, back_near)
    s_sum.step2()
    loop(2 * quarter, 3 * quarter, back_near)
    s_sum.step3()
    for s in both:
        s.step3()
    s_out.step3()
    loop(3 * quarter, spans, back_near)
    gq_ref[...] = tn(act_ref[...], dhid_ref[:, :D]).astype(BF16)
    s_q.step0()
    shares = s_sum.step4()[0] * (1.0 / S)
    for part, g_ref, s in ((0, gk_ref, s_k), (1, gv_ref, s_v)):
        cols = slice(part * D, (part + 1) * D)
        for span in range(spans):
            rows = slice(span * S, (span + 1) * S)
            dhid_ref[rows, (part + 1) * D : (part + 2) * D] = (dkv_ref[rows, cols] + shares[span : span + 1, cols]).astype(BF16)
        g_ref[...] = tn(act_ref[...], dhid_ref[:, (part + 1) * D : (part + 2) * D]).astype(BF16)
        s.step0()

    def write(ref, hbm, i, rows=slice(None)):
        move = pltpu.make_async_copy(ref.at[rows], hbm.at[rows], place_sem.at[i])
        move.start()
        local.append(move)

    def finish_tokens(i):
        rows = slice(i * TILE, (i + 1) * TILE)
        dnormed = nt(dhid_ref[rows, :D], q_mat[...]) + nt(dhid_ref[rows, D : 2 * D], k_mat[...])
        dnormed = dnormed + nt(dhid_ref[rows, 2 * D : 3 * D], v_mat[...])
        xhat, inverse = normed_parts(x_ref[rows, :].astype(F32))
        levels_ref[0, 0:1, :] += jnp.sum(dnormed * xhat, axis=0, keepdims=True)
        levels_ref[0, 1:2, :] += jnp.sum(dnormed, axis=0, keepdims=True)
        dtok_ref[rows, :] += norm_back(dnormed, xhat, inverse, gains_ref[0:1, :])

    def output(i):
        rows = slice(i * TILE, (i + 1) * TILE)
        act2_ref[rows, :] = (resid_ref[rows, :] + nn(acted_ref[rows, :], down_mat[...])).astype(BF16)

    total = Total(wires, place, levels_ref, came_ref)
    finish_tokens(0)
    s_q.step1()
    s_k.step1()
    finish_tokens(1)
    s_v.step1()
    finish_tokens(2)
    s_q.step2()
    finish_tokens(3)
    total.send(0)
    s_k.step2()
    write(dtok_ref, dtok_hbm, 2)
    output(0)
    total.take(0)
    total.send(1)
    s_v.step2()
    output(1)
    s_q.step3()
    s_k.step3()
    output(2)
    total.take(1)
    total.send(2)
    s_v.step3()
    output(3)
    write(act2_ref, out_hbm, 3)
    dwd_ref[...] = s_down.step4() * grad_scale
    dwu_ref[...] = s_up.step4() * grad_scale
    dwo_ref[...] = s_out.step4() * grad_scale
    write(dwd_ref, dwd_hbm, 4)
    write(dwu_ref, dwu_hbm, 5)
    write(dwo_ref, dwo_hbm, 6)
    total.take(2)
    total.send(3)
    join_heads((s_q.step4() * grad_scale, s_k.step4() * grad_scale, s_v.step4() * grad_scale), dwqkv_ref)
    total.take(3)
    start = place.me * width
    lanes = pl.ds(pl.multiple_of(start // LANES * LANES, LANES), LANES)
    total_ref[...] = pltpu.roll(levels_ref[4, :, lanes] * grad_scale, lax.rem(LANES - lax.rem(start, LANES), LANES), 1)
    for move in local[2:]:
        move.wait()
    wires.finish()


def fold_all(scatters, d, e):
    for s in scatters:
        s.fold(d, e)


def layer(with_z, grad_scale, x, cotangent, wqkv, wo, wu, wd, vectors, span_doc):
    tok = x.shape[0]
    spans = tok // S
    deep = lax.axis_size("head")
    side = math.isqrt(lax.axis_size("seq") // 2)
    devices = 2 * side * side * deep
    owned = devices if with_z else devices // deep
    hidden_size = wu.shape[0] * owned
    whole, anywhere = pl.BlockSpec(memory_space=VMEM), pl.BlockSpec(memory_space=pl.ANY)
    shape = jax.ShapeDtypeStruct
    peers = 1 + 2 * (side - 1) + deep - 1
    n = 8 * copies_of_gather(side, deep, True) + 8
    n += 7 * (side * side + (side - 1) * side + side - 1 + deep - 1) + peers
    held = scatter_scratch(side, deep, 1, (spans, 2 * D), True)
    for total in (hidden_size, hidden_size, D, D, D, D):
        held += scatter_scratch(side, deep, total // devices, (D,), with_z)
    return pl.pallas_call(
        functools.partial(layer_kernel, with_z, grad_scale),
        out_shape=(
            shape((tok, D), BF16),
            shape((tok, D), F32),
            shape((D // owned, 3 * D), F32),
            shape((D // owned, D), F32),
            shape((hidden_size // owned, D), F32),
            shape((hidden_size // owned, D), F32),
            shape((8, LANES), F32),
        ),
        in_specs=[anywhere] * 2 + [whole] * 8 + [pl.BlockSpec(memory_space=pltpu.MemorySpace.SMEM)],
        out_specs=(anywhere, anywhere, whole, anywhere, anywhere, anywhere, whole),
        scratch_shapes=[
            pltpu.VMEM((tok, D), BF16),
            pltpu.VMEM((tok, D), BF16),
            pltpu.VMEM((tok, D), F32),
            pltpu.VMEM((D // owned, D), F32),
            pltpu.VMEM((hidden_size // owned, D), F32),
            pltpu.VMEM((hidden_size // owned, D), F32),
            pltpu.VMEM((1, 8, LANES), F32),
            pltpu.VMEM((WIN, S), jnp.int32),
            pltpu.VMEM((D // owned, D), BF16),
            pltpu.VMEM((D // owned, D), BF16),
            pltpu.VMEM((D // owned, D), BF16),
            pltpu.VMEM((D, D), BF16),
            pltpu.VMEM((D, D), BF16),
            pltpu.VMEM((D, D), BF16),
            pltpu.VMEM((D, D), BF16),
            pltpu.VMEM((hidden_size, D), BF16),
            pltpu.VMEM((hidden_size, D), BF16),
            pltpu.VMEM((8, D), F32),
            pltpu.VMEM((devices, 8, LANES), F32),
            pltpu.VMEM((1, spans, 2 * D), BF16),
            pltpu.VMEM((devices, spans, 2 * D), BF16),
            pltpu.VMEM((FAR, 2 * D), BF16),
            pltpu.VMEM((2 * D, FAR), BF16),
            pltpu.VMEM((tok, D), BF16),
            pltpu.VMEM((tok, 3 * D), BF16),
            pltpu.VMEM((spans * PAIRS, KEYS, 2 * S), BF16),
            pltpu.VMEM((D, tok), BF16),
            pltpu.VMEM((tok, D), F32),
            pltpu.VMEM((tok, D), BF16),
            pltpu.VMEM((tok, hidden_size), BF16),
            pltpu.VMEM((tok, hidden_size), BF16),
            pltpu.VMEM((tok, D), BF16),
            pltpu.VMEM((hidden_size, D), BF16),
            pltpu.VMEM((hidden_size, D), BF16),
            pltpu.VMEM((D, D), BF16),
            pltpu.VMEM((D, D), BF16),
            pltpu.VMEM((D, D), BF16),
            pltpu.VMEM((D, D), BF16),
            pltpu.VMEM((tok, 2 * D), F32),
            pltpu.VMEM((spans * PAIRS, 2 * S), F32),
            pltpu.VMEM((FAR, 2 * D), F32),
            pltpu.VMEM((5, 8, D), F32),
            pltpu.VMEM((peers, 8, D), F32),
            pltpu.SemaphoreType.DMA((n,)),
            pltpu.SemaphoreType.DMA((n,)),
            pltpu.SemaphoreType.DMA((7,)),
            *held,
        ],
        compiler_params=pltpu.CompilerParams(vmem_limit_bytes=VMEM_LIMIT, collective_id=0, has_side_effects=True),
        name="mega_layer",
    )(x, cotangent, wqkv, wo, wu, wd, *vectors, span_doc)


def shards(tokens, cotangent, w_qkv, w_out, w_up, w_down, gain_one, shift_one, gain_two, shift_two, span_doc):
    tok = tokens.shape[0]
    devices = lax.axis_size("seq") * lax.axis_size("head")
    grad_scale = 1.0 / math.sqrt(tok * devices)
    with_z = w_qkv.shape[0] % 16 == 0
    weights = (w_qkv, w_out, w_up.T, w_down)
    if not with_z:
        weights = tuple(lax.all_gather(w, "head", axis=0, tiled=True) for w in weights)
    vectors = [v[None] for v in (gain_one, shift_one, gain_two, shift_two)]
    width = gain_one.shape[0]
    out_tokens, d_tokens, d_qkv, d_out, d_up, d_down, total = layer(
        with_z, grad_scale, tokens, cotangent, *weights, vectors, span_doc
    )
    if not with_z:
        d_qkv, d_out, d_up, d_down = (
            lax.psum_scatter(g, "head", scatter_dimension=0, tiled=True) for g in (d_qkv, d_out, d_up, d_down)
        )
    return out_tokens, d_tokens, d_qkv, d_out, d_up.T, d_down, *(total[k, :width] for k in range(4))


def solution(mesh):
    rows, cols, vec = P(BOTH, None), P(None, BOTH), P(BOTH)
    in_specs = (rows, rows, rows, rows, cols, rows, vec, vec, vec, vec, P())
    out_specs = (rows, rows, rows, rows, cols, rows, vec, vec, vec, vec)
    return jax.shard_map(shards, mesh=mesh, in_specs=in_specs, out_specs=out_specs, check_vma=False)
```

```python
import functools
import math

import jax
import jax.numpy as jnp
from jax import lax
from jax.experimental import pallas as pl
from jax.experimental.pallas import tpu as pltpu
from jax.sharding import PartitionSpec as P

H = 8
HD = 64
D = H * HD
S = 128
MOST = 16
PSPANS = 128
WIN = 2 * MOST
PAIRS = H // 2
LANES = 2 * HD
FAR = PSPANS + WIN
KEYS = S + FAR
EPS = 1e-05
MASKED = -1e30
F32 = jnp.float32
BF16 = jnp.bfloat16
VMEM = pltpu.MemorySpace.VMEM
VMEM_LIMIT = 67043328
TILE = 256
CHUNK = 256


def nn(a, b):
    return lax.dot_general(a, b, (((1,), (0,)), ((), ())), preferred_element_type=F32)


def nt(a, b):
    return lax.dot_general(a, b, (((1,), (1,)), ((), ())), preferred_element_type=F32)


def tn(a, b):
    return lax.dot_general(a, b, (((0,), (0,)), ((), ())), preferred_element_type=F32)


def loop(start, stop, body):
    def step(i, carry):
        body(i)
        return carry

    lax.fori_loop(start, stop, step, 0)


def tile_rows(i, size):
    return pl.ds(pl.multiple_of(i * size, size), size)


def summary_bias(first, span, docs_ref):
    index = first + span
    row = lax.broadcasted_iota(jnp.int32, (PSPANS, S), 0)
    prompt = jnp.where(row < index, 0.0, MASKED)
    wrow = first - MOST + lax.broadcasted_iota(jnp.int32, (WIN, S), 0)
    same = docs_ref[...] == docs_ref[pl.ds(span + MOST, 1), :]
    window = jnp.where(same & (wrow >= PSPANS) & (wrow < index), 0.0, MASKED)
    return jnp.concatenate([prompt, window], axis=0).astype(F32)


def window_docs(first, spans, span_doc_ref):
    row = lax.broadcasted_iota(jnp.int32, (WIN, S), 0)
    docs = jnp.full((WIN, S), -1, jnp.int32)
    for i in range(MOST + spans):
        at = first - MOST - PSPANS + i
        docs = jnp.where((row == i) & (at >= 0), span_doc_ref[jnp.maximum(at, 0)], docs)
    return docs


def head_masks(scale):
    lane = lax.broadcasted_iota(jnp.int32, (1, LANES), 1)
    first = jnp.where(lane < HD, scale, 0.0).astype(BF16)
    second = jnp.where(lane < HD, 0.0, scale).astype(BF16)
    return first, second


def stack_heads(block, masks):
    return jnp.concatenate([block * masks[0], block * masks[1]], axis=0)


def pair_cols(part, pair):
    return slice(part * D + pair * LANES, part * D + (pair + 1) * LANES)


def unstack(pair_t):
    return jnp.concatenate([pair_t[:HD, :S], pair_t[HD:, S:]], axis=0)


def both_heads(pair):
    return slice(pair * 2 * S, (pair + 1) * 2 * S)


def span_scores(span, qkv_ref, scores_ref):
    rows = tile_rows(span, S)
    key_row = lax.broadcasted_iota(jnp.int32, (S, S), 0)
    query = lax.broadcasted_iota(jnp.int32, (S, S), 1)
    causal = jnp.where(key_row <= query, 0.0, MASKED).astype(F32)
    causal = jnp.concatenate([causal, causal], axis=1)
    masks = head_masks(1.0 / math.sqrt(HD))
    for pair in range(PAIRS):
        queries = stack_heads(qkv_ref[rows, pair_cols(0, pair)], masks)
        scores_ref[rows, both_heads(pair)] = nt(qkv_ref[rows, pair_cols(1, pair)], queries) + causal


def attend_span(span, first, qkv_ref, sums_ref, sums_t_ref, docs_ref, scores_ref, attn_t_ref, probs_ref):
    rows = tile_rows(span, S)
    bias = summary_bias(first, span, docs_ref)
    bias = jnp.concatenate([bias, bias], axis=1)
    masks = head_masks(1.0 / math.sqrt(HD))
    for pair in range(PAIRS):
        queries = stack_heads(qkv_ref[rows, pair_cols(0, pair)], masks)
        own = scores_ref[rows, both_heads(pair)]
        far = nt(sums_ref[:, pair_cols(0, pair)], queries) + bias
        top = jnp.maximum(jnp.max(own, axis=0, keepdims=True), jnp.max(far, axis=0, keepdims=True))
        own, far = jnp.exp(own - top), jnp.exp(far - top)
        share = 1.0 / (jnp.sum(own, axis=0, keepdims=True) + jnp.sum(far, axis=0, keepdims=True))
        probs = jnp.concatenate([(own * share).astype(BF16), (far * share).astype(BF16)], axis=0)
        probs_ref[span * PAIRS + pair] = probs
        vals_t = jnp.concatenate([qkv_ref[rows, pair_cols(2, pair)].T, sums_t_ref[pair_cols(1, pair), :]], axis=1)
        attn_t_ref[pair * LANES : (pair + 1) * LANES, rows] = unstack(nn(vals_t, probs)).astype(BF16)


def summary_back(span, qkv_ref, sums_ref, probs_ref, attn_t_ref, dattn_ref, delta_ref, dsum_ref):
    rows = tile_rows(span, S)
    masks = head_masks(1.0 / math.sqrt(HD))
    ones = head_masks(1.0)
    for pair in range(PAIRS):
        cols, vcols = pair_cols(0, pair), pair_cols(1, pair)
        block = dattn_ref[rows, cols]
        each = block.T.astype(F32) * attn_t_ref[pair * LANES : (pair + 1) * LANES, rows].astype(F32)
        delta = jnp.concatenate(
            [jnp.sum(each[:HD], axis=0, keepdims=True), jnp.sum(each[HD:], axis=0, keepdims=True)], axis=1
        )
        delta_ref[pl.ds(span * PAIRS + pair, 1), :] = delta
        queries = stack_heads(qkv_ref[rows, cols], masks)
        grads = stack_heads(block, ones)
        probs = probs_ref[span * PAIRS + pair, S:, :]
        dprobs = nt(sums_ref[:, vcols], grads)
        dscores = (probs.astype(F32) * (dprobs - delta)).astype(BF16)
        dsum_ref[:, cols] += nn(dscores, queries)
        dsum_ref[:, vcols] += nn(probs, grads)
        probs_ref[span * PAIRS + pair, S:, :] = dscores


def span_back(span, qkv_ref, sums_t_ref, probs_ref, dattn_ref, delta_ref, dqkv_ref, dkv_ref):
    rows = tile_rows(span, S)
    scale = 1.0 / math.sqrt(HD)
    masks = head_masks(scale)
    ones = head_masks(1.0)
    for pair in range(PAIRS):
        cols, vcols = pair_cols(0, pair), pair_cols(1, pair)
        queries = stack_heads(qkv_ref[rows, cols], masks)
        grads = stack_heads(dattn_ref[rows, cols], ones)
        probs = probs_ref[span * PAIRS + pair, :S, :]
        dprobs = nt(qkv_ref[rows, pair_cols(2, pair)], grads)
        delta = delta_ref[pl.ds(span * PAIRS + pair, 1), :]
        dscores = (probs.astype(F32) * (dprobs - delta)).astype(BF16)
        dkv_ref[rows, cols] = nn(dscores, queries)
        dkv_ref[rows, vcols] = nn(probs, grads)
        every = jnp.concatenate([dscores, probs_ref[span * PAIRS + pair, S:, :]], axis=0)
        keys_t = jnp.concatenate([qkv_ref[rows, pair_cols(1, pair)].T, sums_t_ref[cols, :]], axis=1)
        dq_t = unstack(nn(keys_t, every)) * scale
        dqkv_ref[rows, cols] = dq_t.T.astype(BF16)


def split_heads(block, parts):
    low = lax.broadcasted_iota(jnp.int32, (1, LANES), 1) < HD
    for pair in range(PAIRS):
        one, two, three = [block[:, (3 * pair + i) * LANES : (3 * pair + i + 1) * LANES].astype(F32) for i in range(3)]
        mixed = jnp.where(low, one, two), pltpu.roll(jnp.where(low, three, one), HD, 1), jnp.where(low, two, three)
        for part, value in zip(parts, mixed):
            part[:, pair * LANES : (pair + 1) * LANES] = value.astype(part.dtype)


def join_heads(parts, out_ref):
    low = lax.broadcasted_iota(jnp.int32, (1, LANES), 1) < HD
    for pair in range(PAIRS):
        q, k, v = [part[:, pair * LANES : (pair + 1) * LANES] for part in parts]
        k = pltpu.roll(k, HD, 1)
        for i, value in enumerate((jnp.where(low, q, k), jnp.where(low, v, q), jnp.where(low, k, v))):
            out_ref[:, (3 * pair + i) * LANES : (3 * pair + i + 1) * LANES] = value


MESH = pl.DeviceIdType.MESH
BOTH = ("seq", "head")


class Place:
    def __init__(self):
        seq, self.z = lax.axis_index("seq"), lax.axis_index("head")
        self.side = math.isqrt(lax.axis_size("seq") // 2)
        self.deep = lax.axis_size("head")
        self.devices = lax.axis_size("seq") * self.deep
        self.c = lax.rem(seq, 2)
        self.x = lax.rem(seq // 2, self.side)
        self.y = seq // 2 // self.side
        self.me = seq * self.deep + self.z

    def seq(self, y, x, c):
        return (y * self.side + x) * 2 + c

    def along(self, axis, step):
        n, turn = self.side, self.c if axis == 0 else 1 - self.c
        return lax.rem(self.y + turn * step, n), lax.rem(self.x + (1 - turn) * step, n)

    def sibling(self):
        return (self.seq(self.y, self.x, 1 - self.c), self.z)

    def peers(self, axis):
        if axis == "z":
            seq = self.seq(self.y, self.x, self.c)
            return [(seq, lax.rem(self.z + d, self.deep)) for d in range(1, self.deep)]
        return [(self.seq(*self.along(axis, d), self.c), self.z) for d in range(1, self.side)]

    def spot(self, turn, d, e):
        n = self.side
        return lax.rem(self.y + turn * d + (1 - turn) * e, n), lax.rem(self.x + turn * e + (1 - turn) * d, n)

    def steps(self):
        line = [*range(1, self.side), 0]
        return [(d, e) for d in line for e in line][:-1]

    def plane(self):
        return [(self.seq(*self.spot(self.c, d, e), self.c), self.z) for d, e in self.steps()]

    def greet(self):
        barrier = pltpu.get_barrier_semaphore()
        others = [self.sibling(), *self.plane(), *self.peers("z")]
        for other in others:
            pl.semaphore_signal(barrier, inc=1, device_id=other, device_id_type=MESH)
        pl.semaphore_wait(barrier, len(others))


class Wires:
    def __init__(self, send, recv):
        self.send, self.recv, self.used, self.sent = send, recv, 0, []

    def copy(self, src, dst, device):
        i = self.used
        self.used += 1
        move = pltpu.make_async_remote_copy(
            src_ref=src, dst_ref=dst, send_sem=self.send.at[i], recv_sem=self.recv.at[i],
            device_id=device, device_id_type=MESH,
        )
        move.start()
        self.sent.append(move)
        return move

    def local(self, src, dst):
        i = self.used
        self.used += 1
        move = pltpu.make_async_copy(src, dst, self.send.at[i])
        move.start()
        return move

    def settle(self, moves):
        for move in moves:
            move.wait_send()
        done = {id(move) for move in moves}
        self.sent = [move for move in self.sent if id(move) not in done]

    def finish(self):
        self.settle(list(self.sent))


def copies_of_gather(side, deep, with_z):
    return 1 + (deep - 1 if with_z else 0) + (side - 1) + (side - 1) * side + side * side


class Gather:
    def __init__(self, wires, place, shard, full, rows, with_z, direct):
        self.w, self.p, self.full, self.shard = wires, place, full, shard
        self.rows, self.with_z, self.direct, self.sent = rows, with_z, direct, []
        self.group = rows * place.deep if with_z else rows

    def block(self, y, x):
        start = self.p.seq(y, x, self.p.c) * self.group
        return self.full.at[pl.ds(pl.multiple_of(start, self.group), self.group)]

    def step0(self):
        p = self.p
        start = pl.multiple_of(p.me * self.rows, self.rows) if self.with_z else p.seq(p.y, p.x, p.c) * self.rows
        own = self.full.at[pl.ds(start, self.rows)]
        self.moves = [self.w.copy(self.shard, own, d) for d in p.peers("z")] if self.with_z else []
        self.sent += self.moves
        self.placed = self.w.local(self.shard, own)

    def _line(self, step):
        p, n = self.p, self.p.side
        y1, x1 = p.along(1, step)
        turn = 1 - p.c
        mine = [p.along(0, d) for d in range(n)]
        return [(turn * y1 + (1 - turn) * y, turn * x + (1 - turn) * x1) for y, x in mine]

    def _send(self, place, device):
        move = self.w.copy(self.block(*place), self.block(*place), device)
        self.sent.append(move)
        return move

    def step1(self):
        p = self.p
        for move in self.moves:
            move.wait_recv()
        self.placed.wait()
        own = (p.y, p.x)
        self.moves = [] if self.direct else [self._send(own, d) for d in p.peers(0)]
        self.turned = [self._send(own, d) for d in (p.plane() if self.direct else p.peers(1))]
        self.across = [self._send(own, p.sibling())]

    def step2(self):
        p = self.p
        if self.direct:
            return
        for move in self.moves:
            move.wait_recv()
        line = self._line(0)[1:]
        self.turned += [self._send(place, d) for d in p.peers(1) for place in line]
        self.across += [self._send(place, p.sibling()) for place in line]

    def step3(self):
        for move in self.turned:
            move.wait_recv()
        p = self.p
        came = [place for e in range(1, p.side) for place in self._line(e)]
        if self.direct:
            came += self._line(0)[1:]
        self.across += [self._send(place, p.sibling()) for place in came]

    def step4(self):
        for move in self.across:
            move.wait_recv()


def spread_small(gathered, devices):
    width = D // devices
    table = gathered.reshape(devices * 8, LANES).astype(BF16)
    pick = lax.broadcasted_iota(jnp.int32, (LANES, D), 0) == lax.broadcasted_iota(jnp.int32, (LANES, D), 1) % width
    every = nn(table, jnp.where(pick, 1.0, 0.0).astype(BF16))
    owner = lax.broadcasted_iota(jnp.int32, (devices * 8, D), 0) // 8
    column = lax.broadcasted_iota(jnp.int32, (devices * 8, D), 1) // width
    return jnp.sum(jnp.where(owner == column, every, 0.0).reshape(devices, 8, D), axis=0)


def normed_parts(values):
    mean = jnp.mean(values, axis=-1, keepdims=True)
    centred = values - mean
    inverse = lax.rsqrt(jnp.mean(centred * centred, axis=-1, keepdims=True) + EPS)
    return centred * inverse, inverse


def norm_back(dnormed, xhat, inverse, gain):
    grown = dnormed * gain
    along = jnp.mean(grown * xhat, axis=-1, keepdims=True)
    return (grown - jnp.mean(grown, axis=-1, keepdims=True) - xhat * along) * inverse


def gelu_parts(h):
    square = h * h
    t = jnp.tanh(0.7978845608 * (h + 0.044715 * h * square))
    half = 0.5 * (1.0 + t)
    slope = 0.7978845608 * (1.0 + 3 * 0.044715 * square)
    return h * half, half + 0.5 * h * (1.0 - t * t) * slope


def add_into(held, index, others):
    total = held[index].astype(F32)
    for other in others:
        total = total + other.astype(F32)
    held[index] = total.astype(held.dtype)


class Scatter:
    def __init__(self, wires, place, grads, direct, held, hop1, hop2, hopz):
        self.w, self.p, self.grads, self.held = wires, place, grads, held
        self.direct, self.hop1, self.hop2, self.hopz = direct, hop1, hop2, hopz
        self.group = held.shape[1]
        self.crossed, self.first, self.second, self.third = {}, {}, {}, []
        n = place.side
        self.line = [*range(1, n), 0]
        self.order = [(d, e) for d in self.line for e in self.line]

    def at(self, turn, d, e):
        y, x = self.p.spot(turn, d, e)
        return y * self.p.side + x

    def hop(self, d, e):
        return self.hop1.at[d - 1, e] if d else self.hop2.at[e - 1]

    def rows_of(self, j, core):
        return pl.ds(pl.multiple_of((2 * j + core) * self.group, self.group), self.group)

    def cross(self, d, e):
        p = self.p
        j = self.at(1 - p.c, d, e)
        self.crossed[d, e] = self.w.copy(self.grads.at[self.rows_of(j, 1 - p.c)], self.held.at[j], p.sibling())

    def fold(self, d, e):
        p = self.p
        j = self.at(p.c, d, e)
        self.crossed[d, e].wait_recv()
        add_into(self.held, j, [self.grads[self.rows_of(j, p.c)]])
        if self.direct and (d or e):
            owner = p.seq(*p.spot(p.c, d, e), p.c), p.z
            self.first[d, e] = self.w.copy(self.held.at[j], self.hop(d, e), owner)
        elif d:
            self.first[d, e] = self.w.copy(self.held.at[j], self.hop1.at[d - 1, e], p.peers(0)[d - 1])

    def turn(self, e):
        p, n = self.p, self.p.side
        j = self.at(p.c, 0, e)
        for d in range(1, n):
            self.first[d, e].wait_recv()
        add_into(self.held, j, [self.hop1[d - 1, e] for d in range(1, n)])
        if e:
            self.second[e] = self.w.copy(self.held.at[j], self.hop2.at[e - 1], p.peers(1)[e - 1])

    def step0(self):
        for d, e in self.order:
            self.cross(d, e)

    def step1(self):
        for d, e in self.order:
            self.fold(d, e)

    def step2(self):
        for e in self.line if not self.direct else ():
            self.turn(e)

    def step3(self):
        p = self.p
        self.mine = self.at(p.c, 0, 0)
        if self.direct:
            for move in self.first.values():
                move.wait_recv()
            add_into(self.held, self.mine, [self.hop(d, e)[...] for d, e in p.steps()])
        else:
            for move in self.second.values():
                move.wait_recv()
            add_into(self.held, self.mine, [self.hop2[e - 1] for e in range(1, p.side)])
        if self.hopz is not None:
            self.unit = self.group // p.deep
            for d, other in enumerate(p.peers("z"), 1):
                self.third.append(self.w.copy(self.held.at[self.mine, self.unit_rows(d)], self.hopz.at[d - 1], other))

    def unit_rows(self, d):
        p = self.p
        return pl.ds(pl.multiple_of(lax.rem(p.z + d, p.deep) * self.unit, self.unit), self.unit)

    def step4(self):
        if self.hopz is None:
            return self.held[self.mine].astype(F32)
        total = self.held[self.mine, self.unit_rows(0)].astype(F32)
        for d, move in enumerate(self.third):
            move.wait_recv()
            total = total + self.hopz[d].astype(F32)
        return total


def scatter_scratch(side, deep, unit, tail, with_z):
    group = deep * unit
    shapes = [(side * side, group), (side - 1, side, group), (side - 1, group)]
    if with_z:
        shapes.append((deep - 1, unit))
    return [pltpu.VMEM((*shape, *tail), BF16) for shape in shapes]


class Total:
    def __init__(self, wires, place, sums, came):
        self.w, self.p, self.sums, self.came = wires, place, sums, came
        self.slot = 0

    def send(self, level):
        p = self.p
        peers = [[p.sibling()], p.plane(), p.peers("z")][level]
        self.moves = []
        for peer in peers:
            self.moves.append(self.w.copy(self.sums.at[level], self.came.at[self.slot], peer))
            self.slot += 1

    def take(self, level):
        total = self.sums[level]
        for i, move in enumerate(self.moves):
            move.wait_recv()
            total = total + self.came[self.slot - len(self.moves) + i]
        self.sums[level + 1] = total


def layer_kernel(
    with_z, grad_scale,
    x_hbm, cot_hbm, wqkv_ref, wo_ref, wu_ref, wd_ref, gain1_ref, shift1_ref, gain2_ref, shift2_ref, span_doc_ref,
    act2_ref, dtok_ref, dwqkv_ref, dwo_ref, dwu_ref, dwd_ref, total_ref,
    x_ref, cot_ref, small_ref, docs_ref, own_q, own_k, own_v,
    q_mat, k_mat, v_mat, out_mat, up_mat, down_mat, gains_ref, small_all, own_sums, sums_all, sums_ref, sums_t_ref,
    act_ref, qkv_ref, probs_ref, attn_t_ref, resid_ref, acted_ref, dhid_ref, dattn_ref,
    gdown_ref, gup_ref, gout_ref, gq_ref, gk_ref, gv_ref, dkv_ref, delta_ref, dsum_ref, levels_ref, came_ref,
    send, recv, place_sem, *held,
):
    place = Place()
    wires = Wires(send, recv)
    tok = x_ref.shape[0]
    spans = tok // S
    tiles = tok // TILE
    first = place.me * spans
    held = list(held)
    local = [pltpu.make_async_copy(x_hbm, x_ref, place_sem.at[0]), pltpu.make_async_copy(cot_hbm, cot_ref, place_sem.at[1])]
    for move in local:
        move.start()

    def gather(shard, full, direct):
        return Gather(wires, place, shard, full, shard.shape[0], with_z, direct)

    def scatter(grads, z, direct):
        parts = [held.pop(0) for _ in range(4 if z else 3)]
        return Scatter(wires, place, grads, direct, *parts, *([] if z else [None]))

    small = Gather(wires, place, small_ref, small_all, 1, True, True)
    sums = Gather(wires, place, own_sums, sums_all, 1, True, True)
    g_k, g_v, g_q = gather(own_k, k_mat, True), gather(own_v, v_mat, True), gather(own_q, q_mat, True)
    g_out, g_down, g_up = gather(wo_ref, out_mat, False), gather(wd_ref, down_mat, False), gather(wu_ref, up_mat, False)
    s_sum = scatter(sums_all, True, True)
    s_down, s_up, s_out = [scatter(g, with_z, False) for g in (gdown_ref, gup_ref, gout_ref)]
    s_q, s_k, s_v = [scatter(g, with_z, True) for g in (gq_ref, gk_ref, gv_ref)]

    width = gain1_ref.shape[1]
    small_ref[...] = jnp.zeros_like(small_ref)
    for k, ref in enumerate((gain1_ref, shift1_ref, gain2_ref, shift2_ref)):
        small_ref[0, k : k + 1, :width] = ref[...].astype(F32)
    split_heads(wqkv_ref[...], (own_q, own_k, own_v))
    place.greet()
    for g in (small, g_k, g_v, g_q, g_down, g_out, g_up):
        g.step0()
    small.step1()
    g_k.step1()
    g_v.step1()
    g_q.step1()
    small.step3()
    g_k.step3()
    docs_ref[...] = window_docs(first, spans, span_doc_ref)
    small.step4()
    gains_ref[...] = spread_small(small_all[...], place.devices)
    local[0].wait()

    def norm(i):
        rows = tile_rows(i, S)
        xhat, _ = normed_parts(x_ref[rows, :].astype(F32))
        act_ref[rows, :] = (xhat * gains_ref[0:1, :] + gains_ref[1:2, :]).astype(BF16)

    loop(0, spans, norm)
    g_v.step3()
    g_k.step4()

    def project(mat, part):
        block = nn(act_ref[...], mat[...]).astype(BF16)
        qkv_ref[:, part * D : (part + 1) * D] = block
        if part:
            mean = jnp.sum(block.astype(F32).reshape(spans, S, D), axis=1) * (1.0 / S)
            own_sums[0, :, (part - 1) * D : part * D] = mean.astype(BF16)

    project(k_mat, 1)
    g_q.step3()
    g_v.step4()
    project(v_mat, 2)
    sums.step0()
    g_down.step1()
    g_q.step4()
    project(q_mat, 0)
    half = spans // 2
    loop(0, half, lambda i: span_scores(i, qkv_ref, dkv_ref))
    sums.step1()
    g_out.step1()
    loop(half, spans, lambda i: span_scores(i, qkv_ref, dkv_ref))
    g_down.step2()
    g_up.step1()
    sums.step3()
    sums.step4()
    for i in range(PSPANS // MOST):
        two = sums_all[pl.ds(2 * i, 2)].astype(F32)
        sums_ref[MOST * i : MOST * (i + 1), :] = two.reshape(MOST, 2 * D).astype(BF16)
    before = sums_all[pl.ds(lax.rem(place.me + place.devices - 2, place.devices), 1)].astype(F32)
    last = sums_all[pl.ds(lax.rem(place.me + place.devices - 1, place.devices), 1)].astype(F32)
    here = sums_all[pl.ds(place.me, 1)].astype(F32)
    nothing = jnp.zeros_like(here)
    sums_ref[PSPANS : PSPANS + MOST, :] = jnp.concatenate([before, last], axis=0).reshape(MOST, 2 * D).astype(BF16)
    sums_ref[PSPANS + MOST :, :] = jnp.concatenate([here, nothing], axis=0).reshape(MOST, 2 * D).astype(BF16)
    sums_t_ref[...] = sums_ref[...].T

    def attend(span):
        attend_span(span, first, qkv_ref, sums_ref, sums_t_ref, docs_ref, dkv_ref, attn_t_ref, probs_ref)

    quarter = spans // 4
    loop(0, quarter, attend)
    g_out.step2()
    loop(quarter, 2 * quarter, attend)
    g_up.step2()
    g_down.step3()
    loop(2 * quarter, 3 * quarter, attend)
    g_out.step3()
    loop(3 * quarter, spans, attend)
    g_out.step4()

    def residual(i):
        rows = tile_rows(i, TILE)
        resid = x_ref[rows, :].astype(F32) + tn(attn_t_ref[:, rows], out_mat[...])
        resid_ref[rows, :] = resid
        xhat, _ = normed_parts(resid)
        act2_ref[rows, :] = (xhat * gains_ref[2:3, :] + gains_ref[3:4, :]).astype(BF16)

    loop(0, tiles, residual)
    local[1].wait()
    g_up.step3()
    g_down.step4()
    g_up.step4()

    def feed(i):
        part = tile_rows(i, CHUNK)
        acted, slope = gelu_parts(nt(act2_ref[...], up_mat[part, :]))
        acted = acted.astype(BF16)
        acted_ref[:, part] = acted
        dhid = (nt(cot_ref[...], down_mat[part, :]) * slope).astype(BF16)
        dhid_ref[:, part] = dhid
        gdown_ref[part, :] = tn(acted, cot_ref[...]).astype(BF16)
        gup_ref[part, :] = tn(dhid, act2_ref[...]).astype(BF16)

    both = (s_down, s_up)
    waiting = []
    if s_up.group == CHUNK:
        for d, e in s_up.order:
            theirs = 2 * s_up.at(1 - place.c, d, e) + 1 - place.c
            ours = 2 * s_up.at(place.c, d, e) + place.c
            loop(0, 2, lambda i: feed(theirs + i * (ours - theirs)))
            for s in both:
                s.cross(d, e)
            waiting.append((d, e))
            if len(waiting) > 1:
                fold_all(both, *waiting.pop(0))
    else:
        loop(0, up_mat.shape[0] // CHUNK, feed)
        for s in both:
            s.step0()
        waiting = list(s_up.order)
    levels_ref[...] = jnp.zeros_like(levels_ref)

    def finish(i):
        rows = tile_rows(i, TILE)
        dnormed = nn(dhid_ref[rows, :], up_mat[...])
        xhat, inverse = normed_parts(resid_ref[rows, :])
        levels_ref[0, 2:3, :] += jnp.sum(dnormed * xhat, axis=0, keepdims=True)
        levels_ref[0, 3:4, :] += jnp.sum(dnormed, axis=0, keepdims=True)
        dresid = cot_ref[rows, :].astype(F32) + norm_back(dnormed, xhat, inverse, gains_ref[2:3, :])
        dtok_ref[rows, :] = dresid
        branch = dresid.astype(BF16)
        act2_ref[rows, :] = branch
        dattn_ref[rows, :] = nt(branch, out_mat[...]).astype(BF16)

    loop(0, tiles // 2, finish)
    for d, e in waiting:
        fold_all(both, d, e)
    for e in s_up.line[:-1]:
        for s in both:
            s.turn(e)
    loop(tiles // 2, tiles, finish)
    gout_ref[...] = nn(attn_t_ref[...], act2_ref[...]).astype(BF16)
    s_out.step0()
    dsum_ref[...] = jnp.zeros_like(dsum_ref)

    def back_far(span):
        summary_back(span, qkv_ref, sums_ref, probs_ref, attn_t_ref, dattn_ref, delta_ref, dsum_ref)

    def back_near(span):
        span_back(span, qkv_ref, sums_t_ref, probs_ref, dattn_ref, delta_ref, dhid_ref, dkv_ref)

    loop(0, quarter, back_far)
    s_out.step1()
    loop(quarter, 2 * quarter, back_far)
    for s in both:
        s.turn(0)
    loop(2 * quarter, 3 * quarter, back_far)
    s_out.step2()
    loop(3 * quarter, spans, back_far)
    wires.settle(sums.sent)
    sums_all[...] = jnp.zeros_like(sums_all)
    for i in range(3):
        block = lax.rem(place.me + place.devices - 2 + i, place.devices)
        rows = slice(PSPANS + i * spans, PSPANS + (i + 1) * spans)
        sums_all[pl.ds(block, 1)] = dsum_ref[rows, :].astype(BF16)[None]
    for i in range(PSPANS // spans):
        sums_all[i] = dsum_ref[i * spans : (i + 1) * spans, :].astype(BF16)
    s_sum.step0()
    loop(0, quarter, back_near)
    s_sum.step1()
    loop(quarter, 3 * quarter, back_near)
    s_sum.step3()
    for s in both:
        s.step3()
    s_out.step3()
    loop(3 * quarter, spans, back_near)
    gq_ref[...] = tn(act_ref[...], dhid_ref[:, :D]).astype(BF16)
    s_q.step0()
    shares = s_sum.step4()[0] * (1.0 / S)
    for part, g_ref, s in ((0, gk_ref, s_k), (1, gv_ref, s_v)):
        cols = slice(part * D, (part + 1) * D)
        for span in range(spans):
            rows = slice(span * S, (span + 1) * S)
            dhid_ref[rows, (part + 1) * D : (part + 2) * D] = (dkv_ref[rows, cols] + shares[span : span + 1, cols]).astype(BF16)
        g_ref[...] = tn(act_ref[...], dhid_ref[:, (part + 1) * D : (part + 2) * D]).astype(BF16)
        s.step0()

    def finish_tokens(i):
        rows = slice(i * TILE, (i + 1) * TILE)
        dnormed = nt(dhid_ref[rows, :D], q_mat[...]) + nt(dhid_ref[rows, D : 2 * D], k_mat[...])
        dnormed = dnormed + nt(dhid_ref[rows, 2 * D : 3 * D], v_mat[...])
        xhat, inverse = normed_parts(x_ref[rows, :].astype(F32))
        levels_ref[0, 0:1, :] += jnp.sum(dnormed * xhat, axis=0, keepdims=True)
        levels_ref[0, 1:2, :] += jnp.sum(dnormed, axis=0, keepdims=True)
        dtok_ref[rows, :] += norm_back(dnormed, xhat, inverse, gains_ref[0:1, :])

    def output(i):
        rows = slice(i * TILE, (i + 1) * TILE)
        act2_ref[rows, :] = (resid_ref[rows, :] + nn(acted_ref[rows, :], down_mat[...])).astype(BF16)

    total = Total(wires, place, levels_ref, came_ref)
    finish_tokens(0)
    s_q.step1()
    s_k.step1()
    finish_tokens(1)
    s_v.step1()
    finish_tokens(2)
    finish_tokens(3)
    total.send(0)
    s_q.step3()
    output(0)
    s_k.step3()
    output(1)
    total.take(0)
    total.send(1)
    s_v.step3()
    output(2)
    output(3)
    total.take(1)
    total.send(2)
    dwd_ref[...] = s_down.step4() * grad_scale
    dwu_ref[...] = s_up.step4() * grad_scale
    dwo_ref[...] = s_out.step4() * grad_scale
    join_heads((s_q.step4() * grad_scale, s_k.step4() * grad_scale, s_v.step4() * grad_scale), dwqkv_ref)
    total.take(2)
    start = place.me * width
    lanes = pl.ds(pl.multiple_of(start // LANES * LANES, LANES), LANES)
    total_ref[...] = pltpu.roll(levels_ref[3, :, lanes] * grad_scale, lax.rem(LANES - lax.rem(start, LANES), LANES), 1)
    wires.finish()


def fold_all(scatters, d, e):
    for s in scatters:
        s.fold(d, e)


def layer(with_z, grad_scale, x, cotangent, wqkv, wo, wu, wd, vectors, span_doc):
    tok = x.shape[0]
    spans = tok // S
    deep = lax.axis_size("head")
    side = math.isqrt(lax.axis_size("seq") // 2)
    devices = 2 * side * side * deep
    owned = devices if with_z else devices // deep
    hidden_size = wu.shape[0] * owned
    whole, anywhere = pl.BlockSpec(memory_space=VMEM), pl.BlockSpec(memory_space=pl.ANY)
    shape = jax.ShapeDtypeStruct
    peers = 1 + side * side - 1 + deep - 1
    n = 8 * copies_of_gather(side, deep, True) + 8
    n += 7 * (side * side + (side - 1) * side + side - 1 + deep - 1) + peers
    held = scatter_scratch(side, deep, 1, (spans, 2 * D), True)
    for total in (hidden_size, hidden_size, D, D, D, D):
        held += scatter_scratch(side, deep, total // devices, (D,), with_z)
    return pl.pallas_call(
        functools.partial(layer_kernel, with_z, grad_scale),
        out_shape=(
            pltpu.VMEM((tok, D), BF16),
            pltpu.VMEM((tok, D), F32),
            pltpu.VMEM((D // owned, 3 * D), F32),
            pltpu.VMEM((D // owned, D), F32),
            pltpu.VMEM((hidden_size // owned, D), F32),
            pltpu.VMEM((hidden_size // owned, D), F32),
            pltpu.VMEM((8, LANES), F32),
        ),
        in_specs=[anywhere] * 2 + [whole] * 8 + [pl.BlockSpec(memory_space=pltpu.MemorySpace.SMEM)],
        out_specs=(whole,) * 7,
        scratch_shapes=[
            pltpu.VMEM((tok, D), BF16),
            pltpu.VMEM((tok, D), BF16),
            pltpu.VMEM((1, 8, LANES), F32),
            pltpu.VMEM((WIN, S), jnp.int32),
            pltpu.VMEM((D // owned, D), BF16),
            pltpu.VMEM((D // owned, D), BF16),
            pltpu.VMEM((D // owned, D), BF16),
            pltpu.VMEM((D, D), BF16),
            pltpu.VMEM((D, D), BF16),
            pltpu.VMEM((D, D), BF16),
            pltpu.VMEM((D, D), BF16),
            pltpu.VMEM((hidden_size, D), BF16),
            pltpu.VMEM((hidden_size, D), BF16),
            pltpu.VMEM((8, D), F32),
            pltpu.VMEM((devices, 8, LANES), F32),
            pltpu.VMEM((1, spans, 2 * D), BF16),
            pltpu.VMEM((devices, spans, 2 * D), BF16),
            pltpu.VMEM((FAR, 2 * D), BF16),
            pltpu.VMEM((2 * D, FAR), BF16),
            pltpu.VMEM((tok, D), BF16),
            pltpu.VMEM((tok, 3 * D), BF16),
            pltpu.VMEM((spans * PAIRS, KEYS, 2 * S), BF16),
            pltpu.VMEM((D, tok), BF16),
            pltpu.VMEM((tok, D), F32),
            pltpu.VMEM((tok, hidden_size), BF16),
            pltpu.VMEM((tok, hidden_size), BF16),
            pltpu.VMEM((tok, D), BF16),
            pltpu.VMEM((hidden_size, D), BF16),
            pltpu.VMEM((hidden_size, D), BF16),
            pltpu.VMEM((D, D), BF16),
            pltpu.VMEM((D, D), BF16),
            pltpu.VMEM((D, D), BF16),
            pltpu.VMEM((D, D), BF16),
            pltpu.VMEM((tok, 2 * D), F32),
            pltpu.VMEM((spans * PAIRS, 2 * S), F32),
            pltpu.VMEM((FAR, 2 * D), F32),
            pltpu.VMEM((4, 8, D), F32),
            pltpu.VMEM((peers, 8, D), F32),
            pltpu.SemaphoreType.DMA((n,)),
            pltpu.SemaphoreType.DMA((n,)),
            pltpu.SemaphoreType.DMA((2,)),
            *held,
        ],
        compiler_params=pltpu.CompilerParams(vmem_limit_bytes=VMEM_LIMIT - 7 * tok * D, collective_id=0, has_side_effects=True),
        name="mega_layer",
    )(x, cotangent, wqkv, wo, wu, wd, *vectors, span_doc)


def deliver_kernel(*refs):
    count = (len(refs) - 1) // 2
    sems = refs[-1]
    moves = [pltpu.make_async_copy(refs[i], refs[count + i], sems.at[i]) for i in range(count)]
    for move in moves:
        move.start()
    for move in moves:
        move.wait()


def deliver(arrays):
    anywhere = pl.BlockSpec(memory_space=pl.ANY)
    return pl.pallas_call(
        deliver_kernel,
        out_shape=[jax.ShapeDtypeStruct(a.shape, a.dtype) for a in arrays],
        in_specs=[anywhere] * len(arrays),
        out_specs=[anywhere] * len(arrays),
        scratch_shapes=[pltpu.SemaphoreType.DMA((len(arrays),))],
        compiler_params=pltpu.CompilerParams(vmem_limit_bytes=2**20),
        name="deliver",
    )(*arrays)


def shards(tokens, cotangent, w_qkv, w_out, w_up, w_down, gain_one, shift_one, gain_two, shift_two, span_doc):
    tok = tokens.shape[0]
    devices = lax.axis_size("seq") * lax.axis_size("head")
    grad_scale = 1.0 / math.sqrt(tok * devices)
    with_z = w_qkv.shape[0] % 16 == 0
    weights = (w_qkv, w_out, w_up.T, w_down)
    if not with_z:
        weights = tuple(lax.all_gather(w, "head", axis=0, tiled=True) for w in weights)
    vectors = [v[None] for v in (gain_one, shift_one, gain_two, shift_two)]
    width = gain_one.shape[0]
    out_tokens, d_tokens, d_qkv, d_out, d_up, d_down, total = deliver(
        layer(with_z, grad_scale, tokens, cotangent, *weights, vectors, span_doc)
    )
    if not with_z:
        d_qkv, d_out, d_up, d_down = (
            lax.psum_scatter(g, "head", scatter_dimension=0, tiled=True) for g in (d_qkv, d_out, d_up, d_down)
        )
    return out_tokens, d_tokens, d_qkv, d_out, d_up.T, d_down, *(total[k, :width] for k in range(4))


def solution(mesh):
    rows, cols, vec = P(BOTH, None), P(None, BOTH), P(BOTH)
    in_specs = (rows, rows, rows, rows, cols, rows, vec, vec, vec, vec, P())
    out_specs = (rows, rows, rows, rows, cols, rows, vec, vec, vec, vec)
    return jax.shard_map(shards, mesh=mesh, in_specs=in_specs, out_specs=out_specs, check_vma=False)
```

```python
import functools
import math

import jax
import jax.numpy as jnp
from jax import lax
from jax.experimental import pallas as pl
from jax.experimental.pallas import tpu as pltpu
from jax.sharding import PartitionSpec as P

H = 8
HD = 64
D = H * HD
S = 128
MOST = 16
PSPANS = 128
WIN = 2 * MOST
PAIRS = H // 2
LANES = 2 * HD
FAR = PSPANS + WIN
KEYS = S + FAR
EPS = 1e-05
MASKED = -1e30
F32 = jnp.float32
BF16 = jnp.bfloat16
VMEM = pltpu.MemorySpace.VMEM
VMEM_LIMIT = 67043328
TILE = 256
CHUNK = 256


def nn(a, b):
    return lax.dot_general(a, b, (((1,), (0,)), ((), ())), preferred_element_type=F32)


def nt(a, b):
    return lax.dot_general(a, b, (((1,), (1,)), ((), ())), preferred_element_type=F32)


def tn(a, b):
    return lax.dot_general(a, b, (((0,), (0,)), ((), ())), preferred_element_type=F32)


def loop(start, stop, body):
    def step(i, carry):
        body(i)
        return carry

    lax.fori_loop(start, stop, step, 0)


def tile_rows(i, size):
    return pl.ds(pl.multiple_of(i * size, size), size)


def summary_bias(first, span, docs_ref):
    index = first + span
    row = lax.broadcasted_iota(jnp.int32, (PSPANS, S), 0)
    prompt = jnp.where(row < index, 0.0, MASKED)
    wrow = first - MOST + lax.broadcasted_iota(jnp.int32, (WIN, S), 0)
    same = docs_ref[...] == docs_ref[pl.ds(span + MOST, 1), :]
    window = jnp.where(same & (wrow >= PSPANS) & (wrow < index), 0.0, MASKED)
    return jnp.concatenate([prompt, window], axis=0).astype(F32)


def window_docs(first, spans, span_doc_ref):
    row = lax.broadcasted_iota(jnp.int32, (WIN, S), 0)
    docs = jnp.full((WIN, S), -1, jnp.int32)
    for i in range(MOST + spans):
        at = first - MOST - PSPANS + i
        docs = jnp.where((row == i) & (at >= 0), span_doc_ref[jnp.maximum(at, 0)], docs)
    return docs


def head_masks(scale):
    lane = lax.broadcasted_iota(jnp.int32, (1, LANES), 1)
    first = jnp.where(lane < HD, scale, 0.0).astype(BF16)
    second = jnp.where(lane < HD, 0.0, scale).astype(BF16)
    return first, second


def stack_heads(block, masks):
    return jnp.concatenate([block * masks[0], block * masks[1]], axis=0)


def pair_cols(part, pair):
    return slice(part * D + pair * LANES, part * D + (pair + 1) * LANES)


def unstack(pair_t):
    return jnp.concatenate([pair_t[:HD, :S], pair_t[HD:, S:]], axis=0)


def both_heads(pair):
    return slice(pair * 2 * S, (pair + 1) * 2 * S)


def span_scores(span, qkv_ref, grown_ref, stats_ref):
    rows = tile_rows(span, S)
    key_row = lax.broadcasted_iota(jnp.int32, (S, S), 0)
    query = lax.broadcasted_iota(jnp.int32, (S, S), 1)
    causal = jnp.where(key_row <= query, 0.0, MASKED).astype(F32)
    causal = jnp.concatenate([causal, causal], axis=1)
    masks = head_masks(1.0 / math.sqrt(HD))
    for pair in range(PAIRS):
        queries = stack_heads(qkv_ref[rows, pair_cols(0, pair)], masks)
        scores = nt(qkv_ref[rows, pair_cols(1, pair)], queries) + causal
        top = jnp.max(scores, axis=0, keepdims=True)
        grown = jnp.exp(scores - top)
        grown_ref[rows, both_heads(pair)] = grown
        stats_ref[0, pl.ds(span * PAIRS + pair, 1), :] = top
        stats_ref[1, pl.ds(span * PAIRS + pair, 1), :] = jnp.sum(grown, axis=0, keepdims=True)


def attend_span(span, first, qkv_ref, sums_ref, sums_t_ref, docs_ref, grown_ref, stats_ref, attn_t_ref, probs_ref):
    rows = tile_rows(span, S)
    bias = summary_bias(first, span, docs_ref)
    bias = jnp.concatenate([bias, bias], axis=1)
    masks = head_masks(1.0 / math.sqrt(HD))
    for pair in range(PAIRS):
        queries = stack_heads(qkv_ref[rows, pair_cols(0, pair)], masks)
        own_top = stats_ref[0, pl.ds(span * PAIRS + pair, 1), :]
        own_sum = stats_ref[1, pl.ds(span * PAIRS + pair, 1), :]
        far = nt(sums_ref[:, pair_cols(0, pair)], queries) + bias
        top = jnp.maximum(own_top, jnp.max(far, axis=0, keepdims=True))
        far = jnp.exp(far - top)
        fade = jnp.exp(own_top - top)
        share = 1.0 / (own_sum * fade + jnp.sum(far, axis=0, keepdims=True))
        own = grown_ref[rows, both_heads(pair)] * (fade * share)
        probs = jnp.concatenate([own.astype(BF16), (far * share).astype(BF16)], axis=0)
        probs_ref[span * PAIRS + pair] = probs
        vals_t = jnp.concatenate([qkv_ref[rows, pair_cols(2, pair)].T, sums_t_ref[pair_cols(1, pair), :]], axis=1)
        attn_t_ref[pair * LANES : (pair + 1) * LANES, rows] = unstack(nn(vals_t, probs)).astype(BF16)


def summary_back(span, qkv_ref, sums_ref, probs_ref, attn_t_ref, dattn_ref, delta_ref, dsum_ref):
    rows = tile_rows(span, S)
    masks = head_masks(1.0 / math.sqrt(HD))
    ones = head_masks(1.0)
    for pair in range(PAIRS):
        cols, vcols = pair_cols(0, pair), pair_cols(1, pair)
        block = dattn_ref[rows, cols]
        each = block.T.astype(F32) * attn_t_ref[pair * LANES : (pair + 1) * LANES, rows].astype(F32)
        delta = jnp.concatenate(
            [jnp.sum(each[:HD], axis=0, keepdims=True), jnp.sum(each[HD:], axis=0, keepdims=True)], axis=1
        )
        delta_ref[pl.ds(span * PAIRS + pair, 1), :] = delta
        queries = stack_heads(qkv_ref[rows, cols], masks)
        grads = stack_heads(block, ones)
        probs = probs_ref[span * PAIRS + pair, S:, :]
        dprobs = nt(sums_ref[:, vcols], grads)
        dscores = (probs.astype(F32) * (dprobs - delta)).astype(BF16)
        dsum_ref[:, cols] += nn(dscores, queries)
        dsum_ref[:, vcols] += nn(probs, grads)
        probs_ref[span * PAIRS + pair, S:, :] = dscores


def span_back(span, qkv_ref, sums_t_ref, probs_ref, dattn_ref, delta_ref, dqkv_ref, dkv_ref):
    rows = tile_rows(span, S)
    scale = 1.0 / math.sqrt(HD)
    masks = head_masks(scale)
    ones = head_masks(1.0)
    for pair in range(PAIRS):
        cols, vcols = pair_cols(0, pair), pair_cols(1, pair)
        queries = stack_heads(qkv_ref[rows, cols], masks)
        grads = stack_heads(dattn_ref[rows, cols], ones)
        probs = probs_ref[span * PAIRS + pair, :S, :]
        dprobs = nt(qkv_ref[rows, pair_cols(2, pair)], grads)
        delta = delta_ref[pl.ds(span * PAIRS + pair, 1), :]
        dscores = (probs.astype(F32) * (dprobs - delta)).astype(BF16)
        dkv_ref[rows, cols] = nn(dscores, queries)
        dkv_ref[rows, vcols] = nn(probs, grads)
        every = jnp.concatenate([dscores, probs_ref[span * PAIRS + pair, S:, :]], axis=0)
        keys_t = jnp.concatenate([qkv_ref[rows, pair_cols(1, pair)].T, sums_t_ref[cols, :]], axis=1)
        dq_t = unstack(nn(keys_t, every)) * scale
        dqkv_ref[rows, cols] = dq_t.T.astype(BF16)


def split_heads(block, parts):
    low = lax.broadcasted_iota(jnp.int32, (1, LANES), 1) < HD
    for pair in range(PAIRS):
        one, two, three = [block[:, (3 * pair + i) * LANES : (3 * pair + i + 1) * LANES].astype(F32) for i in range(3)]
        mixed = jnp.where(low, one, two), pltpu.roll(jnp.where(low, three, one), HD, 1), jnp.where(low, two, three)
        for part, value in zip(parts, mixed):
            part[:, pair * LANES : (pair + 1) * LANES] = value.astype(part.dtype)


def join_heads(parts, out_ref):
    low = lax.broadcasted_iota(jnp.int32, (1, LANES), 1) < HD
    for pair in range(PAIRS):
        q, k, v = [part[:, pair * LANES : (pair + 1) * LANES] for part in parts]
        k = pltpu.roll(k, HD, 1)
        for i, value in enumerate((jnp.where(low, q, k), jnp.where(low, v, q), jnp.where(low, k, v))):
            out_ref[:, (3 * pair + i) * LANES : (3 * pair + i + 1) * LANES] = value


MESH = pl.DeviceIdType.MESH
BOTH = ("seq", "head")


class Place:
    def __init__(self):
        seq, self.z = lax.axis_index("seq"), lax.axis_index("head")
        self.side = math.isqrt(lax.axis_size("seq") // 2)
        self.deep = lax.axis_size("head")
        self.devices = lax.axis_size("seq") * self.deep
        self.c = lax.rem(seq, 2)
        self.x = lax.rem(seq // 2, self.side)
        self.y = seq // 2 // self.side
        self.me = seq * self.deep + self.z

    def seq(self, y, x, c):
        return (y * self.side + x) * 2 + c

    def along(self, axis, step):
        n, turn = self.side, self.c if axis == 0 else 1 - self.c
        return lax.rem(self.y + turn * step, n), lax.rem(self.x + (1 - turn) * step, n)

    def sibling(self):
        return (self.seq(self.y, self.x, 1 - self.c), self.z)

    def peers(self, axis):
        if axis == "z":
            seq = self.seq(self.y, self.x, self.c)
            return [(seq, lax.rem(self.z + d, self.deep)) for d in range(1, self.deep)]
        return [(self.seq(*self.along(axis, d), self.c), self.z) for d in range(1, self.side)]

    def spot(self, turn, d, e):
        n = self.side
        return lax.rem(self.y + turn * d + (1 - turn) * e, n), lax.rem(self.x + turn * e + (1 - turn) * d, n)

    def steps(self):
        line = [*range(1, self.side), 0]
        return [(d, e) for d in line for e in line][:-1]

    def plane(self):
        return [(self.seq(*self.spot(self.c, d, e), self.c), self.z) for d, e in self.steps()]

    def greet(self):
        barrier = pltpu.get_barrier_semaphore()
        others = [self.sibling(), *self.plane(), *self.peers("z")]
        for other in others:
            pl.semaphore_signal(barrier, inc=1, device_id=other, device_id_type=MESH)
        pl.semaphore_wait(barrier, len(others))


class Wires:
    def __init__(self, send, recv):
        self.send, self.recv, self.used, self.sent = send, recv, 0, []

    def copy(self, src, dst, device):
        i = self.used
        self.used += 1
        move = pltpu.make_async_remote_copy(
            src_ref=src, dst_ref=dst, send_sem=self.send.at[i], recv_sem=self.recv.at[i],
            device_id=device, device_id_type=MESH,
        )
        move.start()
        self.sent.append(move)
        return move

    def local(self, src, dst):
        i = self.used
        self.used += 1
        move = pltpu.make_async_copy(src, dst, self.send.at[i])
        move.start()
        return move

    def settle(self, moves):
        for move in moves:
            move.wait_send()
        done = {id(move) for move in moves}
        self.sent = [move for move in self.sent if id(move) not in done]

    def finish(self):
        self.settle(list(self.sent))


def copies_of_gather(side, deep, with_z):
    return 1 + (deep - 1 if with_z else 0) + (side - 1) + (side - 1) * side + side * side


class Gather:
    def __init__(self, wires, place, shard, full, rows, with_z, direct):
        self.w, self.p, self.full, self.shard = wires, place, full, shard
        self.rows, self.with_z, self.direct, self.sent = rows, with_z, direct, []
        self.group = rows * place.deep if with_z else rows

    def block(self, y, x):
        start = self.p.seq(y, x, self.p.c) * self.group
        return self.full.at[pl.ds(pl.multiple_of(start, self.group), self.group)]

    def step0(self):
        p = self.p
        start = pl.multiple_of(p.me * self.rows, self.rows) if self.with_z else p.seq(p.y, p.x, p.c) * self.rows
        own = self.full.at[pl.ds(start, self.rows)]
        self.moves = [self.w.copy(self.shard, own, d) for d in p.peers("z")] if self.with_z else []
        self.sent += self.moves
        self.placed = self.w.local(self.shard, own)

    def _send(self, place, device):
        move = self.w.copy(self.block(*place), self.block(*place), device)
        self.sent.append(move)
        return move

    def step1(self):
        p, n = self.p, self.p.side
        for move in self.moves:
            move.wait_recv()
        self.placed.wait()
        own = (p.y, p.x)
        self.come, self.crossed = {}, {(0, 0): self._send(own, p.sibling())}
        if self.direct:
            for (d, e), device in zip(p.steps(), p.plane()):
                self.come[-d % n, -e % n] = self._send(own, device)
            return
        for d, device in enumerate(p.peers(0), 1):
            self.come[n - d, 0] = self._send(own, device)
        for e, device in enumerate(p.peers(1), 1):
            self.come[0, n - e] = self._send(own, device)

    def step2(self):
        p, n = self.p, self.p.side
        for d in range(1, n):
            self.come[d, 0].wait_recv()
        for d in range(1, n):
            place = p.spot(p.c, d, 0)
            for e, device in enumerate(p.peers(1), 1):
                self.come[d, n - e] = self._send(place, device)
            self.crossed[d, 0] = self._send(place, p.sibling())

    def step3(self):
        p, n = self.p, self.p.side
        rest = [(d, e) for e in range(n) for d in range(n) if (d, e) not in self.crossed]
        for d, e in rest:
            self.come[d, e].wait_recv()
        for d, e in rest:
            self.crossed[d, e] = self._send(p.spot(p.c, d, e), p.sibling())

    def ready(self, d, e):
        self.crossed[d, e].wait_recv()

    def step4(self):
        for d, e in self.crossed:
            self.ready(d, e)


def spread_small(gathered, devices):
    width = D // devices
    table = gathered.reshape(devices * 8, LANES).astype(BF16)
    pick = lax.broadcasted_iota(jnp.int32, (LANES, D), 0) == lax.broadcasted_iota(jnp.int32, (LANES, D), 1) % width
    every = nn(table, jnp.where(pick, 1.0, 0.0).astype(BF16))
    owner = lax.broadcasted_iota(jnp.int32, (devices * 8, D), 0) // 8
    column = lax.broadcasted_iota(jnp.int32, (devices * 8, D), 1) // width
    return jnp.sum(jnp.where(owner == column, every, 0.0).reshape(devices, 8, D), axis=0)


def normed_parts(values):
    mean = jnp.mean(values, axis=-1, keepdims=True)
    centred = values - mean
    inverse = lax.rsqrt(jnp.mean(centred * centred, axis=-1, keepdims=True) + EPS)
    return centred * inverse, inverse


def norm_back(dnormed, xhat, inverse, gain):
    grown = dnormed * gain
    along = jnp.mean(grown * xhat, axis=-1, keepdims=True)
    return (grown - jnp.mean(grown, axis=-1, keepdims=True) - xhat * along) * inverse


def gelu_parts(h):
    square = h * h
    half = 0.5 + 0.5 * jnp.tanh(h * (0.7978845608 + (0.7978845608 * 0.044715) * square))
    acted = h * half
    slope = 2 * 0.7978845608 + (6 * 0.7978845608 * 0.044715) * square
    return acted, half + acted * (1.0 - half) * slope


def add_into(held, index, others):
    total = held[index].astype(F32)
    for other in others:
        total = total + other.astype(F32)
    held[index] = total.astype(held.dtype)


class Scatter:
    def __init__(self, wires, place, grads, direct, held, hop1, hop2, hopz):
        self.w, self.p, self.grads, self.held = wires, place, grads, held
        self.direct, self.hop1, self.hop2, self.hopz = direct, hop1, hop2, hopz
        self.group = held.shape[1]
        self.crossed, self.first, self.second, self.third = {}, {}, {}, []
        n = place.side
        self.line = [*range(1, n), 0]
        self.order = [(d, e) for d in self.line for e in self.line]

    def at(self, turn, d, e):
        y, x = self.p.spot(turn, d, e)
        return y * self.p.side + x

    def hop(self, d, e):
        return self.hop1.at[d - 1, e] if d else self.hop2.at[e - 1]

    def rows_of(self, j, core):
        return pl.ds(pl.multiple_of((2 * j + core) * self.group, self.group), self.group)

    def cross(self, d, e):
        p = self.p
        j = self.at(1 - p.c, d, e)
        self.crossed[d, e] = self.w.copy(self.grads.at[self.rows_of(j, 1 - p.c)], self.held.at[j], p.sibling())

    def fold(self, d, e):
        p = self.p
        j = self.at(p.c, d, e)
        self.crossed[d, e].wait_recv()
        add_into(self.held, j, [self.grads[self.rows_of(j, p.c)]])
        if self.direct and (d or e):
            owner = p.seq(*p.spot(p.c, d, e), p.c), p.z
            self.first[d, e] = self.w.copy(self.held.at[j], self.hop(d, e), owner)
        elif d:
            self.first[d, e] = self.w.copy(self.held.at[j], self.hop1.at[d - 1, e], p.peers(0)[d - 1])

    def turn(self, e):
        p, n = self.p, self.p.side
        j = self.at(p.c, 0, e)
        for d in range(1, n):
            self.first[d, e].wait_recv()
        add_into(self.held, j, [self.hop1[d - 1, e] for d in range(1, n)])
        if e:
            self.second[e] = self.w.copy(self.held.at[j], self.hop2.at[e - 1], p.peers(1)[e - 1])

    def step0(self):
        for d, e in self.order:
            self.cross(d, e)

    def step1(self):
        for d, e in self.order:
            self.fold(d, e)

    def step2(self):
        for e in self.line if not self.direct else ():
            self.turn(e)

    def step3(self):
        p = self.p
        self.mine = self.at(p.c, 0, 0)
        if self.direct:
            for move in self.first.values():
                move.wait_recv()
            add_into(self.held, self.mine, [self.hop(d, e)[...] for d, e in p.steps()])
        else:
            for move in self.second.values():
                move.wait_recv()
            add_into(self.held, self.mine, [self.hop2[e - 1] for e in range(1, p.side)])
        if self.hopz is not None:
            self.unit = self.group // p.deep
            for d, other in enumerate(p.peers("z"), 1):
                self.third.append(self.w.copy(self.held.at[self.mine, self.unit_rows(d)], self.hopz.at[d - 1], other))

    def unit_rows(self, d):
        p = self.p
        return pl.ds(pl.multiple_of(lax.rem(p.z + d, p.deep) * self.unit, self.unit), self.unit)

    def step4(self):
        if self.hopz is None:
            return self.held[self.mine].astype(F32)
        total = self.held[self.mine, self.unit_rows(0)].astype(F32)
        for d, move in enumerate(self.third):
            move.wait_recv()
            total = total + self.hopz[d].astype(F32)
        return total


def scatter_scratch(side, deep, unit, tail, with_z):
    group = deep * unit
    shapes = [(side * side, group), (side - 1, side, group), (side - 1, group)]
    if with_z:
        shapes.append((deep - 1, unit))
    return [pltpu.VMEM((*shape, *tail), BF16) for shape in shapes]


class Total:
    def __init__(self, wires, place, sums, came):
        self.w, self.p, self.sums, self.came = wires, place, sums, came
        self.slot = 0

    def send(self, level):
        p = self.p
        peers = [[p.sibling()], p.plane(), p.peers("z")][level]
        self.moves = []
        for peer in peers:
            self.moves.append(self.w.copy(self.sums.at[level], self.came.at[self.slot], peer))
            self.slot += 1

    def take(self, level):
        total = self.sums[level]
        for i, move in enumerate(self.moves):
            move.wait_recv()
            total = total + self.came[self.slot - len(self.moves) + i]
        self.sums[level + 1] = total


def layer_kernel(
    with_z, grad_scale,
    x_hbm, cot_hbm, wqkv_ref, wo_ref, wu_ref, wd_ref, gain1_ref, shift1_ref, gain2_ref, shift2_ref, span_doc_ref,
    act2_ref, dtok_ref, dwqkv_ref, dwo_ref, dwu_ref, dwd_ref, total_ref,
    x_ref, cot_ref, small_ref, docs_ref, own_q, own_k, own_v,
    q_mat, k_mat, v_mat, out_mat, up_mat, down_mat, gains_ref, small_all, own_sums, sums_all, sums_ref, sums_t_ref,
    act_ref, qkv_ref, probs_ref, attn_t_ref, resid_ref, acted_ref, dhid_ref, dattn_ref,
    gdown_ref, gup_ref, gout_ref, gq_ref, gk_ref, gv_ref, dkv_ref, stats_ref, delta_ref, dsum_ref, levels_ref, came_ref,
    send, recv, place_sem, *held,
):
    place = Place()
    wires = Wires(send, recv)
    tok = x_ref.shape[0]
    spans = tok // S
    tiles = tok // TILE
    first = place.me * spans
    held = list(held)
    local = [pltpu.make_async_copy(x_hbm, x_ref, place_sem.at[0]), pltpu.make_async_copy(cot_hbm, cot_ref, place_sem.at[1])]
    for move in local:
        move.start()

    def gather(shard, full, direct):
        return Gather(wires, place, shard, full, shard.shape[0], with_z, direct)

    def scatter(grads, z, direct):
        parts = [held.pop(0) for _ in range(4 if z else 3)]
        return Scatter(wires, place, grads, direct, *parts, *([] if z else [None]))

    small = Gather(wires, place, small_ref, small_all, 1, True, True)
    sums = Gather(wires, place, own_sums, sums_all, 1, True, True)
    g_k, g_v, g_q = gather(own_k, k_mat, True), gather(own_v, v_mat, True), gather(own_q, q_mat, True)
    g_out, g_down, g_up = gather(wo_ref, out_mat, False), gather(wd_ref, down_mat, False), gather(wu_ref, up_mat, False)
    s_sum = scatter(sums_all, True, True)
    s_down, s_up, s_out = [scatter(g, with_z, False) for g in (gdown_ref, gup_ref, gout_ref)]
    s_q, s_k, s_v = [scatter(g, with_z, True) for g in (gq_ref, gk_ref, gv_ref)]

    width = gain1_ref.shape[1]
    small_ref[...] = jnp.zeros_like(small_ref)
    for k, ref in enumerate((gain1_ref, shift1_ref, gain2_ref, shift2_ref)):
        small_ref[0, k : k + 1, :width] = ref[...].astype(F32)
    split_heads(wqkv_ref[...], (own_q, own_k, own_v))
    place.greet()
    for g in (small, g_k, g_v, g_q, g_down, g_out):
        g.step0()
    small.step1()
    g_k.step1()
    g_v.step1()
    small.step3()
    g_k.step3()
    g_q.step1()
    docs_ref[...] = window_docs(first, spans, span_doc_ref)
    small.step4()
    gains_ref[...] = spread_small(small_all[...], place.devices)
    local[0].wait()

    def norm(i):
        rows = tile_rows(i, S)
        xhat, _ = normed_parts(x_ref[rows, :].astype(F32))
        act_ref[rows, :] = (xhat * gains_ref[0:1, :] + gains_ref[1:2, :]).astype(BF16)

    loop(0, spans, norm)
    g_v.step3()
    g_k.step4()

    def project(mat, part):
        block = nn(act_ref[...], mat[...]).astype(BF16)
        qkv_ref[:, part * D : (part + 1) * D] = block
        if part:
            mean = jnp.sum(block.astype(F32).reshape(spans, S, D), axis=1) * (1.0 / S)
            own_sums[0, :, (part - 1) * D : part * D] = mean.astype(BF16)

    project(k_mat, 1)
    g_q.step3()
    g_down.step1()
    g_out.step1()
    g_v.step4()
    project(v_mat, 2)
    sums.step0()
    g_up.step0()
    g_q.step4()
    project(q_mat, 0)
    half = spans // 2
    loop(0, half, lambda i: span_scores(i, qkv_ref, dkv_ref, stats_ref))
    sums.step1()
    loop(half, spans, lambda i: span_scores(i, qkv_ref, dkv_ref, stats_ref))
    sums.step3()
    g_out.step2()
    sums.step4()
    for i in range(PSPANS // MOST):
        two = sums_all[pl.ds(2 * i, 2)].astype(F32)
        sums_ref[MOST * i : MOST * (i + 1), :] = two.reshape(MOST, 2 * D).astype(BF16)
    before = sums_all[pl.ds(lax.rem(place.me + place.devices - 2, place.devices), 1)].astype(F32)
    last = sums_all[pl.ds(lax.rem(place.me + place.devices - 1, place.devices), 1)].astype(F32)
    here = sums_all[pl.ds(place.me, 1)].astype(F32)
    nothing = jnp.zeros_like(here)
    sums_ref[PSPANS : PSPANS + MOST, :] = jnp.concatenate([before, last], axis=0).reshape(MOST, 2 * D).astype(BF16)
    sums_ref[PSPANS + MOST :, :] = jnp.concatenate([here, nothing], axis=0).reshape(MOST, 2 * D).astype(BF16)
    sums_t_ref[...] = sums_ref[...].T

    def attend(span):
        attend_span(span, first, qkv_ref, sums_ref, sums_t_ref, docs_ref, dkv_ref, stats_ref, attn_t_ref, probs_ref)

    quarter = spans // 4
    g_up.step1()
    loop(0, quarter, attend)
    g_down.step2()
    loop(quarter, 3 * quarter, attend)
    g_out.step3()
    loop(3 * quarter, spans, attend)
    g_out.step4()

    def residual(i):
        rows = tile_rows(i, TILE)
        resid = x_ref[rows, :].astype(F32) + tn(attn_t_ref[:, rows], out_mat[...])
        resid_ref[rows, :] = resid
        xhat, _ = normed_parts(resid)
        act2_ref[rows, :] = (xhat * gains_ref[2:3, :] + gains_ref[3:4, :]).astype(BF16)

    loop(0, tiles, residual)
    local[1].wait()
    g_up.step2()

    def feed(i):
        part = tile_rows(i, CHUNK)
        acted, slope = gelu_parts(nt(act2_ref[...], up_mat[part, :]))
        acted = acted.astype(BF16)
        acted_ref[:, part] = acted
        dhid = (nt(cot_ref[...], down_mat[part, :]) * slope).astype(BF16)
        dhid_ref[:, part] = dhid
        gdown_ref[part, :] = tn(acted, cot_ref[...]).astype(BF16)
        gup_ref[part, :] = tn(dhid, act2_ref[...]).astype(BF16)

    both = (s_down, s_up)
    blocks = [(d, e) for e in range(place.side) for d in range(place.side)]
    waiting = []
    if s_up.group == CHUNK:
        for d, e in blocks:
            if (d, e) == (0, 1):
                g_down.step3()
                g_up.step3()
            g_down.ready(d, e)
            g_up.ready(d, e)
            theirs = 2 * s_up.at(1 - place.c, d, e) + 1 - place.c
            ours = 2 * s_up.at(place.c, d, e) + place.c
            loop(0, 2, lambda i: feed(theirs + i * (ours - theirs)))
            for s in both:
                s.cross(d, e)
            waiting.append((d, e))
            if len(waiting) > 1:
                fold_all(both, *waiting.pop(0))
    else:
        for g in (g_down, g_up):
            g.step3()
            g.step4()
        loop(0, up_mat.shape[0] // CHUNK, feed)
        for s in both:
            s.step0()
        waiting = list(s_up.order)
    levels_ref[...] = jnp.zeros_like(levels_ref)

    def finish(i):
        rows = tile_rows(i, TILE)
        dnormed = nn(dhid_ref[rows, :], up_mat[...])
        xhat, inverse = normed_parts(resid_ref[rows, :])
        levels_ref[0, 2:3, :] += jnp.sum(dnormed * xhat, axis=0, keepdims=True)
        levels_ref[0, 3:4, :] += jnp.sum(dnormed, axis=0, keepdims=True)
        dresid = cot_ref[rows, :].astype(F32) + norm_back(dnormed, xhat, inverse, gains_ref[2:3, :])
        dtok_ref[rows, :] = dresid
        branch = dresid.astype(BF16)
        act2_ref[rows, :] = branch
        dattn_ref[rows, :] = nt(branch, out_mat[...]).astype(BF16)

    loop(0, tiles // 2, finish)
    for d, e in waiting:
        fold_all(both, d, e)
    loop(tiles // 2, tiles, finish)
    gout_ref[...] = nn(attn_t_ref[...], act2_ref[...]).astype(BF16)
    s_out.step0()
    dsum_ref[...] = jnp.zeros_like(dsum_ref)

    def back_far(span):
        summary_back(span, qkv_ref, sums_ref, probs_ref, attn_t_ref, dattn_ref, delta_ref, dsum_ref)

    def back_near(span):
        span_back(span, qkv_ref, sums_t_ref, probs_ref, dattn_ref, delta_ref, dhid_ref, dkv_ref)

    loop(0, quarter, back_far)
    s_out.step1()
    loop(quarter, 2 * quarter, back_far)
    for e in s_up.line:
        for s in both:
            s.turn(e)
    loop(2 * quarter, spans, back_far)
    wires.settle(sums.sent)
    sums_all[...] = jnp.zeros_like(sums_all)
    for i in range(3):
        block = lax.rem(place.me + place.devices - 2 + i, place.devices)
        rows = slice(PSPANS + i * spans, PSPANS + (i + 1) * spans)
        sums_all[pl.ds(block, 1)] = dsum_ref[rows, :].astype(BF16)[None]
    for i in range(PSPANS // spans):
        sums_all[i] = dsum_ref[i * spans : (i + 1) * spans, :].astype(BF16)
    s_sum.step0()
    loop(0, quarter, back_near)
    s_sum.step1()
    s_out.step2()
    loop(quarter, 3 * quarter, back_near)
    s_sum.step3()
    for s in both:
        s.step3()
    s_out.step3()
    loop(3 * quarter, spans, back_near)
    gq_ref[...] = tn(act_ref[...], dhid_ref[:, :D]).astype(BF16)
    s_q.step0()
    shares = s_sum.step4()[0] * (1.0 / S)
    for part, g_ref, s in ((0, gk_ref, s_k), (1, gv_ref, s_v)):
        cols = slice(part * D, (part + 1) * D)
        for span in range(spans):
            rows = slice(span * S, (span + 1) * S)
            dhid_ref[rows, (part + 1) * D : (part + 2) * D] = (dkv_ref[rows, cols] + shares[span : span + 1, cols]).astype(BF16)
        g_ref[...] = tn(act_ref[...], dhid_ref[:, (part + 1) * D : (part + 2) * D]).astype(BF16)
        s.step0()

    def finish_tokens(i):
        rows = slice(i * TILE, (i + 1) * TILE)
        dnormed = nt(dhid_ref[rows, :D], q_mat[...]) + nt(dhid_ref[rows, D : 2 * D], k_mat[...])
        dnormed = dnormed + nt(dhid_ref[rows, 2 * D : 3 * D], v_mat[...])
        xhat, inverse = normed_parts(x_ref[rows, :].astype(F32))
        levels_ref[0, 0:1, :] += jnp.sum(dnormed * xhat, axis=0, keepdims=True)
        levels_ref[0, 1:2, :] += jnp.sum(dnormed, axis=0, keepdims=True)
        dtok_ref[rows, :] += norm_back(dnormed, xhat, inverse, gains_ref[0:1, :])

    def output(i):
        rows = slice(i * TILE, (i + 1) * TILE)
        act2_ref[rows, :] = (resid_ref[rows, :] + nn(acted_ref[rows, :], down_mat[...])).astype(BF16)

    total = Total(wires, place, levels_ref, came_ref)
    finish_tokens(0)
    s_q.step1()
    s_k.step1()
    finish_tokens(1)
    s_v.step1()
    finish_tokens(2)
    finish_tokens(3)
    total.send(0)
    output(0)
    total.take(0)
    total.send(1)
    s_q.step3()
    output(1)
    s_k.step3()
    output(2)
    total.take(1)
    total.send(2)
    s_v.step3()
    output(3)
    dwd_ref[...] = s_down.step4() * grad_scale
    dwu_ref[...] = s_up.step4() * grad_scale
    dwo_ref[...] = s_out.step4() * grad_scale
    join_heads((s_q.step4() * grad_scale, s_k.step4() * grad_scale, s_v.step4() * grad_scale), dwqkv_ref)
    total.take(2)
    start = place.me * width
    lanes = pl.ds(pl.multiple_of(start // LANES * LANES, LANES), LANES)
    total_ref[...] = pltpu.roll(levels_ref[3, :, lanes] * grad_scale, lax.rem(LANES - lax.rem(start, LANES), LANES), 1)
    wires.finish()


def fold_all(scatters, d, e):
    for s in scatters:
        s.fold(d, e)


def layer(with_z, grad_scale, x, cotangent, wqkv, wo, wu, wd, vectors, span_doc):
    tok = x.shape[0]
    spans = tok // S
    deep = lax.axis_size("head")
    side = math.isqrt(lax.axis_size("seq") // 2)
    devices = 2 * side * side * deep
    owned = devices if with_z else devices // deep
    hidden_size = wu.shape[0] * owned
    whole, anywhere = pl.BlockSpec(memory_space=VMEM), pl.BlockSpec(memory_space=pl.ANY)
    shape = jax.ShapeDtypeStruct
    peers = 1 + side * side - 1 + deep - 1
    n = 8 * copies_of_gather(side, deep, True) + 8
    n += 7 * (side * side + (side - 1) * side + side - 1 + deep - 1) + peers
    held = scatter_scratch(side, deep, 1, (spans, 2 * D), True)
    for total in (hidden_size, hidden_size, D, D, D, D):
        held += scatter_scratch(side, deep, total // devices, (D,), with_z)
    return pl.pallas_call(
        functools.partial(layer_kernel, with_z, grad_scale),
        out_shape=(
            pltpu.VMEM((tok, D), BF16),
            pltpu.VMEM((tok, D), F32),
            pltpu.VMEM((D // owned, 3 * D), F32),
            pltpu.VMEM((D // owned, D), F32),
            pltpu.VMEM((hidden_size // owned, D), F32),
            pltpu.VMEM((hidden_size // owned, D), F32),
            pltpu.VMEM((8, LANES), F32),
        ),
        in_specs=[anywhere] * 2 + [whole] * 8 + [pl.BlockSpec(memory_space=pltpu.MemorySpace.SMEM)],
        out_specs=(whole,) * 7,
        scratch_shapes=[
            pltpu.VMEM((tok, D), BF16),
            pltpu.VMEM((tok, D), BF16),
            pltpu.VMEM((1, 8, LANES), F32),
            pltpu.VMEM((WIN, S), jnp.int32),
            pltpu.VMEM((D // owned, D), BF16),
            pltpu.VMEM((D // owned, D), BF16),
            pltpu.VMEM((D // owned, D), BF16),
            pltpu.VMEM((D, D), BF16),
            pltpu.VMEM((D, D), BF16),
            pltpu.VMEM((D, D), BF16),
            pltpu.VMEM((D, D), BF16),
            pltpu.VMEM((hidden_size, D), BF16),
            pltpu.VMEM((hidden_size, D), BF16),
            pltpu.VMEM((8, D), F32),
            pltpu.VMEM((devices, 8, LANES), F32),
            pltpu.VMEM((1, spans, 2 * D), BF16),
            pltpu.VMEM((devices, spans, 2 * D), BF16),
            pltpu.VMEM((FAR, 2 * D), BF16),
            pltpu.VMEM((2 * D, FAR), BF16),
            pltpu.VMEM((tok, D), BF16),
            pltpu.VMEM((tok, 3 * D), BF16),
            pltpu.VMEM((spans * PAIRS, KEYS, 2 * S), BF16),
            pltpu.VMEM((D, tok), BF16),
            pltpu.VMEM((tok, D), F32),
            pltpu.VMEM((tok, hidden_size), BF16),
            pltpu.VMEM((tok, hidden_size), BF16),
            pltpu.VMEM((tok, D), BF16),
            pltpu.VMEM((hidden_size, D), BF16),
            pltpu.VMEM((hidden_size, D), BF16),
            pltpu.VMEM((D, D), BF16),
            pltpu.VMEM((D, D), BF16),
            pltpu.VMEM((D, D), BF16),
            pltpu.VMEM((D, D), BF16),
            pltpu.VMEM((tok, 2 * D), F32),
            pltpu.VMEM((2, spans * PAIRS, 2 * S), F32),
            pltpu.VMEM((spans * PAIRS, 2 * S), F32),
            pltpu.VMEM((FAR, 2 * D), F32),
            pltpu.VMEM((4, 8, D), F32),
            pltpu.VMEM((peers, 8, D), F32),
            pltpu.SemaphoreType.DMA((n,)),
            pltpu.SemaphoreType.DMA((n,)),
            pltpu.SemaphoreType.DMA((2,)),
            *held,
        ],
        compiler_params=pltpu.CompilerParams(vmem_limit_bytes=VMEM_LIMIT - 7 * tok * D, collective_id=0, has_side_effects=True),
        name="mega_layer",
    )(x, cotangent, wqkv, wo, wu, wd, *vectors, span_doc)


def deliver_kernel(*refs):
    count = (len(refs) - 1) // 2
    sems = refs[-1]
    moves = [pltpu.make_async_copy(refs[i], refs[count + i], sems.at[i]) for i in range(count)]
    for move in moves:
        move.start()
    for move in moves:
        move.wait()


def deliver(arrays):
    anywhere = pl.BlockSpec(memory_space=pl.ANY)
    return pl.pallas_call(
        deliver_kernel,
        out_shape=[jax.ShapeDtypeStruct(a.shape, a.dtype) for a in arrays],
        in_specs=[anywhere] * len(arrays),
        out_specs=[anywhere] * len(arrays),
        scratch_shapes=[pltpu.SemaphoreType.DMA((len(arrays),))],
        compiler_params=pltpu.CompilerParams(vmem_limit_bytes=2**20),
        name="deliver",
    )(*arrays)


def shards(tokens, cotangent, w_qkv, w_out, w_up, w_down, gain_one, shift_one, gain_two, shift_two, span_doc):
    tok = tokens.shape[0]
    devices = lax.axis_size("seq") * lax.axis_size("head")
    grad_scale = 1.0 / math.sqrt(tok * devices)
    with_z = w_qkv.shape[0] % 16 == 0
    weights = (w_qkv, w_out, w_up.T, w_down)
    if not with_z:
        weights = tuple(lax.all_gather(w, "head", axis=0, tiled=True) for w in weights)
    vectors = [v[None] for v in (gain_one, shift_one, gain_two, shift_two)]
    width = gain_one.shape[0]
    out_tokens, d_tokens, d_qkv, d_out, d_up, d_down, total = deliver(
        layer(with_z, grad_scale, tokens, cotangent, *weights, vectors, span_doc)
    )
    if not with_z:
        d_qkv, d_out, d_up, d_down = (
            lax.psum_scatter(g, "head", scatter_dimension=0, tiled=True) for g in (d_qkv, d_out, d_up, d_down)
        )
    return out_tokens, d_tokens, d_qkv, d_out, d_up.T, d_down, *(total[k, :width] for k in range(4))


def solution(mesh):
    rows, cols, vec = P(BOTH, None), P(None, BOTH), P(BOTH)
    in_specs = (rows, rows, rows, rows, cols, rows, vec, vec, vec, vec, P())
    out_specs = (rows, rows, rows, rows, cols, rows, vec, vec, vec, vec)
    return jax.shard_map(shards, mesh=mesh, in_specs=in_specs, out_specs=out_specs, check_vma=False)
```

```python
import functools
import math

import jax
import jax.numpy as jnp
from jax import lax
from jax.experimental import pallas as pl
from jax.experimental.pallas import tpu as pltpu
from jax.sharding import PartitionSpec as P

H = 8
HD = 64
D = H * HD
S = 128
MOST = 16
PSPANS = 128
WIN = 2 * MOST
PAIRS = H // 2
LANES = 2 * HD
FAR = PSPANS + WIN
KEYS = S + FAR
EPS = 1e-05
MASKED = -1e30
F32 = jnp.float32
BF16 = jnp.bfloat16
VMEM = pltpu.MemorySpace.VMEM
VMEM_LIMIT = 67043328
TILE = 256
CHUNK = 256


def nn(a, b):
    return lax.dot_general(a, b, (((1,), (0,)), ((), ())), preferred_element_type=F32)


def nt(a, b):
    return lax.dot_general(a, b, (((1,), (1,)), ((), ())), preferred_element_type=F32)


def tn(a, b):
    return lax.dot_general(a, b, (((0,), (0,)), ((), ())), preferred_element_type=F32)


def loop(start, stop, body):
    def step(i, carry):
        body(i)
        return carry

    lax.fori_loop(start, stop, step, 0)


def tile_rows(i, size):
    return pl.ds(pl.multiple_of(i * size, size), size)


def summary_bias(first, span, docs_ref):
    index = first + span
    row = lax.broadcasted_iota(jnp.int32, (PSPANS, S), 0)
    prompt = jnp.where(row < index, 0.0, MASKED)
    wrow = first - MOST + lax.broadcasted_iota(jnp.int32, (WIN, S), 0)
    same = docs_ref[...] == docs_ref[pl.ds(span + MOST, 1), :]
    window = jnp.where(same & (wrow >= PSPANS) & (wrow < index), 0.0, MASKED)
    return jnp.concatenate([prompt, window], axis=0).astype(F32)


def window_docs(first, spans, span_doc_ref):
    row = lax.broadcasted_iota(jnp.int32, (WIN, S), 0)
    docs = jnp.full((WIN, S), -1, jnp.int32)
    for i in range(MOST + spans):
        at = first - MOST - PSPANS + i
        docs = jnp.where((row == i) & (at >= 0), span_doc_ref[jnp.maximum(at, 0)], docs)
    return docs


def head_masks(scale):
    lane = lax.broadcasted_iota(jnp.int32, (1, LANES), 1)
    first = jnp.where(lane < HD, scale, 0.0).astype(BF16)
    second = jnp.where(lane < HD, 0.0, scale).astype(BF16)
    return first, second


def stack_heads(block, masks):
    return jnp.concatenate([block * masks[0], block * masks[1]], axis=0)


def pair_cols(part, pair):
    return slice(part * D + pair * LANES, part * D + (pair + 1) * LANES)


def unstack(pair_t):
    return jnp.concatenate([pair_t[:HD, :S], pair_t[HD:, S:]], axis=0)


def both_heads(pair):
    return slice(pair * 2 * S, (pair + 1) * 2 * S)


def span_scores(span, qkv_ref, grown_ref, stats_ref):
    rows = tile_rows(span, S)
    key_row = lax.broadcasted_iota(jnp.int32, (S, S), 0)
    query = lax.broadcasted_iota(jnp.int32, (S, S), 1)
    causal = jnp.where(key_row <= query, 0.0, MASKED).astype(F32)
    causal = jnp.concatenate([causal, causal], axis=1)
    masks = head_masks(1.0 / math.sqrt(HD))
    for pair in range(PAIRS):
        queries = stack_heads(qkv_ref[rows, pair_cols(0, pair)], masks)
        scores = nt(qkv_ref[rows, pair_cols(1, pair)], queries) + causal
        top = jnp.max(scores, axis=0, keepdims=True)
        grown = jnp.exp(scores - top)
        grown_ref[rows, both_heads(pair)] = grown
        stats_ref[0, pl.ds(span * PAIRS + pair, 1), :] = top
        stats_ref[1, pl.ds(span * PAIRS + pair, 1), :] = jnp.sum(grown, axis=0, keepdims=True)


def attend_span(span, first, qkv_ref, sums_ref, sums_t_ref, docs_ref, grown_ref, stats_ref, attn_t_ref, probs_ref):
    rows = tile_rows(span, S)
    bias = summary_bias(first, span, docs_ref)
    bias = jnp.concatenate([bias, bias], axis=1)
    masks = head_masks(1.0 / math.sqrt(HD))
    for pair in range(PAIRS):
        queries = stack_heads(qkv_ref[rows, pair_cols(0, pair)], masks)
        own_top = stats_ref[0, pl.ds(span * PAIRS + pair, 1), :]
        own_sum = stats_ref[1, pl.ds(span * PAIRS + pair, 1), :]
        far = nt(sums_ref[:, pair_cols(0, pair)], queries) + bias
        top = jnp.maximum(own_top, jnp.max(far, axis=0, keepdims=True))
        far = jnp.exp(far - top)
        fade = jnp.exp(own_top - top)
        share = 1.0 / (own_sum * fade + jnp.sum(far, axis=0, keepdims=True))
        own = grown_ref[rows, both_heads(pair)] * (fade * share)
        probs = jnp.concatenate([own.astype(BF16), (far * share).astype(BF16)], axis=0)
        probs_ref[span * PAIRS + pair] = probs
        vals_t = jnp.concatenate([qkv_ref[rows, pair_cols(2, pair)].T, sums_t_ref[pair_cols(1, pair), :]], axis=1)
        attn_t_ref[pair * LANES : (pair + 1) * LANES, rows] = unstack(nn(vals_t, probs)).astype(BF16)


def summary_back(span, qkv_ref, sums_ref, probs_ref, attn_t_ref, dattn_ref, delta_ref, dsum_ref):
    rows = tile_rows(span, S)
    masks = head_masks(1.0 / math.sqrt(HD))
    ones = head_masks(1.0)
    for pair in range(PAIRS):
        cols, vcols = pair_cols(0, pair), pair_cols(1, pair)
        block = dattn_ref[rows, cols]
        each = block.T.astype(F32) * attn_t_ref[pair * LANES : (pair + 1) * LANES, rows].astype(F32)
        delta = jnp.concatenate(
            [jnp.sum(each[:HD], axis=0, keepdims=True), jnp.sum(each[HD:], axis=0, keepdims=True)], axis=1
        )
        delta_ref[pl.ds(span * PAIRS + pair, 1), :] = delta
        queries = stack_heads(qkv_ref[rows, cols], masks)
        grads = stack_heads(block, ones)
        probs = probs_ref[span * PAIRS + pair, S:, :]
        dprobs = nt(sums_ref[:, vcols], grads)
        dscores = (probs.astype(F32) * (dprobs - delta)).astype(BF16)
        dsum_ref[:, cols] += nn(dscores, queries)
        dsum_ref[:, vcols] += nn(probs, grads)
        probs_ref[span * PAIRS + pair, S:, :] = dscores


def span_back(span, qkv_ref, sums_t_ref, probs_ref, dattn_ref, delta_ref, dqkv_ref, dkv_ref):
    rows = tile_rows(span, S)
    scale = 1.0 / math.sqrt(HD)
    masks = head_masks(scale)
    ones = head_masks(1.0)
    for pair in range(PAIRS):
        cols, vcols = pair_cols(0, pair), pair_cols(1, pair)
        queries = stack_heads(qkv_ref[rows, cols], masks)
        grads = stack_heads(dattn_ref[rows, cols], ones)
        probs = probs_ref[span * PAIRS + pair, :S, :]
        dprobs = nt(qkv_ref[rows, pair_cols(2, pair)], grads)
        delta = delta_ref[pl.ds(span * PAIRS + pair, 1), :]
        dscores = (probs.astype(F32) * (dprobs - delta)).astype(BF16)
        dkv_ref[rows, cols] = nn(dscores, queries)
        dkv_ref[rows, vcols] = nn(probs, grads)
        every = jnp.concatenate([dscores, probs_ref[span * PAIRS + pair, S:, :]], axis=0)
        keys_t = jnp.concatenate([qkv_ref[rows, pair_cols(1, pair)].T, sums_t_ref[cols, :]], axis=1)
        dq_t = unstack(nn(keys_t, every)) * scale
        dqkv_ref[rows, cols] = dq_t.T.astype(BF16)


def split_heads(block, parts):
    low = lax.broadcasted_iota(jnp.int32, (1, LANES), 1) < HD
    for pair in range(PAIRS):
        one, two, three = [block[:, (3 * pair + i) * LANES : (3 * pair + i + 1) * LANES].astype(F32) for i in range(3)]
        mixed = jnp.where(low, one, two), pltpu.roll(jnp.where(low, three, one), HD, 1), jnp.where(low, two, three)
        for part, value in zip(parts, mixed):
            part[:, pair * LANES : (pair + 1) * LANES] = value.astype(part.dtype)


def join_heads(parts, out_ref):
    low = lax.broadcasted_iota(jnp.int32, (1, LANES), 1) < HD
    for pair in range(PAIRS):
        q, k, v = [part[:, pair * LANES : (pair + 1) * LANES] for part in parts]
        k = pltpu.roll(k, HD, 1)
        for i, value in enumerate((jnp.where(low, q, k), jnp.where(low, v, q), jnp.where(low, k, v))):
            out_ref[:, (3 * pair + i) * LANES : (3 * pair + i + 1) * LANES] = value


MESH = pl.DeviceIdType.MESH
BOTH = ("seq", "head")


class Place:
    def __init__(self):
        seq, self.z = lax.axis_index("seq"), lax.axis_index("head")
        self.side = math.isqrt(lax.axis_size("seq") // 2)
        self.deep = lax.axis_size("head")
        self.devices = lax.axis_size("seq") * self.deep
        self.c = lax.rem(seq, 2)
        self.x = lax.rem(seq // 2, self.side)
        self.y = seq // 2 // self.side
        self.me = seq * self.deep + self.z

    def seq(self, y, x, c):
        return (y * self.side + x) * 2 + c

    def along(self, axis, step):
        n, turn = self.side, self.c if axis == 0 else 1 - self.c
        return lax.rem(self.y + turn * step, n), lax.rem(self.x + (1 - turn) * step, n)

    def sibling(self):
        return (self.seq(self.y, self.x, 1 - self.c), self.z)

    def peers(self, axis):
        if axis == "z":
            seq = self.seq(self.y, self.x, self.c)
            return [(seq, lax.rem(self.z + d, self.deep)) for d in range(1, self.deep)]
        return [(self.seq(*self.along(axis, d), self.c), self.z) for d in range(1, self.side)]

    def spot(self, turn, d, e):
        n = self.side
        return lax.rem(self.y + turn * d + (1 - turn) * e, n), lax.rem(self.x + turn * e + (1 - turn) * d, n)

    def steps(self):
        line = [*range(1, self.side), 0]
        return [(d, e) for d in line for e in line][:-1]

    def plane(self):
        return [(self.seq(*self.spot(self.c, d, e), self.c), self.z) for d, e in self.steps()]

    def greet(self):
        barrier = pltpu.get_barrier_semaphore()
        others = [self.sibling(), *self.plane(), *self.peers("z")]
        for other in others:
            pl.semaphore_signal(barrier, inc=1, device_id=other, device_id_type=MESH)
        pl.semaphore_wait(barrier, len(others))


def wait_bytes(ref, sem):
    pltpu.make_async_copy(ref, ref, sem).wait()


class Wires:
    def __init__(self, sems):
        self.sems, self.used, self.unsent = sems, 0, []

    def sem(self):
        self.used += 1
        return self.sems.at[self.used - 1]

    def copy(self, src, dst, device, sent, came):
        pltpu.make_async_remote_copy(
            src_ref=src, dst_ref=dst, send_sem=sent, recv_sem=came, device_id=device, device_id_type=MESH
        ).start()

    def finish(self):
        for ref, sem in self.unsent:
            wait_bytes(ref, sem)


def semaphores(side):
    return 5 * 5 + 3 * 8 + 3 * (side * side + side + 3) + 4 * 4 + 4


class Gather:
    def __init__(self, wires, place, shard, full, rows, with_z, direct):
        self.w, self.p, self.full, self.shard = wires, place, full, shard
        self.rows, self.with_z, self.direct = rows, with_z, direct
        self.group = rows * place.deep if with_z else rows
        self.out, self.local, self.deep = wires.sem(), wires.sem(), wires.sem()
        self.level, self.cross = wires.sem(), wires.sem()
        if not direct:
            self.column, self.cross_row, self.cross_rest = wires.sem(), wires.sem(), wires.sem()
        sent = (2 * place.side**2 - 1) * self.group + (place.deep - 1 if with_z else 0) * rows
        self.unsent = (full.at[pl.ds(0, sent)], self.out)
        wires.unsent.append(self.unsent)
        self.done = set()

    def block(self, y, x):
        start = self.p.seq(y, x, self.p.c) * self.group
        return self.full.at[pl.ds(pl.multiple_of(start, self.group), self.group)]

    def _send(self, place, device, came):
        self.w.copy(self.block(*place), self.block(*place), device, self.out, came)

    def _wait(self, groups, sem):
        wait_bytes(self.full.at[pl.ds(0, groups * self.group)], sem)

    def step0(self):
        p = self.p
        start = pl.multiple_of(p.me * self.rows, self.rows) if self.with_z else p.seq(p.y, p.x, p.c) * self.rows
        own = self.full.at[pl.ds(start, self.rows)]
        for device in p.peers("z") if self.with_z else ():
            self.w.copy(self.shard, own, device, self.out, self.deep)
        self.placed = pltpu.make_async_copy(self.shard, own, self.local)
        self.placed.start()

    def step1(self):
        p = self.p
        if self.with_z:
            wait_bytes(self.full.at[pl.ds(0, (p.deep - 1) * self.rows)], self.deep)
        self.placed.wait()
        own = (p.y, p.x)
        if self.direct:
            for device in p.plane():
                self._send(own, device, self.level)
        else:
            for device in p.peers(0):
                self._send(own, device, self.level)
            for device in p.peers(1):
                self._send(own, device, self.column)
        self._send(own, p.sibling(), self.cross)

    def step2(self):
        p, n = self.p, self.p.side
        self._wait(n - 1, self.level)
        for d in range(1, n):
            place = p.spot(p.c, d, 0)
            for device in p.peers(1):
                self._send(place, device, self.column)
            self._send(place, p.sibling(), self.cross_row)

    def step3(self):
        p, n = self.p, self.p.side
        if self.direct:
            self._wait(n * n - 1, self.level)
            for d, e in p.steps():
                self._send(p.spot(p.c, d, e), p.sibling(), self.cross)
        else:
            self._wait(n * (n - 1), self.column)
            for e in range(1, n):
                for d in range(n):
                    self._send(p.spot(p.c, d, e), p.sibling(), self.cross_rest)

    def ready(self, d, e):
        n = self.p.side
        sems = (1, self.cross), (n - 1, self.cross_row), (n * (n - 1), self.cross_rest)
        which = 2 if e else 1 if d else 0
        if which not in self.done:
            self.done.add(which)
            self._wait(*sems[which])

    def step4(self):
        n = self.p.side
        if self.direct:
            self._wait(n * n, self.cross)
            return
        for d, e in [(0, 0), *self.p.steps()]:
            self.ready(d, e)

    def settle(self):
        wait_bytes(*self.unsent)
        self.w.unsent = [pair for pair in self.w.unsent if pair is not self.unsent]


def spread_small(gathered, devices):
    width = D // devices
    table = gathered.reshape(devices * 8, LANES).astype(BF16)
    pick = lax.broadcasted_iota(jnp.int32, (LANES, D), 0) == lax.broadcasted_iota(jnp.int32, (LANES, D), 1) % width
    every = nn(table, jnp.where(pick, 1.0, 0.0).astype(BF16))
    owner = lax.broadcasted_iota(jnp.int32, (devices * 8, D), 0) // 8
    column = lax.broadcasted_iota(jnp.int32, (devices * 8, D), 1) // width
    return jnp.sum(jnp.where(owner == column, every, 0.0).reshape(devices, 8, D), axis=0)


def normed_parts(values):
    mean = jnp.mean(values, axis=-1, keepdims=True)
    centred = values - mean
    inverse = lax.rsqrt(jnp.mean(centred * centred, axis=-1, keepdims=True) + EPS)
    return centred * inverse, inverse


def norm_back(dnormed, xhat, inverse, gain):
    grown = dnormed * gain
    along = jnp.mean(grown * xhat, axis=-1, keepdims=True)
    return (grown - jnp.mean(grown, axis=-1, keepdims=True) - xhat * along) * inverse


def gelu_parts(h):
    square = h * h
    half = 0.5 + 0.5 * jnp.tanh(h * (0.7978845608 + (0.7978845608 * 0.044715) * square))
    acted = h * half
    slope = 2 * 0.7978845608 + (6 * 0.7978845608 * 0.044715) * square
    return acted, half + acted * (1.0 - half) * slope


def add_into(held, index, others):
    total = held[index].astype(F32)
    for other in others:
        total = total + other.astype(F32)
    held[index] = total.astype(held.dtype)


class Scatter:
    def __init__(self, wires, place, grads, mode, held, hop, hopz):
        self.w, self.p, self.grads, self.held = wires, place, grads, held
        self.mode, self.hops, self.hopz = mode, hop, hopz
        self.group = held.shape[1]
        self.unit = self.group // place.deep
        n = place.side
        self.line = [*range(1, n), 0]
        self.order = [(d, e) for d in self.line for e in self.line]
        self.out, self.deep = wires.sem(), wires.sem()
        if mode == "axes":
            self.crossed = {step: wires.sem() for step in self.order}
            self.first = [wires.sem() for _ in range(n)]
            self.second = wires.sem()
        else:
            self.cross, self.level = wires.sem(), wires.sem()
        sent = (2 * n * n - 1) * self.group + (0 if hopz is None else self.group - self.unit)
        wires.unsent.append((grads.at[pl.ds(0, sent)], self.out))

    def at(self, turn, d, e):
        y, x = self.p.spot(turn, d, e)
        return y * self.p.side + x

    def hop(self, d, e):
        return self.hops.at[self.order.index((d, e))]

    def rows_of(self, j, core):
        return pl.ds(pl.multiple_of((2 * j + core) * self.group, self.group), self.group)

    def unit_rows(self, d):
        p = self.p
        return pl.ds(pl.multiple_of(lax.rem(p.z + d, p.deep) * self.unit, self.unit), self.unit)

    def owner(self, d, e):
        p = self.p
        return p.seq(*p.spot(p.c, d, e), p.c), p.z

    def send(self, src, dst, device, came):
        self.w.copy(src, dst, device, self.out, came)

    def cross_over(self, d, e):
        p = self.p
        j = self.at(1 - p.c, d, e)
        came = self.crossed[d, e] if self.mode == "axes" else self.cross
        self.send(self.grads.at[self.rows_of(j, 1 - p.c)], self.held.at[j], p.sibling(), came)

    def fold(self, d, e):
        p = self.p
        j = self.at(p.c, d, e)
        if self.mode == "axes":
            wait_bytes(self.held.at[j], self.crossed[d, e])
        add_into(self.held, j, [self.grads[self.rows_of(j, p.c)]])
        if self.mode == "axes" and d:
            self.send(self.held.at[j], self.hop(d, e), p.peers(0)[d - 1], self.first[e])
        if self.mode == "direct" and (d or e):
            self.send(self.held.at[j], self.hop(d, e), self.owner(d, e), self.level)

    def turn(self, e):
        p, n = self.p, self.p.side
        j = self.at(p.c, 0, e)
        wait_bytes(self.held.at[pl.ds(0, n - 1)], self.first[e])
        add_into(self.held, j, [self.hop(d, e)[...] for d in range(1, n)])
        if e:
            self.send(self.held.at[j], self.hop(0, e), p.peers(1)[e - 1], self.second)

    def step0(self):
        for d, e in self.order:
            self.cross_over(d, e)

    def step1(self):
        if self.mode != "axes":
            wait_bytes(self.held, self.cross)
        for d, e in self.order:
            self.fold(d, e)

    def step2(self):
        for e in self.line if self.mode == "axes" else ():
            self.turn(e)

    def step3(self):
        p = self.p
        self.mine = self.at(p.c, 0, 0)
        if self.mode == "direct":
            wait_bytes(self.hops, self.level)
            add_into(self.held, self.mine, [self.hop(d, e)[...] for d, e in p.steps()])
        else:
            wait_bytes(self.held.at[pl.ds(0, p.side - 1)], self.second)
            add_into(self.held, self.mine, [self.hop(0, e)[...] for e in range(1, p.side)])
        if self.hopz is not None:
            for d, other in enumerate(p.peers("z"), 1):
                self.send(self.held.at[self.mine, self.unit_rows(d)], self.hopz.at[d - 1], other, self.deep)

    def step4(self):
        if self.hopz is None:
            return self.held[self.mine].astype(F32)
        total = self.held[self.mine, self.unit_rows(0)].astype(F32)
        wait_bytes(self.hopz, self.deep)
        for d in range(self.p.deep - 1):
            total = total + self.hopz[d].astype(F32)
        return total


def scatter_scratch(side, deep, unit, tail, with_z):
    group = deep * unit
    shapes = [(side * side, group), (side * side - 1, group)]
    if with_z:
        shapes.append((deep - 1, unit))
    return [pltpu.VMEM((*shape, *tail), BF16) for shape in shapes]


class Total:
    def __init__(self, wires, place, sums, came):
        self.w, self.p, self.sums, self.came = wires, place, sums, came
        self.out, self.slot = wires.sem(), 0
        wires.unsent.append((came, self.out))

    def send(self, level):
        p = self.p
        peers = [[p.sibling()], p.plane(), p.peers("z")][level]
        self.sem, self.first, self.count = self.w.sem(), self.slot, len(peers)
        for peer in peers:
            self.w.copy(self.sums.at[level], self.came.at[self.slot], peer, self.out, self.sem)
            self.slot += 1

    def take(self, level):
        wait_bytes(self.came.at[pl.ds(self.first, self.count)], self.sem)
        total = self.sums[level]
        for i in range(self.count):
            total = total + self.came[self.first + i]
        self.sums[level + 1] = total


def layer_kernel(
    with_z, grad_scale,
    x_hbm, cot_hbm, wqkv_ref, wo_ref, wu_ref, wd_ref, gain1_ref, shift1_ref, gain2_ref, shift2_ref, span_doc_ref,
    act2_ref, dtok_ref, dwqkv_ref, dwo_ref, dwu_ref, dwd_ref, total_ref,
    x_ref, cot_ref, small_ref, docs_ref, own_q, own_k, own_v,
    q_mat, k_mat, v_mat, out_mat, up_mat, down_mat, gains_ref, small_all, own_sums, sums_all, sums_ref, sums_t_ref,
    act_ref, qkv_ref, probs_ref, attn_t_ref, resid_ref, acted_ref, dhid_ref, dattn_ref,
    gdown_ref, gup_ref, gout_ref, gq_ref, gk_ref, gv_ref, dkv_ref, stats_ref, delta_ref, dsum_ref, levels_ref, came_ref,
    sems, place_sem, *held,
):
    place = Place()
    wires = Wires(sems)
    tok = x_ref.shape[0]
    spans = tok // S
    tiles = tok // TILE
    first = place.me * spans
    held = list(held)
    local = [pltpu.make_async_copy(x_hbm, x_ref, place_sem.at[0]), pltpu.make_async_copy(cot_hbm, cot_ref, place_sem.at[1])]
    for move in local:
        move.start()

    def gather(shard, full, direct):
        return Gather(wires, place, shard, full, shard.shape[0], with_z, direct)

    def scatter(grads, z, mode):
        parts = [held.pop(0) for _ in range(3 if z else 2)]
        return Scatter(wires, place, grads, mode, *parts, *([] if z else [None]))

    small = Gather(wires, place, small_ref, small_all, 1, True, True)
    sums = Gather(wires, place, own_sums, sums_all, 1, True, True)
    g_k, g_v, g_q = gather(own_k, k_mat, True), gather(own_v, v_mat, True), gather(own_q, q_mat, True)
    g_out, g_down, g_up = gather(wo_ref, out_mat, False), gather(wd_ref, down_mat, False), gather(wu_ref, up_mat, False)
    s_sum = scatter(sums_all, True, "direct")
    s_down, s_up, s_out = [scatter(g, with_z, "axes") for g in (gdown_ref, gup_ref, gout_ref)]
    s_q, s_k, s_v = [scatter(g, with_z, "direct") for g in (gq_ref, gk_ref, gv_ref)]

    width = gain1_ref.shape[1]
    small_ref[...] = jnp.zeros_like(small_ref)
    for k, ref in enumerate((gain1_ref, shift1_ref, gain2_ref, shift2_ref)):
        small_ref[0, k : k + 1, :width] = ref[...].astype(F32)
    split_heads(wqkv_ref[...], (own_q, own_k, own_v))
    place.greet()
    for g in (small, g_k, g_v, g_q, g_down, g_out):
        g.step0()
    small.step1()
    g_k.step1()
    g_v.step1()
    small.step3()
    g_k.step3()
    g_q.step1()
    docs_ref[...] = window_docs(first, spans, span_doc_ref)
    small.step4()
    gains_ref[...] = spread_small(small_all[...], place.devices)
    local[0].wait()

    def norm(i):
        rows = tile_rows(i, S)
        xhat, _ = normed_parts(x_ref[rows, :].astype(F32))
        act_ref[rows, :] = (xhat * gains_ref[0:1, :] + gains_ref[1:2, :]).astype(BF16)

    loop(0, spans, norm)
    g_v.step3()
    g_k.step4()

    def project(mat, part):
        block = nn(act_ref[...], mat[...]).astype(BF16)
        qkv_ref[:, part * D : (part + 1) * D] = block
        if part:
            mean = jnp.sum(block.astype(F32).reshape(spans, S, D), axis=1) * (1.0 / S)
            own_sums[0, :, (part - 1) * D : part * D] = mean.astype(BF16)

    project(k_mat, 1)
    g_q.step3()
    g_down.step1()
    g_out.step1()
    g_v.step4()
    project(v_mat, 2)
    sums.step0()
    g_up.step0()
    g_q.step4()
    project(q_mat, 0)
    half = spans // 2
    loop(0, half, lambda i: span_scores(i, qkv_ref, dkv_ref, stats_ref))
    sums.step1()
    loop(half, spans, lambda i: span_scores(i, qkv_ref, dkv_ref, stats_ref))
    sums.step3()
    g_out.step2()
    sums.step4()
    for i in range(PSPANS // MOST):
        two = sums_all[pl.ds(2 * i, 2)].astype(F32)
        sums_ref[MOST * i : MOST * (i + 1), :] = two.reshape(MOST, 2 * D).astype(BF16)
    before = sums_all[pl.ds(lax.rem(place.me + place.devices - 2, place.devices), 1)].astype(F32)
    last = sums_all[pl.ds(lax.rem(place.me + place.devices - 1, place.devices), 1)].astype(F32)
    here = sums_all[pl.ds(place.me, 1)].astype(F32)
    nothing = jnp.zeros_like(here)
    sums_ref[PSPANS : PSPANS + MOST, :] = jnp.concatenate([before, last], axis=0).reshape(MOST, 2 * D).astype(BF16)
    sums_ref[PSPANS + MOST :, :] = jnp.concatenate([here, nothing], axis=0).reshape(MOST, 2 * D).astype(BF16)
    sums_t_ref[...] = sums_ref[...].T

    def attend(span):
        attend_span(span, first, qkv_ref, sums_ref, sums_t_ref, docs_ref, dkv_ref, stats_ref, attn_t_ref, probs_ref)

    quarter = spans // 4
    g_up.step1()
    loop(0, quarter, attend)
    g_down.step2()
    loop(quarter, 3 * quarter, attend)
    g_out.step3()
    loop(3 * quarter, spans, attend)
    g_out.step4()

    def residual(i):
        rows = tile_rows(i, TILE)
        resid = x_ref[rows, :].astype(F32) + tn(attn_t_ref[:, rows], out_mat[...])
        resid_ref[rows, :] = resid
        xhat, _ = normed_parts(resid)
        act2_ref[rows, :] = (xhat * gains_ref[2:3, :] + gains_ref[3:4, :]).astype(BF16)

    loop(0, tiles, residual)
    local[1].wait()
    g_up.step2()

    def feed(i):
        part = tile_rows(i, CHUNK)
        acted, slope = gelu_parts(nt(act2_ref[...], up_mat[part, :]))
        acted = acted.astype(BF16)
        acted_ref[:, part] = acted
        dhid = (nt(cot_ref[...], down_mat[part, :]) * slope).astype(BF16)
        dhid_ref[:, part] = dhid
        gdown_ref[part, :] = tn(acted, cot_ref[...]).astype(BF16)
        gup_ref[part, :] = tn(dhid, act2_ref[...]).astype(BF16)

    both = (s_down, s_up)
    blocks = [(d, e) for e in range(place.side) for d in range(place.side)]
    waiting = []
    if s_up.group == CHUNK:
        for d, e in blocks:
            if (d, e) == (0, 1):
                g_down.step3()
                g_up.step3()
            g_down.ready(d, e)
            g_up.ready(d, e)
            theirs = 2 * s_up.at(1 - place.c, d, e) + 1 - place.c
            ours = 2 * s_up.at(place.c, d, e) + place.c
            loop(0, 2, lambda i: feed(theirs + i * (ours - theirs)))
            for s in both:
                s.cross_over(d, e)
            waiting.append((d, e))
            if len(waiting) > 1:
                fold_all(both, *waiting.pop(0))
    else:
        for g in (g_down, g_up):
            g.step3()
            g.step4()
        loop(0, up_mat.shape[0] // CHUNK, feed)
        for s in both:
            s.step0()
        waiting = list(s_up.order)
    levels_ref[...] = jnp.zeros_like(levels_ref)

    def finish(i):
        rows = tile_rows(i, TILE)
        dnormed = nn(dhid_ref[rows, :], up_mat[...])
        xhat, inverse = normed_parts(resid_ref[rows, :])
        levels_ref[0, 2:3, :] += jnp.sum(dnormed * xhat, axis=0, keepdims=True)
        levels_ref[0, 3:4, :] += jnp.sum(dnormed, axis=0, keepdims=True)
        dresid = cot_ref[rows, :].astype(F32) + norm_back(dnormed, xhat, inverse, gains_ref[2:3, :])
        dtok_ref[rows, :] = dresid
        branch = dresid.astype(BF16)
        act2_ref[rows, :] = branch
        dattn_ref[rows, :] = nt(branch, out_mat[...]).astype(BF16)

    loop(0, tiles // 2, finish)
    for d, e in waiting:
        fold_all(both, d, e)
    loop(tiles // 2, tiles, finish)
    gout_ref[...] = nn(attn_t_ref[...], act2_ref[...]).astype(BF16)
    s_out.step0()
    dsum_ref[...] = jnp.zeros_like(dsum_ref)

    def back_far(span):
        summary_back(span, qkv_ref, sums_ref, probs_ref, attn_t_ref, dattn_ref, delta_ref, dsum_ref)

    def back_near(span):
        span_back(span, qkv_ref, sums_t_ref, probs_ref, dattn_ref, delta_ref, dhid_ref, dkv_ref)

    loop(0, quarter, back_far)
    s_out.step1()
    loop(quarter, 2 * quarter, back_far)
    for e in s_up.line:
        for s in both:
            s.turn(e)
    loop(2 * quarter, spans, back_far)
    sums.settle()
    sums_all[...] = jnp.zeros_like(sums_all)
    for i in range(3):
        block = lax.rem(place.me + place.devices - 2 + i, place.devices)
        rows = slice(PSPANS + i * spans, PSPANS + (i + 1) * spans)
        sums_all[pl.ds(block, 1)] = dsum_ref[rows, :].astype(BF16)[None]
    for i in range(PSPANS // spans):
        sums_all[i] = dsum_ref[i * spans : (i + 1) * spans, :].astype(BF16)
    s_sum.step0()
    loop(0, quarter, back_near)
    s_sum.step1()
    s_out.step2()
    loop(quarter, 3 * quarter, back_near)
    s_sum.step3()
    for s in both:
        s.step3()
    s_out.step3()
    loop(3 * quarter, spans, back_near)
    gq_ref[...] = tn(act_ref[...], dhid_ref[:, :D]).astype(BF16)
    s_q.step0()
    shares = s_sum.step4()[0] * (1.0 / S)
    for part, g_ref, s in ((0, gk_ref, s_k), (1, gv_ref, s_v)):
        cols = slice(part * D, (part + 1) * D)
        for span in range(spans):
            rows = slice(span * S, (span + 1) * S)
            dhid_ref[rows, (part + 1) * D : (part + 2) * D] = (dkv_ref[rows, cols] + shares[span : span + 1, cols]).astype(BF16)
        g_ref[...] = tn(act_ref[...], dhid_ref[:, (part + 1) * D : (part + 2) * D]).astype(BF16)
        s.step0()

    def finish_tokens(i):
        rows = slice(i * TILE, (i + 1) * TILE)
        dnormed = nt(dhid_ref[rows, :D], q_mat[...]) + nt(dhid_ref[rows, D : 2 * D], k_mat[...])
        dnormed = dnormed + nt(dhid_ref[rows, 2 * D : 3 * D], v_mat[...])
        xhat, inverse = normed_parts(x_ref[rows, :].astype(F32))
        levels_ref[0, 0:1, :] += jnp.sum(dnormed * xhat, axis=0, keepdims=True)
        levels_ref[0, 1:2, :] += jnp.sum(dnormed, axis=0, keepdims=True)
        dtok_ref[rows, :] += norm_back(dnormed, xhat, inverse, gains_ref[0:1, :])

    def output(i):
        rows = slice(i * TILE, (i + 1) * TILE)
        act2_ref[rows, :] = (resid_ref[rows, :] + nn(acted_ref[rows, :], down_mat[...])).astype(BF16)

    total = Total(wires, place, levels_ref, came_ref)
    finish_tokens(0)
    s_q.step1()
    s_k.step1()
    finish_tokens(1)
    s_v.step1()
    finish_tokens(2)
    finish_tokens(3)
    total.send(0)
    output(0)
    total.take(0)
    total.send(1)
    s_q.step3()
    output(1)
    s_k.step3()
    output(2)
    total.take(1)
    total.send(2)
    s_v.step3()
    output(3)
    dwd_ref[...] = s_down.step4() * grad_scale
    dwu_ref[...] = s_up.step4() * grad_scale
    dwo_ref[...] = s_out.step4() * grad_scale
    join_heads((s_q.step4() * grad_scale, s_k.step4() * grad_scale, s_v.step4() * grad_scale), dwqkv_ref)
    total.take(2)
    start = place.me * width
    lanes = pl.ds(pl.multiple_of(start // LANES * LANES, LANES), LANES)
    total_ref[...] = pltpu.roll(levels_ref[3, :, lanes] * grad_scale, lax.rem(LANES - lax.rem(start, LANES), LANES), 1)
    wires.finish()


def fold_all(scatters, d, e):
    for s in scatters:
        s.fold(d, e)


def layer(with_z, grad_scale, x, cotangent, wqkv, wo, wu, wd, vectors, span_doc):
    tok = x.shape[0]
    spans = tok // S
    deep = lax.axis_size("head")
    side = math.isqrt(lax.axis_size("seq") // 2)
    devices = 2 * side * side * deep
    owned = devices if with_z else devices // deep
    hidden_size = wu.shape[0] * owned
    whole, anywhere = pl.BlockSpec(memory_space=VMEM), pl.BlockSpec(memory_space=pl.ANY)
    shape = jax.ShapeDtypeStruct
    peers = 1 + side * side - 1 + deep - 1
    held = scatter_scratch(side, deep, 1, (spans, 2 * D), True)
    for total in (hidden_size, hidden_size, D, D, D, D):
        held += scatter_scratch(side, deep, total // devices, (D,), with_z)
    return pl.pallas_call(
        functools.partial(layer_kernel, with_z, grad_scale),
        out_shape=(
            pltpu.VMEM((tok, D), BF16),
            pltpu.VMEM((tok, D), F32),
            pltpu.VMEM((D // owned, 3 * D), F32),
            pltpu.VMEM((D // owned, D), F32),
            pltpu.VMEM((hidden_size // owned, D), F32),
            pltpu.VMEM((hidden_size // owned, D), F32),
            pltpu.VMEM((8, LANES), F32),
        ),
        in_specs=[anywhere] * 2 + [whole] * 8 + [pl.BlockSpec(memory_space=pltpu.MemorySpace.SMEM)],
        out_specs=(whole,) * 7,
        scratch_shapes=[
            pltpu.VMEM((tok, D), BF16),
            pltpu.VMEM((tok, D), BF16),
            pltpu.VMEM((1, 8, LANES), F32),
            pltpu.VMEM((WIN, S), jnp.int32),
            pltpu.VMEM((D // owned, D), BF16),
            pltpu.VMEM((D // owned, D), BF16),
            pltpu.VMEM((D // owned, D), BF16),
            pltpu.VMEM((D, D), BF16),
            pltpu.VMEM((D, D), BF16),
            pltpu.VMEM((D, D), BF16),
            pltpu.VMEM((D, D), BF16),
            pltpu.VMEM((hidden_size, D), BF16),
            pltpu.VMEM((hidden_size, D), BF16),
            pltpu.VMEM((8, D), F32),
            pltpu.VMEM((devices, 8, LANES), F32),
            pltpu.VMEM((1, spans, 2 * D), BF16),
            pltpu.VMEM((devices, spans, 2 * D), BF16),
            pltpu.VMEM((FAR, 2 * D), BF16),
            pltpu.VMEM((2 * D, FAR), BF16),
            pltpu.VMEM((tok, D), BF16),
            pltpu.VMEM((tok, 3 * D), BF16),
            pltpu.VMEM((spans * PAIRS, KEYS, 2 * S), BF16),
            pltpu.VMEM((D, tok), BF16),
            pltpu.VMEM((tok, D), F32),
            pltpu.VMEM((tok, hidden_size), BF16),
            pltpu.VMEM((tok, hidden_size), BF16),
            pltpu.VMEM((tok, D), BF16),
            pltpu.VMEM((hidden_size, D), BF16),
            pltpu.VMEM((hidden_size, D), BF16),
            pltpu.VMEM((D, D), BF16),
            pltpu.VMEM((D, D), BF16),
            pltpu.VMEM((D, D), BF16),
            pltpu.VMEM((D, D), BF16),
            pltpu.VMEM((tok, 2 * D), F32),
            pltpu.VMEM((2, spans * PAIRS, 2 * S), F32),
            pltpu.VMEM((spans * PAIRS, 2 * S), F32),
            pltpu.VMEM((FAR, 2 * D), F32),
            pltpu.VMEM((4, 8, D), F32),
            pltpu.VMEM((peers, 8, D), F32),
            pltpu.SemaphoreType.DMA((semaphores(side),)),
            pltpu.SemaphoreType.DMA((2,)),
            *held,
        ],
        compiler_params=pltpu.CompilerParams(vmem_limit_bytes=VMEM_LIMIT - 7 * tok * D, collective_id=0, has_side_effects=True),
        name="mega_layer",
    )(x, cotangent, wqkv, wo, wu, wd, *vectors, span_doc)


def deliver_kernel(*refs):
    count = (len(refs) - 1) // 2
    sems = refs[-1]
    moves = [pltpu.make_async_copy(refs[i], refs[count + i], sems.at[i]) for i in range(count)]
    for move in moves:
        move.start()
    for move in moves:
        move.wait()


def deliver(arrays):
    anywhere = pl.BlockSpec(memory_space=pl.ANY)
    return pl.pallas_call(
        deliver_kernel,
        out_shape=[jax.ShapeDtypeStruct(a.shape, a.dtype) for a in arrays],
        in_specs=[anywhere] * len(arrays),
        out_specs=[anywhere] * len(arrays),
        scratch_shapes=[pltpu.SemaphoreType.DMA((len(arrays),))],
        compiler_params=pltpu.CompilerParams(vmem_limit_bytes=2**20),
        name="deliver",
    )(*arrays)


def shards(tokens, cotangent, w_qkv, w_out, w_up, w_down, gain_one, shift_one, gain_two, shift_two, span_doc):
    tok = tokens.shape[0]
    devices = lax.axis_size("seq") * lax.axis_size("head")
    grad_scale = 1.0 / math.sqrt(tok * devices)
    with_z = w_qkv.shape[0] % 16 == 0
    weights = (w_qkv, w_out, w_up.T, w_down)
    if not with_z:
        weights = tuple(lax.all_gather(w, "head", axis=0, tiled=True) for w in weights)
    vectors = [v[None] for v in (gain_one, shift_one, gain_two, shift_two)]
    width = gain_one.shape[0]
    out_tokens, d_tokens, d_qkv, d_out, d_up, d_down, total = deliver(
        layer(with_z, grad_scale, tokens, cotangent, *weights, vectors, span_doc)
    )
    if not with_z:
        d_qkv, d_out, d_up, d_down = (
            lax.psum_scatter(g, "head", scatter_dimension=0, tiled=True) for g in (d_qkv, d_out, d_up, d_down)
        )
    return out_tokens, d_tokens, d_qkv, d_out, d_up.T, d_down, *(total[k, :width] for k in range(4))


def solution(mesh):
    rows, cols, vec = P(BOTH, None), P(None, BOTH), P(BOTH)
    in_specs = (rows, rows, rows, rows, cols, rows, vec, vec, vec, vec, P())
    out_specs = (rows, rows, rows, rows, cols, rows, vec, vec, vec, vec)
    return jax.shard_map(shards, mesh=mesh, in_specs=in_specs, out_specs=out_specs, check_vma=False)
```

```python
import functools
import math

import jax
import jax.numpy as jnp
from jax import lax
from jax.experimental import pallas as pl
from jax.experimental.pallas import tpu as pltpu
from jax.sharding import PartitionSpec as P

H = 8
HD = 64
D = H * HD
S = 128
MOST = 16
PSPANS = 128
WIN = 2 * MOST
PAIRS = H // 2
LANES = 2 * HD
FAR = PSPANS + WIN
KEYS = S + FAR
EPS = 1e-05
MASKED = -1e30
F32 = jnp.float32
BF16 = jnp.bfloat16
VMEM = pltpu.MemorySpace.VMEM
VMEM_LIMIT = 67043328
TILE = 256
TOGETHER = 2
CHUNK = 256


def nn(a, b):
    return lax.dot_general(a, b, (((1,), (0,)), ((), ())), preferred_element_type=F32)


def nt(a, b):
    return lax.dot_general(a, b, (((1,), (1,)), ((), ())), preferred_element_type=F32)


def tn(a, b):
    return lax.dot_general(a, b, (((0,), (0,)), ((), ())), preferred_element_type=F32)


def loop(start, stop, body, unroll=1):
    def step(i, carry):
        body(i)
        return carry

    lax.fori_loop(start, stop, step, 0, unroll=unroll)


def tile_rows(i, size):
    return pl.ds(pl.multiple_of(i * size, size), size)


def summary_bias(first, span, docs_ref):
    index = first + span
    row = lax.broadcasted_iota(jnp.int32, (PSPANS, S), 0)
    prompt = jnp.where(row < index, 0.0, MASKED)
    wrow = first - MOST + lax.broadcasted_iota(jnp.int32, (WIN, S), 0)
    same = docs_ref[...] == docs_ref[pl.ds(span + MOST, 1), :]
    window = jnp.where(same & (wrow >= PSPANS) & (wrow < index), 0.0, MASKED)
    return jnp.concatenate([prompt, window], axis=0).astype(F32)


def window_docs(first, spans, span_doc_ref):
    row = lax.broadcasted_iota(jnp.int32, (WIN, S), 0)
    docs = jnp.full((WIN, S), -1, jnp.int32)
    for i in range(MOST + spans):
        at = first - MOST - PSPANS + i
        docs = jnp.where((row == i) & (at >= 0), span_doc_ref[jnp.maximum(at, 0)], docs)
    return docs


def head_masks(scale):
    lane = lax.broadcasted_iota(jnp.int32, (1, LANES), 1)
    first = jnp.where(lane < HD, scale, 0.0).astype(BF16)
    second = jnp.where(lane < HD, 0.0, scale).astype(BF16)
    return first, second


def stack_heads(block, masks):
    return jnp.concatenate([block * masks[0], block * masks[1]], axis=0)


def pair_cols(part, pair):
    return slice(part * D + pair * LANES, part * D + (pair + 1) * LANES)


def unstack(pair_t):
    return jnp.concatenate([pair_t[:HD, :S], pair_t[HD:, S:]], axis=0)


def both_heads(pair):
    return slice(pair * 2 * S, (pair + 1) * 2 * S)


def span_scores(span, qkv_ref, grown_ref, stats_ref):
    rows = tile_rows(span, S)
    key_row = lax.broadcasted_iota(jnp.int32, (S, S), 0)
    query = lax.broadcasted_iota(jnp.int32, (S, S), 1)
    causal = jnp.where(key_row <= query, 0.0, MASKED).astype(F32)
    causal = jnp.concatenate([causal, causal], axis=1)
    masks = head_masks(1.0 / math.sqrt(HD))
    for pair in range(PAIRS):
        queries = stack_heads(qkv_ref[rows, pair_cols(0, pair)], masks)
        scores = nt(qkv_ref[rows, pair_cols(1, pair)], queries) + causal
        top = jnp.max(scores, axis=0, keepdims=True)
        grown = jnp.exp(scores - top)
        grown_ref[rows, both_heads(pair)] = grown
        stats_ref[0, pl.ds(span * PAIRS + pair, 1), :] = top
        stats_ref[1, pl.ds(span * PAIRS + pair, 1), :] = jnp.sum(grown, axis=0, keepdims=True)


def attend_span(span, first, qkv_ref, sums_ref, sums_t_ref, docs_ref, grown_ref, stats_ref, attn_t_ref, probs_ref):
    rows = tile_rows(span, S)
    bias = summary_bias(first, span, docs_ref)
    bias = jnp.concatenate([bias, bias], axis=1)
    masks = head_masks(1.0 / math.sqrt(HD))
    for pair in range(PAIRS):
        queries = stack_heads(qkv_ref[rows, pair_cols(0, pair)], masks)
        own_top = stats_ref[0, pl.ds(span * PAIRS + pair, 1), :]
        own_sum = stats_ref[1, pl.ds(span * PAIRS + pair, 1), :]
        far = nt(sums_ref[:, pair_cols(0, pair)], queries) + bias
        top = jnp.maximum(own_top, jnp.max(far, axis=0, keepdims=True))
        far = jnp.exp(far - top)
        fade = jnp.exp(own_top - top)
        share = 1.0 / (own_sum * fade + jnp.sum(far, axis=0, keepdims=True))
        own = grown_ref[rows, both_heads(pair)] * (fade * share)
        probs = jnp.concatenate([own.astype(BF16), (far * share).astype(BF16)], axis=0)
        probs_ref[span * PAIRS + pair] = probs
        vals_t = jnp.concatenate([qkv_ref[rows, pair_cols(2, pair)].T, sums_t_ref[pair_cols(1, pair), :]], axis=1)
        attn_t_ref[pair * LANES : (pair + 1) * LANES, rows] = unstack(nn(vals_t, probs)).astype(BF16)


def summary_back(span, qkv_ref, sums_ref, probs_ref, attn_t_ref, dattn_ref, delta_ref, dsum_ref):
    rows = tile_rows(span, S)
    masks = head_masks(1.0 / math.sqrt(HD))
    ones = head_masks(1.0)
    for pair in range(PAIRS):
        cols, vcols = pair_cols(0, pair), pair_cols(1, pair)
        block = dattn_ref[rows, cols]
        each = block.T.astype(F32) * attn_t_ref[pair * LANES : (pair + 1) * LANES, rows].astype(F32)
        delta = jnp.concatenate(
            [jnp.sum(each[:HD], axis=0, keepdims=True), jnp.sum(each[HD:], axis=0, keepdims=True)], axis=1
        )
        delta_ref[pl.ds(span * PAIRS + pair, 1), :] = delta
        queries = stack_heads(qkv_ref[rows, cols], masks)
        grads = stack_heads(block, ones)
        probs = probs_ref[span * PAIRS + pair, S:, :]
        dprobs = nt(sums_ref[:, vcols], grads)
        dscores = (probs.astype(F32) * (dprobs - delta)).astype(BF16)
        dsum_ref[:, cols] += nn(dscores, queries)
        dsum_ref[:, vcols] += nn(probs, grads)
        probs_ref[span * PAIRS + pair, S:, :] = dscores


def span_back(span, qkv_ref, sums_t_ref, probs_ref, dattn_ref, delta_ref, dqkv_ref, dkv_ref):
    rows = tile_rows(span, S)
    scale = 1.0 / math.sqrt(HD)
    masks = head_masks(scale)
    ones = head_masks(1.0)
    for pair in range(PAIRS):
        cols, vcols = pair_cols(0, pair), pair_cols(1, pair)
        queries = stack_heads(qkv_ref[rows, cols], masks)
        grads = stack_heads(dattn_ref[rows, cols], ones)
        probs = probs_ref[span * PAIRS + pair, :S, :]
        dprobs = nt(qkv_ref[rows, pair_cols(2, pair)], grads)
        delta = delta_ref[pl.ds(span * PAIRS + pair, 1), :]
        dscores = (probs.astype(F32) * (dprobs - delta)).astype(BF16)
        dkv_ref[rows, cols] = nn(dscores, queries)
        dkv_ref[rows, vcols] = nn(probs, grads)
        every = jnp.concatenate([dscores, probs_ref[span * PAIRS + pair, S:, :]], axis=0)
        keys_t = jnp.concatenate([qkv_ref[rows, pair_cols(1, pair)].T, sums_t_ref[cols, :]], axis=1)
        dq_t = unstack(nn(keys_t, every)) * scale
        dqkv_ref[rows, cols] = dq_t.T.astype(BF16)


def split_heads(block, parts):
    low = lax.broadcasted_iota(jnp.int32, (1, LANES), 1) < HD
    for pair in range(PAIRS):
        one, two, three = [block[:, (3 * pair + i) * LANES : (3 * pair + i + 1) * LANES].astype(F32) for i in range(3)]
        mixed = jnp.where(low, one, two), pltpu.roll(jnp.where(low, three, one), HD, 1), jnp.where(low, two, three)
        for part, value in zip(parts, mixed):
            part[:, pair * LANES : (pair + 1) * LANES] = value.astype(part.dtype)


def join_heads(parts, out_ref):
    low = lax.broadcasted_iota(jnp.int32, (1, LANES), 1) < HD
    for pair in range(PAIRS):
        q, k, v = [part[:, pair * LANES : (pair + 1) * LANES] for part in parts]
        k = pltpu.roll(k, HD, 1)
        for i, value in enumerate((jnp.where(low, q, k), jnp.where(low, v, q), jnp.where(low, k, v))):
            out_ref[:, (3 * pair + i) * LANES : (3 * pair + i + 1) * LANES] = value


MESH = pl.DeviceIdType.MESH
BOTH = ("seq", "head")


class Place:
    def __init__(self):
        seq, self.z = lax.axis_index("seq"), lax.axis_index("head")
        self.side = math.isqrt(lax.axis_size("seq") // 2)
        self.deep = lax.axis_size("head")
        self.devices = lax.axis_size("seq") * self.deep
        self.c = lax.rem(seq, 2)
        self.x = lax.rem(seq // 2, self.side)
        self.y = seq // 2 // self.side
        self.me = seq * self.deep + self.z

    def seq(self, y, x, c):
        return (y * self.side + x) * 2 + c

    def along(self, axis, step):
        n, turn = self.side, self.c if axis == 0 else 1 - self.c
        return lax.rem(self.y + turn * step, n), lax.rem(self.x + (1 - turn) * step, n)

    def sibling(self):
        return (self.seq(self.y, self.x, 1 - self.c), self.z)

    def peers(self, axis):
        if axis == "z":
            seq = self.seq(self.y, self.x, self.c)
            return [(seq, lax.rem(self.z + d, self.deep)) for d in range(1, self.deep)]
        return [(self.seq(*self.along(axis, d), self.c), self.z) for d in range(1, self.side)]

    def spot(self, turn, d, e):
        n = self.side
        return lax.rem(self.y + turn * d + (1 - turn) * e, n), lax.rem(self.x + turn * e + (1 - turn) * d, n)

    def steps(self):
        line = [*range(1, self.side), 0]
        return [(d, e) for d in line for e in line][:-1]

    def plane(self):
        return [(self.seq(*self.spot(self.c, d, e), self.c), self.z) for d, e in self.steps()]

    def greet(self):
        barrier = pltpu.get_barrier_semaphore()
        others = [self.sibling(), *self.plane(), *self.peers("z")]
        for other in others:
            pl.semaphore_signal(barrier, inc=1, device_id=other, device_id_type=MESH)
        pl.semaphore_wait(barrier, len(others))


def wait_bytes(ref, sem):
    pltpu.make_async_copy(ref, ref, sem).wait()


class Wires:
    def __init__(self, sems):
        self.sems, self.used, self.unsent = sems, 0, []

    def sem(self):
        self.used += 1
        return self.sems.at[self.used - 1]

    def copy(self, src, dst, device, sent, came):
        pltpu.make_async_remote_copy(
            src_ref=src, dst_ref=dst, send_sem=sent, recv_sem=came, device_id=device, device_id_type=MESH
        ).start()

    def finish(self):
        for ref, sem in self.unsent:
            wait_bytes(ref, sem)


def semaphores(side):
    return 5 * 5 + 3 * 8 + 3 * (side * side + side + 3) + 4 * 4 + 4


class Gather:
    def __init__(self, wires, place, shard, full, rows, with_z, direct):
        self.w, self.p, self.full, self.shard = wires, place, full, shard
        self.rows, self.with_z, self.direct = rows, with_z, direct
        self.group = rows * place.deep if with_z else rows
        self.out, self.local, self.deep = wires.sem(), wires.sem(), wires.sem()
        self.level, self.cross = wires.sem(), wires.sem()
        if not direct:
            self.column, self.cross_row, self.cross_rest = wires.sem(), wires.sem(), wires.sem()
        sent = (2 * place.side**2 - 1) * self.group + (place.deep - 1 if with_z else 0) * rows
        self.unsent = (full.at[pl.ds(0, sent)], self.out)
        wires.unsent.append(self.unsent)
        self.done = set()

    def block(self, y, x):
        start = self.p.seq(y, x, self.p.c) * self.group
        return self.full.at[pl.ds(pl.multiple_of(start, self.group), self.group)]

    def _send(self, place, device, came):
        self.w.copy(self.block(*place), self.block(*place), device, self.out, came)

    def _wait(self, groups, sem):
        wait_bytes(self.full.at[pl.ds(0, groups * self.group)], sem)

    def step0(self):
        p = self.p
        start = pl.multiple_of(p.me * self.rows, self.rows) if self.with_z else p.seq(p.y, p.x, p.c) * self.rows
        own = self.full.at[pl.ds(start, self.rows)]
        for device in p.peers("z") if self.with_z else ():
            self.w.copy(self.shard, own, device, self.out, self.deep)
        self.placed = pltpu.make_async_copy(self.shard, own, self.local)
        self.placed.start()

    def step1(self):
        p = self.p
        if self.with_z:
            wait_bytes(self.full.at[pl.ds(0, (p.deep - 1) * self.rows)], self.deep)
        self.placed.wait()
        own = (p.y, p.x)
        if self.direct:
            for device in p.plane():
                self._send(own, device, self.level)
        else:
            for device in p.peers(0):
                self._send(own, device, self.level)
            for device in p.peers(1):
                self._send(own, device, self.column)
        self._send(own, p.sibling(), self.cross)

    def step2(self):
        p, n = self.p, self.p.side
        self._wait(n - 1, self.level)
        for d in range(1, n):
            place = p.spot(p.c, d, 0)
            for device in p.peers(1):
                self._send(place, device, self.column)
            self._send(place, p.sibling(), self.cross_row)

    def step3(self):
        p, n = self.p, self.p.side
        if self.direct:
            self._wait(n * n - 1, self.level)
            for d, e in p.steps():
                self._send(p.spot(p.c, d, e), p.sibling(), self.cross)
        else:
            self._wait(n * (n - 1), self.column)
            for e in range(1, n):
                for d in range(n):
                    self._send(p.spot(p.c, d, e), p.sibling(), self.cross_rest)

    def ready(self, d, e):
        n = self.p.side
        sems = (1, self.cross), (n - 1, self.cross_row), (n * (n - 1), self.cross_rest)
        which = 2 if e else 1 if d else 0
        if which not in self.done:
            self.done.add(which)
            self._wait(*sems[which])

    def step4(self):
        n = self.p.side
        if self.direct:
            self._wait(n * n, self.cross)
            return
        for d, e in [(0, 0), *self.p.steps()]:
            self.ready(d, e)

    def settle(self):
        wait_bytes(*self.unsent)
        self.w.unsent = [pair for pair in self.w.unsent if pair is not self.unsent]


def spread_small(gathered, devices):
    width = D // devices
    table = gathered.reshape(devices * 8, LANES).astype(BF16)
    pick = lax.broadcasted_iota(jnp.int32, (LANES, D), 0) == lax.broadcasted_iota(jnp.int32, (LANES, D), 1) % width
    every = nn(table, jnp.where(pick, 1.0, 0.0).astype(BF16))
    owner = lax.broadcasted_iota(jnp.int32, (devices * 8, D), 0) // 8
    column = lax.broadcasted_iota(jnp.int32, (devices * 8, D), 1) // width
    return jnp.sum(jnp.where(owner == column, every, 0.0).reshape(devices, 8, D), axis=0)


def normed_parts(values):
    mean = jnp.mean(values, axis=-1, keepdims=True)
    centred = values - mean
    inverse = lax.rsqrt(jnp.mean(centred * centred, axis=-1, keepdims=True) + EPS)
    return centred * inverse, inverse


def norm_back(dnormed, xhat, inverse, gain):
    grown = dnormed * gain
    along = jnp.mean(grown * xhat, axis=-1, keepdims=True)
    return (grown - jnp.mean(grown, axis=-1, keepdims=True) - xhat * along) * inverse


def gelu_parts(h):
    square = h * h
    half = 0.5 + 0.5 * jnp.tanh(h * (0.7978845608 + (0.7978845608 * 0.044715) * square))
    acted = h * half
    slope = 2 * 0.7978845608 + (6 * 0.7978845608 * 0.044715) * square
    return acted, half + acted * (1.0 - half) * slope


def add_into(held, index, others):
    total = held[index].astype(F32)
    for other in others:
        total = total + other.astype(F32)
    held[index] = total.astype(held.dtype)


class Scatter:
    def __init__(self, wires, place, grads, mode, held, hop, hopz):
        self.w, self.p, self.grads, self.held = wires, place, grads, held
        self.mode, self.hops, self.hopz = mode, hop, hopz
        self.group = held.shape[1]
        self.unit = self.group // place.deep
        n = place.side
        self.line = [*range(1, n), 0]
        self.order = [(d, e) for d in self.line for e in self.line]
        self.out, self.deep = wires.sem(), wires.sem()
        if mode == "axes":
            self.crossed = {step: wires.sem() for step in self.order}
            self.first = [wires.sem() for _ in range(n)]
            self.second = wires.sem()
        else:
            self.cross, self.level = wires.sem(), wires.sem()
        sent = (2 * n * n - 1) * self.group + (0 if hopz is None else self.group - self.unit)
        wires.unsent.append((grads.at[pl.ds(0, sent)], self.out))

    def at(self, turn, d, e):
        y, x = self.p.spot(turn, d, e)
        return y * self.p.side + x

    def hop(self, d, e):
        return self.hops.at[self.order.index((d, e))]

    def rows_of(self, j, core):
        return pl.ds(pl.multiple_of((2 * j + core) * self.group, self.group), self.group)

    def unit_rows(self, d):
        p = self.p
        return pl.ds(pl.multiple_of(lax.rem(p.z + d, p.deep) * self.unit, self.unit), self.unit)

    def owner(self, d, e):
        p = self.p
        return p.seq(*p.spot(p.c, d, e), p.c), p.z

    def send(self, src, dst, device, came):
        self.w.copy(src, dst, device, self.out, came)

    def cross_over(self, d, e):
        p = self.p
        j = self.at(1 - p.c, d, e)
        came = self.crossed[d, e] if self.mode == "axes" else self.cross
        self.send(self.grads.at[self.rows_of(j, 1 - p.c)], self.held.at[j], p.sibling(), came)

    def fold(self, d, e):
        p = self.p
        j = self.at(p.c, d, e)
        if self.mode == "axes":
            wait_bytes(self.held.at[j], self.crossed[d, e])
        add_into(self.held, j, [self.grads[self.rows_of(j, p.c)]])
        if self.mode == "axes" and d:
            self.send(self.held.at[j], self.hop(d, e), p.peers(0)[d - 1], self.first[e])
        if self.mode == "direct" and (d or e):
            self.send(self.held.at[j], self.hop(d, e), self.owner(d, e), self.level)

    def turn(self, e):
        p, n = self.p, self.p.side
        j = self.at(p.c, 0, e)
        wait_bytes(self.held.at[pl.ds(0, n - 1)], self.first[e])
        add_into(self.held, j, [self.hop(d, e)[...] for d in range(1, n)])
        if e:
            self.send(self.held.at[j], self.hop(0, e), p.peers(1)[e - 1], self.second)

    def step0(self):
        for d, e in self.order:
            self.cross_over(d, e)

    def step1(self):
        if self.mode != "axes":
            wait_bytes(self.held, self.cross)
        for d, e in self.order:
            self.fold(d, e)

    def step2(self):
        for e in self.line if self.mode == "axes" else ():
            self.turn(e)

    def step3(self):
        p = self.p
        self.mine = self.at(p.c, 0, 0)
        if self.mode == "direct":
            wait_bytes(self.hops, self.level)
            add_into(self.held, self.mine, [self.hop(d, e)[...] for d, e in p.steps()])
        else:
            wait_bytes(self.held.at[pl.ds(0, p.side - 1)], self.second)
            add_into(self.held, self.mine, [self.hop(0, e)[...] for e in range(1, p.side)])
        if self.hopz is not None:
            for d, other in enumerate(p.peers("z"), 1):
                self.send(self.held.at[self.mine, self.unit_rows(d)], self.hopz.at[d - 1], other, self.deep)

    def step4(self):
        if self.hopz is None:
            return self.held[self.mine].astype(F32)
        total = self.held[self.mine, self.unit_rows(0)].astype(F32)
        wait_bytes(self.hopz, self.deep)
        for d in range(self.p.deep - 1):
            total = total + self.hopz[d].astype(F32)
        return total


def scatter_scratch(side, deep, unit, tail, with_z):
    group = deep * unit
    shapes = [(side * side, group), (side * side - 1, group)]
    if with_z:
        shapes.append((deep - 1, unit))
    return [pltpu.VMEM((*shape, *tail), BF16) for shape in shapes]


class Total:
    def __init__(self, wires, place, sums, came):
        self.w, self.p, self.sums, self.came = wires, place, sums, came
        self.out, self.slot = wires.sem(), 0
        wires.unsent.append((came, self.out))

    def send(self, level):
        p = self.p
        peers = [[p.sibling()], p.plane(), p.peers("z")][level]
        self.sem, self.first, self.count = self.w.sem(), self.slot, len(peers)
        for peer in peers:
            self.w.copy(self.sums.at[level], self.came.at[self.slot], peer, self.out, self.sem)
            self.slot += 1

    def take(self, level):
        wait_bytes(self.came.at[pl.ds(self.first, self.count)], self.sem)
        total = self.sums[level]
        for i in range(self.count):
            total = total + self.came[self.first + i]
        self.sums[level + 1] = total


def layer_kernel(
    with_z, grad_scale,
    x_hbm, cot_hbm, wqkv_ref, wo_ref, wu_ref, wd_ref, gain1_ref, shift1_ref, gain2_ref, shift2_ref, span_doc_ref,
    act2_ref, dtok_ref, dwqkv_ref, dwo_ref, dwu_ref, dwd_ref, total_ref,
    x_ref, cot_ref, small_ref, docs_ref, own_q, own_k, own_v,
    q_mat, k_mat, v_mat, out_mat, up_mat, down_mat, gains_ref, small_all, own_sums, sums_all, sums_ref, sums_t_ref,
    act_ref, qkv_ref, probs_ref, attn_t_ref, resid_ref, acted_ref, dhid_ref, dattn_ref,
    gdown_ref, gup_ref, gout_ref, gq_ref, gk_ref, gv_ref, dkv_ref, stats_ref, delta_ref, dsum_ref, levels_ref, came_ref,
    sems, place_sem, *held,
):
    place = Place()
    wires = Wires(sems)
    tok = x_ref.shape[0]
    spans = tok // S
    tiles = tok // TILE
    first = place.me * spans
    held = list(held)
    local = [pltpu.make_async_copy(x_hbm, x_ref, place_sem.at[0]), pltpu.make_async_copy(cot_hbm, cot_ref, place_sem.at[1])]
    for move in local:
        move.start()

    def gather(shard, full, direct):
        return Gather(wires, place, shard, full, shard.shape[0], with_z, direct)

    def scatter(grads, z, mode):
        parts = [held.pop(0) for _ in range(3 if z else 2)]
        return Scatter(wires, place, grads, mode, *parts, *([] if z else [None]))

    small = Gather(wires, place, small_ref, small_all, 1, True, True)
    sums = Gather(wires, place, own_sums, sums_all, 1, True, True)
    g_k, g_v, g_q = gather(own_k, k_mat, True), gather(own_v, v_mat, True), gather(own_q, q_mat, True)
    g_out, g_down, g_up = gather(wo_ref, out_mat, False), gather(wd_ref, down_mat, False), gather(wu_ref, up_mat, False)
    s_sum = scatter(sums_all, True, "direct")
    s_down, s_up, s_out = [scatter(g, with_z, "axes") for g in (gdown_ref, gup_ref, gout_ref)]
    s_q, s_k, s_v = [scatter(g, with_z, "direct") for g in (gq_ref, gk_ref, gv_ref)]

    width = gain1_ref.shape[1]
    small_ref[...] = jnp.zeros_like(small_ref)
    for k, ref in enumerate((gain1_ref, shift1_ref, gain2_ref, shift2_ref)):
        small_ref[0, k : k + 1, :width] = ref[...].astype(F32)
    split_heads(wqkv_ref[...], (own_q, own_k, own_v))
    place.greet()
    for g in (small, g_k, g_v, g_q, g_down, g_out):
        g.step0()
    small.step1()
    g_k.step1()
    g_v.step1()
    small.step3()
    g_k.step3()
    g_q.step1()
    docs_ref[...] = window_docs(first, spans, span_doc_ref)
    small.step4()
    gains_ref[...] = spread_small(small_all[...], place.devices)
    local[0].wait()

    def norm(i):
        rows = tile_rows(i, S)
        xhat, _ = normed_parts(x_ref[rows, :].astype(F32))
        act_ref[rows, :] = (xhat * gains_ref[0:1, :] + gains_ref[1:2, :]).astype(BF16)

    loop(0, spans, norm, 4)
    g_v.step3()
    g_k.step4()

    def project(mat, part):
        block = nn(act_ref[...], mat[...]).astype(BF16)
        qkv_ref[:, part * D : (part + 1) * D] = block
        if part:
            mean = jnp.sum(block.astype(F32).reshape(spans, S, D), axis=1) * (1.0 / S)
            own_sums[0, :, (part - 1) * D : part * D] = mean.astype(BF16)

    project(k_mat, 1)
    g_q.step3()
    g_down.step1()
    g_out.step1()
    g_v.step4()
    project(v_mat, 2)
    sums.step0()
    g_up.step0()
    g_q.step4()
    project(q_mat, 0)
    half = spans // 2
    loop(0, half, lambda i: span_scores(i, qkv_ref, dkv_ref, stats_ref), TOGETHER)
    sums.step1()
    loop(half, spans, lambda i: span_scores(i, qkv_ref, dkv_ref, stats_ref), TOGETHER)
    sums.step3()
    g_out.step2()
    sums.step4()
    for i in range(PSPANS // MOST):
        two = sums_all[pl.ds(2 * i, 2)].astype(F32)
        sums_ref[MOST * i : MOST * (i + 1), :] = two.reshape(MOST, 2 * D).astype(BF16)
    before = sums_all[pl.ds(lax.rem(place.me + place.devices - 2, place.devices), 1)].astype(F32)
    last = sums_all[pl.ds(lax.rem(place.me + place.devices - 1, place.devices), 1)].astype(F32)
    here = sums_all[pl.ds(place.me, 1)].astype(F32)
    nothing = jnp.zeros_like(here)
    sums_ref[PSPANS : PSPANS + MOST, :] = jnp.concatenate([before, last], axis=0).reshape(MOST, 2 * D).astype(BF16)
    sums_ref[PSPANS + MOST :, :] = jnp.concatenate([here, nothing], axis=0).reshape(MOST, 2 * D).astype(BF16)
    sums_t_ref[...] = sums_ref[...].T

    def attend(span):
        attend_span(span, first, qkv_ref, sums_ref, sums_t_ref, docs_ref, dkv_ref, stats_ref, attn_t_ref, probs_ref)

    quarter = spans // 4
    g_up.step1()
    loop(0, quarter, attend, TOGETHER)
    g_down.step2()
    loop(quarter, 3 * quarter, attend, TOGETHER)
    g_out.step3()
    loop(3 * quarter, spans, attend, TOGETHER)
    g_out.step4()

    def residual(i):
        rows = tile_rows(i, TILE)
        resid = x_ref[rows, :].astype(F32) + tn(attn_t_ref[:, rows], out_mat[...])
        resid_ref[rows, :] = resid
        xhat, _ = normed_parts(resid)
        act2_ref[rows, :] = (xhat * gains_ref[2:3, :] + gains_ref[3:4, :]).astype(BF16)

    loop(0, tiles, residual, 2)
    local[1].wait()
    g_up.step2()

    def feed(i):
        part = tile_rows(i, CHUNK)
        acted, slope = gelu_parts(nt(act2_ref[...], up_mat[part, :]))
        acted = acted.astype(BF16)
        acted_ref[:, part] = acted
        dhid = (nt(cot_ref[...], down_mat[part, :]) * slope).astype(BF16)
        dhid_ref[:, part] = dhid
        gdown_ref[part, :] = tn(acted, cot_ref[...]).astype(BF16)
        gup_ref[part, :] = tn(dhid, act2_ref[...]).astype(BF16)

    both = (s_down, s_up)
    blocks = [(d, e) for e in range(place.side) for d in range(place.side)]
    waiting = []
    if s_up.group == CHUNK:
        for d, e in blocks:
            if (d, e) == (0, 1):
                g_down.step3()
                g_up.step3()
            g_down.ready(d, e)
            g_up.ready(d, e)
            theirs = 2 * s_up.at(1 - place.c, d, e) + 1 - place.c
            ours = 2 * s_up.at(place.c, d, e) + place.c
            loop(0, 2, lambda i: feed(theirs + i * (ours - theirs)), 2)
            for s in both:
                s.cross_over(d, e)
            waiting.append((d, e))
            if len(waiting) > 1:
                fold_all(both, *waiting.pop(0))
    else:
        for g in (g_down, g_up):
            g.step3()
            g.step4()
        loop(0, up_mat.shape[0] // CHUNK, feed)
        for s in both:
            s.step0()
        waiting = list(s_up.order)
    levels_ref[...] = jnp.zeros_like(levels_ref)

    def finish(i):
        rows = tile_rows(i, TILE)
        dnormed = nn(dhid_ref[rows, :], up_mat[...])
        xhat, inverse = normed_parts(resid_ref[rows, :])
        levels_ref[0, 2:3, :] += jnp.sum(dnormed * xhat, axis=0, keepdims=True)
        levels_ref[0, 3:4, :] += jnp.sum(dnormed, axis=0, keepdims=True)
        dresid = cot_ref[rows, :].astype(F32) + norm_back(dnormed, xhat, inverse, gains_ref[2:3, :])
        dtok_ref[rows, :] = dresid
        branch = dresid.astype(BF16)
        act2_ref[rows, :] = branch
        dattn_ref[rows, :] = nt(branch, out_mat[...]).astype(BF16)

    loop(0, tiles // 2, finish, 2)
    for d, e in waiting:
        fold_all(both, d, e)
    loop(tiles // 2, tiles, finish, 2)
    gout_ref[...] = nn(attn_t_ref[...], act2_ref[...]).astype(BF16)
    s_out.step0()
    dsum_ref[...] = jnp.zeros_like(dsum_ref)

    def back_far(span):
        summary_back(span, qkv_ref, sums_ref, probs_ref, attn_t_ref, dattn_ref, delta_ref, dsum_ref)

    def back_near(span):
        span_back(span, qkv_ref, sums_t_ref, probs_ref, dattn_ref, delta_ref, dhid_ref, dkv_ref)

    loop(0, quarter, back_far, TOGETHER)
    s_out.step1()
    loop(quarter, 2 * quarter, back_far, TOGETHER)
    for e in s_up.line:
        for s in both:
            s.turn(e)
    loop(2 * quarter, spans, back_far, TOGETHER)
    sums.settle()
    sums_all[...] = jnp.zeros_like(sums_all)
    for i in range(3):
        block = lax.rem(place.me + place.devices - 2 + i, place.devices)
        rows = slice(PSPANS + i * spans, PSPANS + (i + 1) * spans)
        sums_all[pl.ds(block, 1)] = dsum_ref[rows, :].astype(BF16)[None]
    for i in range(PSPANS // spans):
        sums_all[i] = dsum_ref[i * spans : (i + 1) * spans, :].astype(BF16)
    s_sum.step0()
    loop(0, quarter, back_near, TOGETHER)
    s_sum.step1()
    s_out.step2()
    loop(quarter, 3 * quarter, back_near, TOGETHER)
    s_sum.step3()
    for s in both:
        s.step3()
    s_out.step3()
    loop(3 * quarter, spans, back_near, TOGETHER)
    gq_ref[...] = tn(act_ref[...], dhid_ref[:, :D]).astype(BF16)
    s_q.step0()
    shares = s_sum.step4()[0] * (1.0 / S)
    for part, g_ref, s in ((0, gk_ref, s_k), (1, gv_ref, s_v)):
        cols = slice(part * D, (part + 1) * D)
        for span in range(spans):
            rows = slice(span * S, (span + 1) * S)
            dhid_ref[rows, (part + 1) * D : (part + 2) * D] = (dkv_ref[rows, cols] + shares[span : span + 1, cols]).astype(BF16)
        g_ref[...] = tn(act_ref[...], dhid_ref[:, (part + 1) * D : (part + 2) * D]).astype(BF16)
        s.step0()

    def finish_tokens(i):
        rows = slice(i * TILE, (i + 1) * TILE)
        dnormed = nt(dhid_ref[rows, :D], q_mat[...]) + nt(dhid_ref[rows, D : 2 * D], k_mat[...])
        dnormed = dnormed + nt(dhid_ref[rows, 2 * D : 3 * D], v_mat[...])
        xhat, inverse = normed_parts(x_ref[rows, :].astype(F32))
        levels_ref[0, 0:1, :] += jnp.sum(dnormed * xhat, axis=0, keepdims=True)
        levels_ref[0, 1:2, :] += jnp.sum(dnormed, axis=0, keepdims=True)
        dtok_ref[rows, :] += norm_back(dnormed, xhat, inverse, gains_ref[0:1, :])

    def output(i):
        rows = slice(i * TILE, (i + 1) * TILE)
        act2_ref[rows, :] = (resid_ref[rows, :] + nn(acted_ref[rows, :], down_mat[...])).astype(BF16)

    total = Total(wires, place, levels_ref, came_ref)
    finish_tokens(0)
    s_q.step1()
    s_k.step1()
    finish_tokens(1)
    s_v.step1()
    finish_tokens(2)
    finish_tokens(3)
    total.send(0)
    output(0)
    total.take(0)
    total.send(1)
    s_q.step3()
    output(1)
    s_k.step3()
    output(2)
    s_v.step3()
    total.take(1)
    total.send(2)
    output(3)
    dwd_ref[...] = s_down.step4() * grad_scale
    dwu_ref[...] = s_up.step4() * grad_scale
    dwo_ref[...] = s_out.step4() * grad_scale
    join_heads((s_q.step4() * grad_scale, s_k.step4() * grad_scale, s_v.step4() * grad_scale), dwqkv_ref)
    total.take(2)
    start = place.me * width
    lanes = pl.ds(pl.multiple_of(start // LANES * LANES, LANES), LANES)
    total_ref[...] = pltpu.roll(levels_ref[3, :, lanes] * grad_scale, lax.rem(LANES - lax.rem(start, LANES), LANES), 1)
    wires.finish()


def fold_all(scatters, d, e):
    for s in scatters:
        s.fold(d, e)


def layer(with_z, grad_scale, x, cotangent, wqkv, wo, wu, wd, vectors, span_doc):
    tok = x.shape[0]
    spans = tok // S
    deep = lax.axis_size("head")
    side = math.isqrt(lax.axis_size("seq") // 2)
    devices = 2 * side * side * deep
    owned = devices if with_z else devices // deep
    hidden_size = wu.shape[0] * owned
    whole, anywhere = pl.BlockSpec(memory_space=VMEM), pl.BlockSpec(memory_space=pl.ANY)
    shape = jax.ShapeDtypeStruct
    peers = 1 + side * side - 1 + deep - 1
    held = scatter_scratch(side, deep, 1, (spans, 2 * D), True)
    for total in (hidden_size, hidden_size, D, D, D, D):
        held += scatter_scratch(side, deep, total // devices, (D,), with_z)
    return pl.pallas_call(
        functools.partial(layer_kernel, with_z, grad_scale),
        out_shape=(
            pltpu.VMEM((tok, D), BF16),
            pltpu.VMEM((tok, D), F32),
            pltpu.VMEM((D // owned, 3 * D), F32),
            pltpu.VMEM((D // owned, D), F32),
            pltpu.VMEM((hidden_size // owned, D), F32),
            pltpu.VMEM((hidden_size // owned, D), F32),
            pltpu.VMEM((8, LANES), F32),
        ),
        in_specs=[anywhere] * 2 + [whole] * 8 + [pl.BlockSpec(memory_space=pltpu.MemorySpace.SMEM)],
        out_specs=(whole,) * 7,
        scratch_shapes=[
            pltpu.VMEM((tok, D), BF16),
            pltpu.VMEM((tok, D), BF16),
            pltpu.VMEM((1, 8, LANES), F32),
            pltpu.VMEM((WIN, S), jnp.int32),
            pltpu.VMEM((D // owned, D), BF16),
            pltpu.VMEM((D // owned, D), BF16),
            pltpu.VMEM((D // owned, D), BF16),
            pltpu.VMEM((D, D), BF16),
            pltpu.VMEM((D, D), BF16),
            pltpu.VMEM((D, D), BF16),
            pltpu.VMEM((D, D), BF16),
            pltpu.VMEM((hidden_size, D), BF16),
            pltpu.VMEM((hidden_size, D), BF16),
            pltpu.VMEM((8, D), F32),
            pltpu.VMEM((devices, 8, LANES), F32),
            pltpu.VMEM((1, spans, 2 * D), BF16),
            pltpu.VMEM((devices, spans, 2 * D), BF16),
            pltpu.VMEM((FAR, 2 * D), BF16),
            pltpu.VMEM((2 * D, FAR), BF16),
            pltpu.VMEM((tok, D), BF16),
            pltpu.VMEM((tok, 3 * D), BF16),
            pltpu.VMEM((spans * PAIRS, KEYS, 2 * S), BF16),
            pltpu.VMEM((D, tok), BF16),
            pltpu.VMEM((tok, D), F32),
            pltpu.VMEM((tok, hidden_size), BF16),
            pltpu.VMEM((tok, hidden_size), BF16),
            pltpu.VMEM((tok, D), BF16),
            pltpu.VMEM((hidden_size, D), BF16),
            pltpu.VMEM((hidden_size, D), BF16),
            pltpu.VMEM((D, D), BF16),
            pltpu.VMEM((D, D), BF16),
            pltpu.VMEM((D, D), BF16),
            pltpu.VMEM((D, D), BF16),
            pltpu.VMEM((tok, 2 * D), F32),
            pltpu.VMEM((2, spans * PAIRS, 2 * S), F32),
            pltpu.VMEM((spans * PAIRS, 2 * S), F32),
            pltpu.VMEM((FAR, 2 * D), F32),
            pltpu.VMEM((4, 8, D), F32),
            pltpu.VMEM((peers, 8, D), F32),
            pltpu.SemaphoreType.DMA((semaphores(side),)),
            pltpu.SemaphoreType.DMA((2,)),
            *held,
        ],
        compiler_params=pltpu.CompilerParams(vmem_limit_bytes=VMEM_LIMIT - 7 * tok * D, collective_id=0, has_side_effects=True),
        name="mega_layer",
    )(x, cotangent, wqkv, wo, wu, wd, *vectors, span_doc)


def deliver_kernel(*refs):
    count = (len(refs) - 1) // 2
    sems = refs[-1]
    moves = [pltpu.make_async_copy(refs[i], refs[count + i], sems.at[i]) for i in range(count)]
    for move in moves:
        move.start()
    for move in moves:
        move.wait()


def deliver(arrays):
    anywhere = pl.BlockSpec(memory_space=pl.ANY)
    return pl.pallas_call(
        deliver_kernel,
        out_shape=[jax.ShapeDtypeStruct(a.shape, a.dtype) for a in arrays],
        in_specs=[anywhere] * len(arrays),
        out_specs=[anywhere] * len(arrays),
        scratch_shapes=[pltpu.SemaphoreType.DMA((len(arrays),))],
        compiler_params=pltpu.CompilerParams(vmem_limit_bytes=2**20),
        name="deliver",
    )(*arrays)


def shards(tokens, cotangent, w_qkv, w_out, w_up, w_down, gain_one, shift_one, gain_two, shift_two, span_doc):
    tok = tokens.shape[0]
    devices = lax.axis_size("seq") * lax.axis_size("head")
    grad_scale = 1.0 / math.sqrt(tok * devices)
    with_z = w_qkv.shape[0] % 16 == 0
    weights = (w_qkv, w_out, w_up.T, w_down)
    if not with_z:
        weights = tuple(lax.all_gather(w, "head", axis=0, tiled=True) for w in weights)
    vectors = [v[None] for v in (gain_one, shift_one, gain_two, shift_two)]
    width = gain_one.shape[0]
    out_tokens, d_tokens, d_qkv, d_out, d_up, d_down, total = deliver(
        layer(with_z, grad_scale, tokens, cotangent, *weights, vectors, span_doc)
    )
    if not with_z:
        d_qkv, d_out, d_up, d_down = (
            lax.psum_scatter(g, "head", scatter_dimension=0, tiled=True) for g in (d_qkv, d_out, d_up, d_down)
        )
    return out_tokens, d_tokens, d_qkv, d_out, d_up.T, d_down, *(total[k, :width] for k in range(4))


def solution(mesh):
    rows, cols, vec = P(BOTH, None), P(None, BOTH), P(BOTH)
    in_specs = (rows, rows, rows, rows, cols, rows, vec, vec, vec, vec, P())
    out_specs = (rows, rows, rows, rows, cols, rows, vec, vec, vec, vec)
    return jax.shard_map(shards, mesh=mesh, in_specs=in_specs, out_specs=out_specs, check_vma=False)
```

```python
import functools
import math

import jax
import jax.numpy as jnp
from jax import lax
from jax.experimental import pallas as pl
from jax.experimental.pallas import tpu as pltpu
from jax.sharding import PartitionSpec as P

H = 8
HD = 64
D = H * HD
S = 128
MOST = 16
PSPANS = 128
WIN = 2 * MOST
PAIRS = H // 2
LANES = 2 * HD
FAR = PSPANS + WIN
KEYS = S + FAR
EPS = 1e-05
MASKED = -1e30
F32 = jnp.float32
BF16 = jnp.bfloat16
VMEM = pltpu.MemorySpace.VMEM
VMEM_LIMIT = 67043328
TILE = 256
TOGETHER = 2
CHUNK = 256


def nn(a, b):
    return lax.dot_general(a, b, (((1,), (0,)), ((), ())), preferred_element_type=F32)


def nt(a, b):
    return lax.dot_general(a, b, (((1,), (1,)), ((), ())), preferred_element_type=F32)


def tn(a, b):
    return lax.dot_general(a, b, (((0,), (0,)), ((), ())), preferred_element_type=F32)


def loop(start, stop, body, unroll=1):
    def step(i, carry):
        body(i)
        return carry

    lax.fori_loop(start, stop, step, 0, unroll=unroll)


def tile_rows(i, size):
    return pl.ds(pl.multiple_of(i * size, size), size)


def summary_bias(first, span, docs_ref):
    index = first + span
    row = lax.broadcasted_iota(jnp.int32, (PSPANS, S), 0)
    prompt = jnp.where(row < index, 0.0, MASKED)
    wrow = first - MOST + lax.broadcasted_iota(jnp.int32, (WIN, S), 0)
    same = docs_ref[...] == docs_ref[pl.ds(span + MOST, 1), :]
    window = jnp.where(same & (wrow >= PSPANS) & (wrow < index), 0.0, MASKED)
    return jnp.concatenate([prompt, window], axis=0).astype(F32)


def window_docs(first, spans, span_doc_ref):
    row = lax.broadcasted_iota(jnp.int32, (WIN, S), 0)
    docs = jnp.full((WIN, S), -1, jnp.int32)
    for i in range(MOST + spans):
        at = first - MOST - PSPANS + i
        docs = jnp.where((row == i) & (at >= 0), span_doc_ref[jnp.maximum(at, 0)], docs)
    return docs


def head_masks(scale):
    lane = lax.broadcasted_iota(jnp.int32, (1, LANES), 1)
    first = jnp.where(lane < HD, scale, 0.0).astype(BF16)
    second = jnp.where(lane < HD, 0.0, scale).astype(BF16)
    return first, second


def stack_heads(block, masks):
    return jnp.concatenate([block * masks[0], block * masks[1]], axis=0)


def pair_cols(part, pair):
    return slice(part * D + pair * LANES, part * D + (pair + 1) * LANES)


def unstack(pair_t):
    return jnp.concatenate([pair_t[:HD, :S], pair_t[HD:, S:]], axis=0)


def both_heads(pair):
    return slice(pair * 2 * S, (pair + 1) * 2 * S)


def span_scores(span, qkv_ref, grown_ref, stats_ref):
    rows = tile_rows(span, S)
    key_row = lax.broadcasted_iota(jnp.int32, (S, S), 0)
    query = lax.broadcasted_iota(jnp.int32, (S, S), 1)
    causal = jnp.where(key_row <= query, 0.0, MASKED).astype(F32)
    causal = jnp.concatenate([causal, causal], axis=1)
    masks = head_masks(1.0 / math.sqrt(HD))
    for pair in range(PAIRS):
        queries = stack_heads(qkv_ref[rows, pair_cols(0, pair)], masks)
        scores = nt(qkv_ref[rows, pair_cols(1, pair)], queries) + causal
        top = jnp.max(scores, axis=0, keepdims=True)
        grown = jnp.exp(scores - top)
        grown_ref[rows, both_heads(pair)] = grown
        stats_ref[0, pl.ds(span * PAIRS + pair, 1), :] = top
        stats_ref[1, pl.ds(span * PAIRS + pair, 1), :] = jnp.sum(grown, axis=0, keepdims=True)


def attend_span(span, first, qkv_ref, sums_ref, sums_t_ref, docs_ref, grown_ref, stats_ref, attn_t_ref, probs_ref):
    rows = tile_rows(span, S)
    bias = summary_bias(first, span, docs_ref)
    bias = jnp.concatenate([bias, bias], axis=1)
    masks = head_masks(1.0 / math.sqrt(HD))
    for pair in range(PAIRS):
        queries = stack_heads(qkv_ref[rows, pair_cols(0, pair)], masks)
        own_top = stats_ref[0, pl.ds(span * PAIRS + pair, 1), :]
        own_sum = stats_ref[1, pl.ds(span * PAIRS + pair, 1), :]
        far = nt(sums_ref[:, pair_cols(0, pair)], queries) + bias
        top = jnp.maximum(own_top, jnp.max(far, axis=0, keepdims=True))
        far = jnp.exp(far - top)
        fade = jnp.exp(own_top - top)
        share = 1.0 / (own_sum * fade + jnp.sum(far, axis=0, keepdims=True))
        own = grown_ref[rows, both_heads(pair)] * (fade * share)
        probs = jnp.concatenate([own.astype(BF16), (far * share).astype(BF16)], axis=0)
        probs_ref[span * PAIRS + pair] = probs
        vals_t = jnp.concatenate([qkv_ref[rows, pair_cols(2, pair)].T, sums_t_ref[pair_cols(1, pair), :]], axis=1)
        attn_t_ref[pair * LANES : (pair + 1) * LANES, rows] = unstack(nn(vals_t, probs)).astype(BF16)


def summary_back(span, qkv_ref, sums_ref, probs_ref, attn_t_ref, dattn_ref, delta_ref, dsum_ref):
    rows = tile_rows(span, S)
    masks = head_masks(1.0 / math.sqrt(HD))
    ones = head_masks(1.0)
    for pair in range(PAIRS):
        cols, vcols = pair_cols(0, pair), pair_cols(1, pair)
        block = dattn_ref[rows, cols]
        each = block.T.astype(F32) * attn_t_ref[pair * LANES : (pair + 1) * LANES, rows].astype(F32)
        delta = jnp.concatenate(
            [jnp.sum(each[:HD], axis=0, keepdims=True), jnp.sum(each[HD:], axis=0, keepdims=True)], axis=1
        )
        delta_ref[pl.ds(span * PAIRS + pair, 1), :] = delta
        queries = stack_heads(qkv_ref[rows, cols], masks)
        grads = stack_heads(block, ones)
        probs = probs_ref[span * PAIRS + pair, S:, :]
        dprobs = nt(sums_ref[:, vcols], grads)
        dscores = (probs.astype(F32) * (dprobs - delta)).astype(BF16)
        dsum_ref[:, cols] += nn(dscores, queries)
        dsum_ref[:, vcols] += nn(probs, grads)
        probs_ref[span * PAIRS + pair, S:, :] = dscores


def span_back(span, qkv_ref, sums_t_ref, probs_ref, dattn_ref, delta_ref, dqkv_ref, dkv_ref):
    rows = tile_rows(span, S)
    scale = 1.0 / math.sqrt(HD)
    masks = head_masks(scale)
    ones = head_masks(1.0)
    for pair in range(PAIRS):
        cols, vcols = pair_cols(0, pair), pair_cols(1, pair)
        queries = stack_heads(qkv_ref[rows, cols], masks)
        grads = stack_heads(dattn_ref[rows, cols], ones)
        probs = probs_ref[span * PAIRS + pair, :S, :]
        dprobs = nt(qkv_ref[rows, pair_cols(2, pair)], grads)
        delta = delta_ref[pl.ds(span * PAIRS + pair, 1), :]
        dscores = (probs.astype(F32) * (dprobs - delta)).astype(BF16)
        dkv_ref[rows, cols] = nn(dscores, queries)
        dkv_ref[rows, vcols] = nn(probs, grads)
        every = jnp.concatenate([dscores, probs_ref[span * PAIRS + pair, S:, :]], axis=0)
        keys_t = jnp.concatenate([qkv_ref[rows, pair_cols(1, pair)].T, sums_t_ref[cols, :]], axis=1)
        dq_t = unstack(nn(keys_t, every)) * scale
        dqkv_ref[rows, cols] = dq_t.T.astype(BF16)


def split_heads(block, parts):
    low = lax.broadcasted_iota(jnp.int32, (1, LANES), 1) < HD
    for pair in range(PAIRS):
        one, two, three = [block[:, (3 * pair + i) * LANES : (3 * pair + i + 1) * LANES].astype(F32) for i in range(3)]
        mixed = jnp.where(low, one, two), pltpu.roll(jnp.where(low, three, one), HD, 1), jnp.where(low, two, three)
        for part, value in zip(parts, mixed):
            part[:, pair * LANES : (pair + 1) * LANES] = value.astype(part.dtype)


def join_heads(parts, out_ref):
    low = lax.broadcasted_iota(jnp.int32, (1, LANES), 1) < HD
    for pair in range(PAIRS):
        q, k, v = [part[:, pair * LANES : (pair + 1) * LANES] for part in parts]
        k = pltpu.roll(k, HD, 1)
        for i, value in enumerate((jnp.where(low, q, k), jnp.where(low, v, q), jnp.where(low, k, v))):
            out_ref[:, (3 * pair + i) * LANES : (3 * pair + i + 1) * LANES] = value


MESH = pl.DeviceIdType.MESH
BOTH = ("seq", "head")


class Place:
    def __init__(self):
        seq, self.z = lax.axis_index("seq"), lax.axis_index("head")
        self.side = math.isqrt(lax.axis_size("seq") // 2)
        self.deep = lax.axis_size("head")
        self.devices = lax.axis_size("seq") * self.deep
        self.c = lax.rem(seq, 2)
        self.x = lax.rem(seq // 2, self.side)
        self.y = seq // 2 // self.side
        self.me = seq * self.deep + self.z

    def seq(self, y, x, c):
        return (y * self.side + x) * 2 + c

    def along(self, axis, step):
        n, turn = self.side, self.c if axis == 0 else 1 - self.c
        return lax.rem(self.y + turn * step, n), lax.rem(self.x + (1 - turn) * step, n)

    def sibling(self):
        return (self.seq(self.y, self.x, 1 - self.c), self.z)

    def peers(self, axis):
        if axis == "z":
            seq = self.seq(self.y, self.x, self.c)
            return [(seq, lax.rem(self.z + d, self.deep)) for d in range(1, self.deep)]
        return [(self.seq(*self.along(axis, d), self.c), self.z) for d in range(1, self.side)]

    def spot(self, turn, d, e):
        n = self.side
        return lax.rem(self.y + turn * d + (1 - turn) * e, n), lax.rem(self.x + turn * e + (1 - turn) * d, n)

    def steps(self):
        line = [*range(1, self.side), 0]
        return [(d, e) for d in line for e in line][:-1]

    def plane(self):
        return [(self.seq(*self.spot(self.c, d, e), self.c), self.z) for d, e in self.steps()]

    def greet(self):
        barrier = pltpu.get_barrier_semaphore()
        others = [self.sibling(), *self.plane(), *self.peers("z")]
        for other in others:
            pl.semaphore_signal(barrier, inc=1, device_id=other, device_id_type=MESH)
        pl.semaphore_wait(barrier, len(others))


def wait_bytes(ref, sem):
    pltpu.make_async_copy(ref, ref, sem).wait()


class Wires:
    def __init__(self, sems):
        self.sems, self.used, self.unsent = sems, 0, []

    def sem(self):
        self.used += 1
        return self.sems.at[self.used - 1]

    def copy(self, src, dst, device, sent, came):
        pltpu.make_async_remote_copy(
            src_ref=src, dst_ref=dst, send_sem=sent, recv_sem=came, device_id=device, device_id_type=MESH
        ).start()

    def finish(self):
        for ref, sem in self.unsent:
            wait_bytes(ref, sem)


def semaphores(side):
    return 5 * 5 + 3 * 8 + 3 * (side * side + side + 3) + 4 * 4 + 4


class Gather:
    def __init__(self, wires, place, shard, full, rows, with_z, direct):
        self.w, self.p, self.full, self.shard = wires, place, full, shard
        self.rows, self.with_z, self.direct = rows, with_z, direct
        self.group = rows * place.deep if with_z else rows
        self.out, self.local, self.deep = wires.sem(), wires.sem(), wires.sem()
        self.level, self.cross = wires.sem(), wires.sem()
        if not direct:
            self.column, self.cross_row, self.cross_rest = wires.sem(), wires.sem(), wires.sem()
        sent = (2 * place.side**2 - 1) * self.group + (place.deep - 1 if with_z else 0) * rows
        self.unsent = (full.at[pl.ds(0, sent)], self.out)
        wires.unsent.append(self.unsent)
        self.done = set()

    def block(self, y, x):
        start = self.p.seq(y, x, self.p.c) * self.group
        return self.full.at[pl.ds(pl.multiple_of(start, self.group), self.group)]

    def _send(self, place, device, came):
        self.w.copy(self.block(*place), self.block(*place), device, self.out, came)

    def _wait(self, groups, sem):
        wait_bytes(self.full.at[pl.ds(0, groups * self.group)], sem)

    def step0(self):
        p = self.p
        start = pl.multiple_of(p.me * self.rows, self.rows) if self.with_z else p.seq(p.y, p.x, p.c) * self.rows
        own = self.full.at[pl.ds(start, self.rows)]
        for device in p.peers("z") if self.with_z else ():
            self.w.copy(self.shard, own, device, self.out, self.deep)
        self.placed = pltpu.make_async_copy(self.shard, own, self.local)
        self.placed.start()

    def step1(self):
        p = self.p
        if self.with_z:
            wait_bytes(self.full.at[pl.ds(0, (p.deep - 1) * self.rows)], self.deep)
        self.placed.wait()
        own = (p.y, p.x)
        if self.direct:
            for device in p.plane():
                self._send(own, device, self.level)
        else:
            for device in p.peers(0):
                self._send(own, device, self.level)
            for device in p.peers(1):
                self._send(own, device, self.column)
        self._send(own, p.sibling(), self.cross)

    def step2(self):
        p, n = self.p, self.p.side
        self._wait(n - 1, self.level)
        for d in range(1, n):
            place = p.spot(p.c, d, 0)
            for device in p.peers(1):
                self._send(place, device, self.column)
            self._send(place, p.sibling(), self.cross_row)

    def step3(self):
        p, n = self.p, self.p.side
        if self.direct:
            self._wait(n * n - 1, self.level)
            for d, e in p.steps():
                self._send(p.spot(p.c, d, e), p.sibling(), self.cross)
        else:
            self._wait(n * (n - 1), self.column)
            for e in range(1, n):
                for d in range(n):
                    self._send(p.spot(p.c, d, e), p.sibling(), self.cross_rest)

    def ready(self, d, e):
        n = self.p.side
        sems = (1, self.cross), (n - 1, self.cross_row), (n * (n - 1), self.cross_rest)
        which = 2 if e else 1 if d else 0
        if which not in self.done:
            self.done.add(which)
            self._wait(*sems[which])

    def step4(self):
        n = self.p.side
        if self.direct:
            self._wait(n * n, self.cross)
            return
        for d, e in [(0, 0), *self.p.steps()]:
            self.ready(d, e)

    def settle(self):
        wait_bytes(*self.unsent)
        self.w.unsent = [pair for pair in self.w.unsent if pair is not self.unsent]


def spread_small(gathered, devices):
    width = D // devices
    table = gathered.reshape(devices * 8, LANES).astype(BF16)
    pick = lax.broadcasted_iota(jnp.int32, (LANES, D), 0) == lax.broadcasted_iota(jnp.int32, (LANES, D), 1) % width
    every = nn(table, jnp.where(pick, 1.0, 0.0).astype(BF16))
    owner = lax.broadcasted_iota(jnp.int32, (devices * 8, D), 0) // 8
    column = lax.broadcasted_iota(jnp.int32, (devices * 8, D), 1) // width
    return jnp.sum(jnp.where(owner == column, every, 0.0).reshape(devices, 8, D), axis=0)


def normed_parts(values):
    mean = jnp.mean(values, axis=-1, keepdims=True)
    centred = values - mean
    inverse = lax.rsqrt(jnp.mean(centred * centred, axis=-1, keepdims=True) + EPS)
    return centred * inverse, inverse


def norm_back(dnormed, xhat, inverse, gain):
    grown = dnormed * gain
    along = jnp.mean(grown * xhat, axis=-1, keepdims=True)
    return (grown - jnp.mean(grown, axis=-1, keepdims=True) - xhat * along) * inverse


def gelu_parts(h):
    square = h * h
    half = 0.5 + 0.5 * jnp.tanh(h * (0.7978845608 + (0.7978845608 * 0.044715) * square))
    acted = h * half
    slope = 2 * 0.7978845608 + (6 * 0.7978845608 * 0.044715) * square
    return acted, half + acted * (1.0 - half) * slope


def add_into(held, index, others):
    total = held[index].astype(F32)
    for other in others:
        total = total + other.astype(F32)
    held[index] = total.astype(held.dtype)


class Scatter:
    def __init__(self, wires, place, grads, mode, held, hop, hopz):
        self.w, self.p, self.grads, self.held = wires, place, grads, held
        self.mode, self.hops, self.hopz = mode, hop, hopz
        self.group = held.shape[1]
        self.unit = self.group // place.deep
        n = place.side
        self.line = [*range(1, n), 0]
        self.order = [(d, e) for d in self.line for e in self.line]
        self.out, self.deep = wires.sem(), wires.sem()
        if mode == "axes":
            self.crossed = {step: wires.sem() for step in self.order}
            self.first = [wires.sem() for _ in range(n)]
            self.second = wires.sem()
        else:
            self.cross, self.level = wires.sem(), wires.sem()
        sent = (2 * n * n - 1) * self.group + (0 if hopz is None else self.group - self.unit)
        wires.unsent.append((grads.at[pl.ds(0, sent)], self.out))

    def at(self, turn, d, e):
        y, x = self.p.spot(turn, d, e)
        return y * self.p.side + x

    def hop(self, d, e):
        return self.hops.at[self.order.index((d, e))]

    def rows_of(self, j, core):
        return pl.ds(pl.multiple_of((2 * j + core) * self.group, self.group), self.group)

    def unit_rows(self, d):
        p = self.p
        return pl.ds(pl.multiple_of(lax.rem(p.z + d, p.deep) * self.unit, self.unit), self.unit)

    def owner(self, d, e):
        p = self.p
        return p.seq(*p.spot(p.c, d, e), p.c), p.z

    def send(self, src, dst, device, came):
        self.w.copy(src, dst, device, self.out, came)

    def cross_over(self, d, e):
        p = self.p
        j = self.at(1 - p.c, d, e)
        came = self.crossed[d, e] if self.mode == "axes" else self.cross
        self.send(self.grads.at[self.rows_of(j, 1 - p.c)], self.held.at[j], p.sibling(), came)

    def fold(self, d, e):
        p = self.p
        j = self.at(p.c, d, e)
        if self.mode == "axes":
            wait_bytes(self.held.at[j], self.crossed[d, e])
        add_into(self.held, j, [self.grads[self.rows_of(j, p.c)]])
        if self.mode == "axes" and d:
            self.send(self.held.at[j], self.hop(d, e), p.peers(0)[d - 1], self.first[e])
        if self.mode == "direct" and (d or e):
            self.send(self.held.at[j], self.hop(d, e), self.owner(d, e), self.level)

    def turn(self, e):
        p, n = self.p, self.p.side
        j = self.at(p.c, 0, e)
        wait_bytes(self.held.at[pl.ds(0, n - 1)], self.first[e])
        add_into(self.held, j, [self.hop(d, e)[...] for d in range(1, n)])
        if e:
            self.send(self.held.at[j], self.hop(0, e), p.peers(1)[e - 1], self.second)

    def step0(self):
        for d, e in self.order:
            self.cross_over(d, e)

    def step1(self):
        if self.mode != "axes":
            wait_bytes(self.held, self.cross)
        for d, e in self.order:
            self.fold(d, e)

    def step2(self):
        for e in self.line if self.mode == "axes" else ():
            self.turn(e)

    def step3(self):
        p = self.p
        self.mine = self.at(p.c, 0, 0)
        if self.mode == "direct":
            wait_bytes(self.hops, self.level)
            add_into(self.held, self.mine, [self.hop(d, e)[...] for d, e in p.steps()])
        else:
            wait_bytes(self.held.at[pl.ds(0, p.side - 1)], self.second)
            add_into(self.held, self.mine, [self.hop(0, e)[...] for e in range(1, p.side)])
        if self.hopz is not None:
            for d, other in enumerate(p.peers("z"), 1):
                self.send(self.held.at[self.mine, self.unit_rows(d)], self.hopz.at[d - 1], other, self.deep)

    def step4(self):
        if self.hopz is None:
            return self.held[self.mine].astype(F32)
        total = self.held[self.mine, self.unit_rows(0)].astype(F32)
        wait_bytes(self.hopz, self.deep)
        for d in range(self.p.deep - 1):
            total = total + self.hopz[d].astype(F32)
        return total


def scatter_scratch(side, deep, unit, tail, with_z):
    group = deep * unit
    shapes = [(side * side, group), (side * side - 1, group)]
    if with_z:
        shapes.append((deep - 1, unit))
    return [pltpu.VMEM((*shape, *tail), BF16) for shape in shapes]


class Total:
    def __init__(self, wires, place, sums, came):
        self.w, self.p, self.sums, self.came = wires, place, sums, came
        self.out, self.slot = wires.sem(), 0
        wires.unsent.append((came, self.out))

    def send(self, level):
        p = self.p
        peers = [[p.sibling()], p.plane(), p.peers("z")][level]
        self.sem, self.first, self.count = self.w.sem(), self.slot, len(peers)
        for peer in peers:
            self.w.copy(self.sums.at[level], self.came.at[self.slot], peer, self.out, self.sem)
            self.slot += 1

    def take(self, level):
        wait_bytes(self.came.at[pl.ds(self.first, self.count)], self.sem)
        total = self.sums[level]
        for i in range(self.count):
            total = total + self.came[self.first + i]
        self.sums[level + 1] = total


def layer_kernel(
    with_z, grad_scale,
    x_hbm, cot_hbm, wqkv_ref, wo_ref, wu_ref, wd_ref, gain1_ref, shift1_ref, gain2_ref, shift2_ref, span_doc_ref,
    act2_ref, dtok_ref, dwqkv_ref, dwo_ref, dwu_ref, dwd_ref, total_ref,
    x_ref, cot_ref, small_ref, docs_ref, own_q, own_k, own_v,
    q_mat, k_mat, v_mat, out_mat, up_mat, down_mat, gains_ref, small_all, own_sums, sums_all, sums_ref, sums_t_ref,
    act_ref, qkv_ref, probs_ref, attn_t_ref, resid_ref, acted_ref, dhid_ref, dattn_ref,
    gdown_ref, gup_ref, gout_ref, gq_ref, gk_ref, gv_ref, dkv_ref, stats_ref, delta_ref, dsum_ref, levels_ref, came_ref,
    sems, place_sem, *held,
):
    place = Place()
    wires = Wires(sems)
    tok = x_ref.shape[0]
    spans = tok // S
    tiles = tok // TILE
    first = place.me * spans
    held = list(held)
    local = [pltpu.make_async_copy(x_hbm, x_ref, place_sem.at[0]), pltpu.make_async_copy(cot_hbm, cot_ref, place_sem.at[1])]
    for move in local:
        move.start()

    def gather(shard, full, direct):
        return Gather(wires, place, shard, full, shard.shape[0], with_z, direct)

    def scatter(grads, z, mode):
        parts = [held.pop(0) for _ in range(3 if z else 2)]
        return Scatter(wires, place, grads, mode, *parts, *([] if z else [None]))

    small = Gather(wires, place, small_ref, small_all, 1, True, True)
    sums = Gather(wires, place, own_sums, sums_all, 1, True, True)
    g_k, g_v, g_q = gather(own_k, k_mat, True), gather(own_v, v_mat, True), gather(own_q, q_mat, True)
    g_out, g_down, g_up = gather(wo_ref, out_mat, False), gather(wd_ref, down_mat, False), gather(wu_ref, up_mat, False)
    s_sum = scatter(sums_all, True, "direct")
    s_down, s_up, s_out = [scatter(g, with_z, "axes") for g in (gdown_ref, gup_ref, gout_ref)]
    s_q, s_k, s_v = [scatter(g, with_z, "direct") for g in (gq_ref, gk_ref, gv_ref)]

    width = gain1_ref.shape[1]
    small_ref[...] = jnp.zeros_like(small_ref)
    for k, ref in enumerate((gain1_ref, shift1_ref, gain2_ref, shift2_ref)):
        small_ref[0, k : k + 1, :width] = ref[...].astype(F32)
    split_heads(wqkv_ref[...], (own_q, own_k, own_v))
    place.greet()
    for g in (small, g_k, g_v, g_q, g_down, g_out):
        g.step0()
    small.step1()
    g_k.step1()
    g_v.step1()
    small.step3()
    g_k.step3()
    g_q.step1()
    docs_ref[...] = window_docs(first, spans, span_doc_ref)
    small.step4()
    gains_ref[...] = spread_small(small_all[...], place.devices)
    local[0].wait()

    def norm(i):
        rows = tile_rows(i, S)
        xhat, _ = normed_parts(x_ref[rows, :].astype(F32))
        act_ref[rows, :] = (xhat * gains_ref[0:1, :] + gains_ref[1:2, :]).astype(BF16)

    loop(0, spans, norm, 4)
    g_v.step3()
    g_k.step4()

    def project(mat, part):
        block = nn(act_ref[...], mat[...]).astype(BF16)
        qkv_ref[:, part * D : (part + 1) * D] = block
        if part:
            mean = jnp.sum(block.astype(F32).reshape(spans, S, D), axis=1) * (1.0 / S)
            own_sums[0, :, (part - 1) * D : part * D] = mean.astype(BF16)

    project(k_mat, 1)
    g_q.step3()
    g_down.step1()
    g_out.step1()
    g_v.step4()
    project(v_mat, 2)
    sums.step0()
    g_up.step0()
    g_q.step4()
    project(q_mat, 0)
    half = spans // 2
    loop(0, half, lambda i: span_scores(i, qkv_ref, dkv_ref, stats_ref), TOGETHER)
    sums.step1()
    loop(half, spans, lambda i: span_scores(i, qkv_ref, dkv_ref, stats_ref), TOGETHER)
    sums.step3()
    g_out.step2()
    sums.step4()
    for i in range(PSPANS // MOST):
        two = sums_all[pl.ds(2 * i, 2)].astype(F32)
        sums_ref[MOST * i : MOST * (i + 1), :] = two.reshape(MOST, 2 * D).astype(BF16)
    before = sums_all[pl.ds(lax.rem(place.me + place.devices - 2, place.devices), 1)].astype(F32)
    last = sums_all[pl.ds(lax.rem(place.me + place.devices - 1, place.devices), 1)].astype(F32)
    here = sums_all[pl.ds(place.me, 1)].astype(F32)
    nothing = jnp.zeros_like(here)
    sums_ref[PSPANS : PSPANS + MOST, :] = jnp.concatenate([before, last], axis=0).reshape(MOST, 2 * D).astype(BF16)
    sums_ref[PSPANS + MOST :, :] = jnp.concatenate([here, nothing], axis=0).reshape(MOST, 2 * D).astype(BF16)
    sums_t_ref[...] = sums_ref[...].T

    def attend(span):
        attend_span(span, first, qkv_ref, sums_ref, sums_t_ref, docs_ref, dkv_ref, stats_ref, attn_t_ref, probs_ref)

    quarter = spans // 4
    g_up.step1()
    loop(0, quarter, attend, TOGETHER)
    g_down.step2()
    loop(quarter, 3 * quarter, attend, TOGETHER)
    g_out.step3()
    loop(3 * quarter, spans, attend, TOGETHER)
    g_out.step4()

    def residual(i):
        rows = tile_rows(i, TILE)
        resid = x_ref[rows, :].astype(F32) + tn(attn_t_ref[:, rows], out_mat[...])
        resid_ref[rows, :] = resid
        xhat, _ = normed_parts(resid)
        act2_ref[rows, :] = (xhat * gains_ref[2:3, :] + gains_ref[3:4, :]).astype(BF16)

    loop(0, tiles, residual, 2)
    local[1].wait()
    g_up.step2()

    def feed(i):
        part = tile_rows(i, CHUNK)
        acted, slope = gelu_parts(nt(act2_ref[...], up_mat[part, :]))
        acted = acted.astype(BF16)
        acted_ref[:, part] = acted
        dhid = (nt(cot_ref[...], down_mat[part, :]) * slope).astype(BF16)
        dhid_ref[:, part] = dhid
        gdown_ref[part, :] = tn(acted, cot_ref[...]).astype(BF16)
        gup_ref[part, :] = tn(dhid, act2_ref[...]).astype(BF16)

    both = (s_down, s_up)
    blocks = [(d, e) for e in range(place.side) for d in range(place.side)]
    waiting = []
    if s_up.group == CHUNK:
        for d, e in blocks:
            if (d, e) == (0, 1):
                g_down.step3()
                g_up.step3()
            g_down.ready(d, e)
            g_up.ready(d, e)
            theirs = 2 * s_up.at(1 - place.c, d, e) + 1 - place.c
            ours = 2 * s_up.at(place.c, d, e) + place.c
            loop(0, 2, lambda i: feed(theirs + i * (ours - theirs)), 2)
            for s in both:
                s.cross_over(d, e)
            waiting.append((d, e))
            if len(waiting) > 1:
                fold_all(both, *waiting.pop(0))
    else:
        for g in (g_down, g_up):
            g.step3()
            g.step4()
        loop(0, up_mat.shape[0] // CHUNK, feed)
        for s in both:
            s.step0()
        waiting = list(s_up.order)
    levels_ref[...] = jnp.zeros_like(levels_ref)

    def finish(i):
        rows = tile_rows(i, TILE)
        dnormed = nn(dhid_ref[rows, :], up_mat[...])
        xhat, inverse = normed_parts(resid_ref[rows, :])
        levels_ref[0, 2:3, :] += jnp.sum(dnormed * xhat, axis=0, keepdims=True)
        levels_ref[0, 3:4, :] += jnp.sum(dnormed, axis=0, keepdims=True)
        dresid = cot_ref[rows, :].astype(F32) + norm_back(dnormed, xhat, inverse, gains_ref[2:3, :])
        dtok_ref[rows, :] = dresid
        branch = dresid.astype(BF16)
        act2_ref[rows, :] = branch
        dattn_ref[rows, :] = nt(branch, out_mat[...]).astype(BF16)

    loop(0, tiles // 2, finish, 2)
    for d, e in waiting:
        fold_all(both, d, e)
    loop(tiles // 2, tiles, finish, 2)
    gout_ref[...] = nn(attn_t_ref[...], act2_ref[...]).astype(BF16)
    s_out.step0()
    dsum_ref[...] = jnp.zeros_like(dsum_ref)

    def back_far(span):
        summary_back(span, qkv_ref, sums_ref, probs_ref, attn_t_ref, dattn_ref, delta_ref, dsum_ref)

    def back_near(span):
        span_back(span, qkv_ref, sums_t_ref, probs_ref, dattn_ref, delta_ref, dhid_ref, dkv_ref)

    loop(0, quarter, back_far, TOGETHER)
    s_out.step1()
    loop(quarter, 2 * quarter, back_far, TOGETHER)
    for e in s_up.line[:-1]:
        for s in both:
            s.turn(e)
    loop(2 * quarter, spans, back_far, TOGETHER)
    for s in both:
        s.turn(0)
    sums.settle()
    sums_all[...] = jnp.zeros_like(sums_all)
    for i in range(3):
        block = lax.rem(place.me + place.devices - 2 + i, place.devices)
        rows = slice(PSPANS + i * spans, PSPANS + (i + 1) * spans)
        sums_all[pl.ds(block, 1)] = dsum_ref[rows, :].astype(BF16)[None]
    for i in range(PSPANS // spans):
        sums_all[i] = dsum_ref[i * spans : (i + 1) * spans, :].astype(BF16)
    s_sum.step0()
    loop(0, quarter, back_near, TOGETHER)
    s_sum.step1()
    s_out.step2()
    loop(quarter, 3 * quarter, back_near, TOGETHER)
    s_sum.step3()
    for s in both:
        s.step3()
    s_out.step3()
    loop(3 * quarter, spans, back_near, TOGETHER)
    gq_ref[...] = tn(act_ref[...], dhid_ref[:, :D]).astype(BF16)
    s_q.step0()
    shares = s_sum.step4()[0] * (1.0 / S)
    for part, g_ref, s in ((0, gk_ref, s_k), (1, gv_ref, s_v)):
        cols = slice(part * D, (part + 1) * D)
        for span in range(spans):
            rows = slice(span * S, (span + 1) * S)
            dhid_ref[rows, (part + 1) * D : (part + 2) * D] = (dkv_ref[rows, cols] + shares[span : span + 1, cols]).astype(BF16)
        g_ref[...] = tn(act_ref[...], dhid_ref[:, (part + 1) * D : (part + 2) * D]).astype(BF16)
        s.step0()

    def finish_tokens(i):
        rows = slice(i * TILE, (i + 1) * TILE)
        dnormed = nt(dhid_ref[rows, :D], q_mat[...]) + nt(dhid_ref[rows, D : 2 * D], k_mat[...])
        dnormed = dnormed + nt(dhid_ref[rows, 2 * D : 3 * D], v_mat[...])
        xhat, inverse = normed_parts(x_ref[rows, :].astype(F32))
        levels_ref[0, 0:1, :] += jnp.sum(dnormed * xhat, axis=0, keepdims=True)
        levels_ref[0, 1:2, :] += jnp.sum(dnormed, axis=0, keepdims=True)
        dtok_ref[rows, :] += norm_back(dnormed, xhat, inverse, gains_ref[0:1, :])

    def output(i):
        rows = slice(i * TILE, (i + 1) * TILE)
        act2_ref[rows, :] = (resid_ref[rows, :] + nn(acted_ref[rows, :], down_mat[...])).astype(BF16)

    total = Total(wires, place, levels_ref, came_ref)
    finish_tokens(0)
    s_q.step1()
    s_k.step1()
    finish_tokens(1)
    s_v.step1()
    finish_tokens(2)
    finish_tokens(3)
    total.send(0)
    output(0)
    total.take(0)
    total.send(1)
    output(1)
    s_q.step3()
    output(2)
    s_k.step3()
    output(3)
    s_v.step3()
    total.take(1)
    total.send(2)
    dwd_ref[...] = s_down.step4() * grad_scale
    dwu_ref[...] = s_up.step4() * grad_scale
    dwo_ref[...] = s_out.step4() * grad_scale
    join_heads((s_q.step4() * grad_scale, s_k.step4() * grad_scale, s_v.step4() * grad_scale), dwqkv_ref)
    total.take(2)
    start = place.me * width
    lanes = pl.ds(pl.multiple_of(start // LANES * LANES, LANES), LANES)
    total_ref[...] = pltpu.roll(levels_ref[3, :, lanes] * grad_scale, lax.rem(LANES - lax.rem(start, LANES), LANES), 1)
    wires.finish()


def fold_all(scatters, d, e):
    for s in scatters:
        s.fold(d, e)


def layer(with_z, grad_scale, x, cotangent, wqkv, wo, wu, wd, vectors, span_doc):
    tok = x.shape[0]
    spans = tok // S
    deep = lax.axis_size("head")
    side = math.isqrt(lax.axis_size("seq") // 2)
    devices = 2 * side * side * deep
    owned = devices if with_z else devices // deep
    hidden_size = wu.shape[0] * owned
    whole, anywhere = pl.BlockSpec(memory_space=VMEM), pl.BlockSpec(memory_space=pl.ANY)
    shape = jax.ShapeDtypeStruct
    peers = 1 + side * side - 1 + deep - 1
    held = scatter_scratch(side, deep, 1, (spans, 2 * D), True)
    for total in (hidden_size, hidden_size, D, D, D, D):
        held += scatter_scratch(side, deep, total // devices, (D,), with_z)
    return pl.pallas_call(
        functools.partial(layer_kernel, with_z, grad_scale),
        out_shape=(
            pltpu.VMEM((tok, D), BF16),
            pltpu.VMEM((tok, D), F32),
            pltpu.VMEM((D // owned, 3 * D), F32),
            pltpu.VMEM((D // owned, D), F32),
            pltpu.VMEM((hidden_size // owned, D), F32),
            pltpu.VMEM((hidden_size // owned, D), F32),
            pltpu.VMEM((8, LANES), F32),
        ),
        in_specs=[anywhere] * 2 + [whole] * 8 + [pl.BlockSpec(memory_space=pltpu.MemorySpace.SMEM)],
        out_specs=(whole,) * 7,
        scratch_shapes=[
            pltpu.VMEM((tok, D), BF16),
            pltpu.VMEM((tok, D), BF16),
            pltpu.VMEM((1, 8, LANES), F32),
            pltpu.VMEM((WIN, S), jnp.int32),
            pltpu.VMEM((D // owned, D), BF16),
            pltpu.VMEM((D // owned, D), BF16),
            pltpu.VMEM((D // owned, D), BF16),
            pltpu.VMEM((D, D), BF16),
            pltpu.VMEM((D, D), BF16),
            pltpu.VMEM((D, D), BF16),
            pltpu.VMEM((D, D), BF16),
            pltpu.VMEM((hidden_size, D), BF16),
            pltpu.VMEM((hidden_size, D), BF16),
            pltpu.VMEM((8, D), F32),
            pltpu.VMEM((devices, 8, LANES), F32),
            pltpu.VMEM((1, spans, 2 * D), BF16),
            pltpu.VMEM((devices, spans, 2 * D), BF16),
            pltpu.VMEM((FAR, 2 * D), BF16),
            pltpu.VMEM((2 * D, FAR), BF16),
            pltpu.VMEM((tok, D), BF16),
            pltpu.VMEM((tok, 3 * D), BF16),
            pltpu.VMEM((spans * PAIRS, KEYS, 2 * S), BF16),
            pltpu.VMEM((D, tok), BF16),
            pltpu.VMEM((tok, D), F32),
            pltpu.VMEM((tok, hidden_size), BF16),
            pltpu.VMEM((tok, hidden_size), BF16),
            pltpu.VMEM((tok, D), BF16),
            pltpu.VMEM((hidden_size, D), BF16),
            pltpu.VMEM((hidden_size, D), BF16),
            pltpu.VMEM((D, D), BF16),
            pltpu.VMEM((D, D), BF16),
            pltpu.VMEM((D, D), BF16),
            pltpu.VMEM((D, D), BF16),
            pltpu.VMEM((tok, 2 * D), F32),
            pltpu.VMEM((2, spans * PAIRS, 2 * S), F32),
            pltpu.VMEM((spans * PAIRS, 2 * S), F32),
            pltpu.VMEM((FAR, 2 * D), F32),
            pltpu.VMEM((4, 8, D), F32),
            pltpu.VMEM((peers, 8, D), F32),
            pltpu.SemaphoreType.DMA((semaphores(side),)),
            pltpu.SemaphoreType.DMA((2,)),
            *held,
        ],
        compiler_params=pltpu.CompilerParams(vmem_limit_bytes=VMEM_LIMIT - 7 * tok * D, collective_id=0, has_side_effects=True),
        name="mega_layer",
    )(x, cotangent, wqkv, wo, wu, wd, *vectors, span_doc)


def deliver_kernel(*refs):
    count = (len(refs) - 1) // 2
    sems = refs[-1]
    moves = [pltpu.make_async_copy(refs[i], refs[count + i], sems.at[i]) for i in range(count)]
    for move in moves:
        move.start()
    for move in moves:
        move.wait()


def deliver(arrays):
    anywhere = pl.BlockSpec(memory_space=pl.ANY)
    return pl.pallas_call(
        deliver_kernel,
        out_shape=[jax.ShapeDtypeStruct(a.shape, a.dtype) for a in arrays],
        in_specs=[anywhere] * len(arrays),
        out_specs=[anywhere] * len(arrays),
        scratch_shapes=[pltpu.SemaphoreType.DMA((len(arrays),))],
        compiler_params=pltpu.CompilerParams(vmem_limit_bytes=2**20),
        name="deliver",
    )(*arrays)


def shards(tokens, cotangent, w_qkv, w_out, w_up, w_down, gain_one, shift_one, gain_two, shift_two, span_doc):
    tok = tokens.shape[0]
    devices = lax.axis_size("seq") * lax.axis_size("head")
    grad_scale = 1.0 / math.sqrt(tok * devices)
    with_z = w_qkv.shape[0] % 16 == 0
    weights = (w_qkv, w_out, w_up.T, w_down)
    if not with_z:
        weights = tuple(lax.all_gather(w, "head", axis=0, tiled=True) for w in weights)
    vectors = [v[None] for v in (gain_one, shift_one, gain_two, shift_two)]
    width = gain_one.shape[0]
    out_tokens, d_tokens, d_qkv, d_out, d_up, d_down, total = deliver(
        layer(with_z, grad_scale, tokens, cotangent, *weights, vectors, span_doc)
    )
    if not with_z:
        d_qkv, d_out, d_up, d_down = (
            lax.psum_scatter(g, "head", scatter_dimension=0, tiled=True) for g in (d_qkv, d_out, d_up, d_down)
        )
    return out_tokens, d_tokens, d_qkv, d_out, d_up.T, d_down, *(total[k, :width] for k in range(4))


def solution(mesh):
    rows, cols, vec = P(BOTH, None), P(None, BOTH), P(BOTH)
    in_specs = (rows, rows, rows, rows, cols, rows, vec, vec, vec, vec, P())
    out_specs = (rows, rows, rows, rows, cols, rows, vec, vec, vec, vec)
    return jax.shard_map(shards, mesh=mesh, in_specs=in_specs, out_specs=out_specs, check_vma=False)
```
